32 devices in a mesh: seq: 4 (over x, core), dp: 8 (over z, y).
Axes of the slice: x: 2, y: 2, z: 4, core: 2. Of those that a mesh axis runs over, the one named last changes fastest.
Arguments:
- tokens: bfloat16 [8, 2048, 1024], P('dp', 'seq'), may hold values from -6 to 6
- lengths: int32 [8, 3], P('dp'), may hold values from 1 to 2046, as said below
- attend_weight: bfloat16 [1024, 3072], P('dp'), may hold values from -0.1875 to 0.1875
- output_weight: bfloat16 [1024, 1024], P('dp'), may hold values from -3 to 3
- expand_weight: bfloat16 [1024, 4096], P('dp'), may hold values from -0.1875 to 0.1875
- shrink_weight: bfloat16 [4096, 1024], P('dp'), may hold values from -0.09375 to 0.09375
- prefix_embed: float32 [10, 1024], replicated, may hold values from -6 to 6
- inner_weight: float32 [1024, 512], replicated, may hold values from -0.1875 to 0.1875
- inner_bias: float32 [512], replicated, may hold values from -3 to 3
- outer_weight: float32 [512, 2048], replicated, may hold values from -0.25 to 0.25
- outer_bias: float32 [2048], replicated, may hold values from -3 to 3
- cotangent: bfloat16 [8, 2048, 1024], P('dp', 'seq'), may hold values from -6 to 6
Outputs:
- outputs: bfloat16 [8, 2048, 1024], P('dp', 'seq')
- grad_tokens: bfloat16 [8, 2048, 1024], P('dp', 'seq')
- embed_grad: float32 [10, 1024], replicated
- inner_grad: float32 [1024, 512], replicated
- inner_bias_grad: float32 [512], replicated
- outer_grad: float32 [512, 2048], replicated
- outer_bias_grad: float32 [2048], replicated
- prefix_kv: float32 [10, 2048], replicated
The draws below stay inside these ranges and needn't reach their ends.
Inputs may be any that keep to these rules, and one draw needn't show every extreme that they name: `lengths`: each row sums to 2048; in each row one document is longer than 1536 tokens and the others hold at most 128 tokens.
All inputs are finite; a program needn't handle non-finite values.
Results may differ from the reference program's by a relative error of at most 0.024.
Values may be sent and summed in bfloat16 or wider, within the bound.
No kernel may reach another device: no remote copies, remote signals or barrier semaphores. Data moves between devices by JAX's collectives and lax.ppermute only.
A program may use at most 256 MiB of HBM per device.

```python
import math
import jax
import jax.numpy as jnp
from jax import lax

D = 1024
HEADS = 16
HEAD_DIM = 64
FF = 4096
RH = 512
PREFIX = 10
NDOC = 3
SHORT_MAX = 128
SEQ_TOK = 2048
GROUPS = 8


def draw_lengths(key, part):
    short_key = jax.random.fold_in(key, 11)
    place_key = jax.random.fold_in(key, 23)
    pick_key = jax.random.fold_in(key, 37)
    shorts = jax.random.randint(short_key, (GROUPS, NDOC), 1, SHORT_MAX + 1, dtype=jnp.int32)
    chosen_group = jax.random.randint(pick_key, (), 0, GROUPS, dtype=jnp.int32)
    group_index = jnp.arange(GROUPS, dtype=jnp.int32)[:, None]
    shorts = jnp.where(group_index == chosen_group, 1, shorts)
    long_place = jax.random.randint(place_key, (GROUPS, 1), 0, NDOC, dtype=jnp.int32)
    column = jnp.arange(NDOC, dtype=jnp.int32)[None, :]
    is_long = column == long_place
    remainder = SEQ_TOK - jnp.sum(jnp.where(is_long, 0, shorts), axis=1, keepdims=True)
    return jnp.where(is_long, remainder, shorts).astype(jnp.int32)


def shard_levels(key, shape, cuts, low, largest):
    def one(position, shards_of):
        heights = jax.random.uniform(jax.random.fold_in(jax.random.fold_in(key, 6), position), (shards_of,), jnp.float32, low / len(cuts), largest / len(cuts))
        return jnp.repeat(jnp.exp(heights), shape[position] // shards_of).reshape((-1,) + (1,) * (len(shape) - position - 1))

    factor_of = one(*cuts[0])
    for cut in cuts[1:]:
        factor_of = factor_of * one(*cut)
    return factor_of


def noise(stream_key, extent, width, bound, cuts=(), kind=jnp.bfloat16):
    loudness = shard_levels(stream_key, extent, cuts, -0.22, 0.18) if cuts else 1.0
    drawn = jax.random.normal(stream_key, extent, jnp.float32) * width * loudness
    return jnp.minimum(jnp.maximum(drawn, -bound), bound).astype(kind)


def setup_inputs(seed: int = 0) -> dict:
    arg_keys = jax.random.split(jax.random.key(seed), 13)
    tokens = noise(arg_keys[0], (GROUPS, SEQ_TOK, D), 1.0, 6.0, ((0, 8), (1, 4)))
    lengths = draw_lengths(jax.random.fold_in(arg_keys[12], 71), 0)
    attend_weight = noise(arg_keys[2], (D, 3 * D), D ** -0.5, 0.1875, ((0, 8),))
    output_weight = noise(arg_keys[3], (D, D), (max(D // 256, 1)) ** -0.5, 3.0, ((0, 8),))
    expand_weight = noise(arg_keys[4], (D, FF), D ** -0.5, 0.1875, ((0, 8),))
    shrink_weight = noise(arg_keys[5], (FF, D), FF ** -0.5, 0.09375, ((0, 8),))
    prefix_embed = noise(arg_keys[6], (PREFIX, D), 1.0, 6.0, (), jnp.float32)
    inner_weight = noise(arg_keys[7], (D, RH), D ** -0.5, 0.1875, (), jnp.float32)
    inner_bias = noise(arg_keys[8], (RH,), 0.5, 3.0, (), jnp.float32)
    outer_weight = noise(arg_keys[9], (RH, 2 * D), RH ** -0.5, 0.25, (), jnp.float32)
    outer_bias = noise(arg_keys[10], (2 * D,), 0.5, 3.0, (), jnp.float32)
    cotangent = noise(arg_keys[11], (GROUPS, SEQ_TOK, D), 1.0, 6.0, ((0, 8), (1, 4)))
    return dict(tokens=tokens, lengths=lengths, attend_weight=attend_weight, output_weight=output_weight, expand_weight=expand_weight, shrink_weight=shrink_weight, prefix_embed=prefix_embed, inner_weight=inner_weight, inner_bias=inner_bias, outer_weight=outer_weight, outer_bias=outer_bias, cotangent=cotangent)


@jax.custom_vjp
def low(v):
    return lax.optimization_barrier(v.astype(jnp.bfloat16)).astype(jnp.float32)

@jax.custom_vjp
def low_back(v):
    return v

def low_keep(v):
    return (low(v), None)

def low_pass(kept, grad):
    return (grad,)

def back_keep(v):
    return (v, None)

def back_low(kept, grad):
    return (low(grad),)
low.defvjp(low_keep, low_pass)
low_back.defvjp(back_keep, back_low)
norm_epsilon = 1e-05
masked_value = -1e+30
highest = lax.Precision.HIGHEST

def matmul(left, right):
    return jnp.dot(left, right, precision=highest, preferred_element_type=jnp.float32)

def layer_norm(hidden):
    centered = hidden - lax.optimization_barrier(jnp.mean(hidden, axis=-1, keepdims=True))
    return centered * lax.rsqrt(lax.optimization_barrier(jnp.mean(centered * centered, axis=-1, keepdims=True)) + norm_epsilon)

def gelu_tanh(values):
    return 0.5 * values * (1.0 + jnp.tanh(0.7978845608028654 * (values + 0.044715 * values * values * values)))

def document_ids(lengths_row, positions):
    doc_ends = jnp.cumsum(lengths_row)
    return lax.optimization_barrier(jnp.sum((positions[:, None] >= doc_ends[None, :]).astype(jnp.int32), axis=1))

def group_forward(tokens_row, lengths_row, weights, prefix_keys, prefix_values):
    attend_weight, output_weight, expand_weight, shrink_weight = weights
    seq_len = tokens_row.shape[0]
    scale = 1.0 / math.sqrt(HEAD_DIM)
    normed_in = low(layer_norm(tokens_row))
    projected = matmul(normed_in, attend_weight)
    queries = low(low_back(projected[:, :D])).reshape(seq_len, HEADS, HEAD_DIM)
    key_rows = low(low_back(projected[:, D:2 * D])).reshape(seq_len, HEADS, HEAD_DIM)
    value_rows = low(low_back(projected[:, 2 * D:])).reshape(seq_len, HEADS, HEAD_DIM)
    positions = jnp.arange(seq_len, dtype=jnp.int32)
    documents = document_ids(lengths_row, positions)
    block_rows = min(512, seq_len)
    block_count = seq_len // block_rows

    def attend(pieces):
        query_block, query_pos, query_doc = pieces
        token_scores = jnp.einsum('qhd,khd->hqk', query_block, key_rows, precision=highest) * scale
        allowed = (documents[None, :] == query_doc[:, None]) & (positions[None, :] <= query_pos[:, None])
        token_scores = jnp.where(allowed[None], token_scores, masked_value)
        prefix_scores = jnp.einsum('qhd,phd->hqp', query_block, prefix_keys, precision=highest) * scale
        scores = low_back(jnp.concatenate([prefix_scores, token_scores], axis=2))
        row_max = lax.optimization_barrier(jnp.max(scores, axis=2, keepdims=True))
        exps = jnp.exp(scores - row_max)
        probs = low(exps / lax.optimization_barrier(jnp.sum(exps, axis=2, keepdims=True)))
        mixed_rows = jnp.einsum('hqp,phd->qhd', probs[:, :, :PREFIX], prefix_values, precision=highest)
        return mixed_rows + jnp.einsum('hqk,khd->qhd', probs[:, :, PREFIX:], value_rows, precision=highest)
    attended = lax.map(jax.checkpoint(attend), (queries.reshape(block_count, block_rows, HEADS, HEAD_DIM), positions.reshape(block_count, block_rows), documents.reshape(block_count, block_rows)))
    merged = low(low_back(attended.reshape(seq_len, D)))
    residual_mid = tokens_row + low_back(matmul(merged, output_weight))
    expanded = low_back(matmul(low(layer_norm(residual_mid)), expand_weight))
    return residual_mid + matmul(low(gelu_tanh(expanded)), shrink_weight)

def reference(tokens, lengths, attend_weight, output_weight, expand_weight, shrink_weight, prefix_embed, inner_weight, inner_bias, outer_weight, outer_bias, cotangent):
    weights = (attend_weight.astype(jnp.float32), output_weight.astype(jnp.float32), expand_weight.astype(jnp.float32), shrink_weight.astype(jnp.float32))

    def forward(token_rows, embedding, inner_matrix, inner_shift, outer_matrix, outer_shift):
        hidden = jnp.tanh(matmul(embedding, inner_matrix) + inner_shift)
        prefix_kv = matmul(hidden, outer_matrix) + outer_shift
        prefix_keys = low(prefix_kv[:, :D]).reshape(PREFIX, HEADS, HEAD_DIM)
        prefix_values = low(prefix_kv[:, D:]).reshape(PREFIX, HEADS, HEAD_DIM)

        def one_group(group_pair):
            return group_forward(group_pair[0], group_pair[1], weights, prefix_keys, prefix_values)
        return (lax.map(jax.checkpoint(one_group), (token_rows, lengths)), prefix_kv)
    (outputs, prefix_kv), pullback = jax.vjp(forward, tokens.astype(jnp.float32), prefix_embed, inner_weight, inner_bias, outer_weight, outer_bias)
    gradients = pullback((cotangent.astype(jnp.float32), jnp.zeros_like(prefix_kv)))
    return (outputs.astype(jnp.bfloat16), gradients[0].astype(jnp.bfloat16), gradients[1], gradients[2], gradients[3], gradients[4], gradients[5], prefix_kv)
```

```python
import functools

import jax
import jax.numpy as jnp
from jax import lax
from jax.experimental import pallas as pl
from jax.experimental.pallas import tpu as pltpu
from jax.sharding import PartitionSpec as P

PREFIX = 10
HEAD = 64
PAIR = 128
PREFIX_ROWS = 16
blocked = -1e30
norm_epsilon = 1e-05
highest = lax.Precision.HIGHEST
VT_ROWS = 80
f32, bf16 = jnp.float32, jnp.bfloat16

def dot(a, b, ca, cb):
    return lax.dot_general(a, b, (((ca,), (cb,)), ((), ())), preferred_element_type=f32)

def lane(shape):
    return lax.broadcasted_iota(jnp.int32, shape, len(shape) - 1)

def head_half(h, shape):
    l = lane(shape)
    return (l < HEAD) if h == 0 else (l >= HEAD)

def split3(v):
    hi = v.astype(bf16)
    r = v - hi.astype(f32)
    mid = r.astype(bf16)
    lo = (r - mid.astype(f32)).astype(bf16)
    return hi.astype(f32), mid.astype(f32), lo.astype(f32)

def fwd_body(bq, bk, q_ref, k_ref, v_ref, pk_ref, pv_ref, mq_ref, mk_ref, pm_ref,
             o_ref, stat_ref, ka, vt, pka, pvt, qh):
    i = pl.program_id(0)
    s_len = k_ref.shape[0]

    @pl.when(i == 0)
    def _():
        ka[:, :PAIR] = k_ref[...]
        ka[:, PAIR:] = mk_ref[...]
        pka[:, :PAIR] = pk_ref[...]
        pka[:, PAIR:] = pm_ref[...]
        ones = jnp.where(lax.broadcasted_iota(jnp.int32, (16, s_len), 0) == 0, 1.0, 0.0).astype(bf16)
        vtr = v_ref[...].T
        pvr = pv_ref[...].T
        for h in (0, 1):
            vt[h, :HEAD, :] = vtr[h * HEAD:(h + 1) * HEAD, :]
            vt[h, HEAD:, :] = ones
            pvt[h, :HEAD, :] = pvr[h * HEAD:(h + 1) * HEAD, :]
            pvt[h, HEAD:, :] = ones[:, :PREFIX_ROWS]

    q = q_ref[...] * bf16(0.125)
    for h in (0, 1):
        qh[h, :, :PAIR] = jnp.where(head_half(h, q.shape), q, bf16(0))
        qh[h, :, PAIR:] = mq_ref[...]
    state = []
    for h in (0, 1):
        s = dot(pka[...], qh[h], 1, 1)
        m = jnp.max(s, axis=0, keepdims=True)
        p = jnp.exp(s - m)
        state += [m, dot(pvt[h], p.astype(bf16), 1, 0)]

    def block(start, state, first, causal):
        out = []
        start = pl.multiple_of(start, bk)
        scores = [dot(ka[pl.ds(start, bk), :], qh[h, first:, :], 1, 1) for h in (0, 1)]
        for h in (0, 1):
            m, acc = state[2 * h], state[2 * h + 1]
            s = scores[h]
            if causal:
                ok = lax.broadcasted_iota(jnp.int32, s.shape, 0) <= lane(s.shape)
                s = jnp.where(ok, s, blocked)
            if first:
                keep_m, keep_acc = m[:, :first], acc[:, :first]
                m, acc = m[:, first:], acc[:, first:]
            new = jnp.maximum(m, jnp.max(s, axis=0, keepdims=True))
            p = jnp.exp(s - new)
            acc = acc * jnp.exp(m - new) + dot(vt[h, :, pl.ds(start, bk)], p.astype(bf16), 1, 0)
            if first:
                new, acc = jnp.concatenate([keep_m, new], axis=1), jnp.concatenate([keep_acc, acc], axis=1)
            out += [new, acc]
        return tuple(out)

    state = lax.fori_loop(
        0, i * (bq // bk), lambda j, st: block(j * bk, st, 0, False), tuple(state)
    )
    for jj in range(bq // bk):
        state = block(i * bq + jj * bk, state, jj * bk, True)
    outs, rows = [], []
    for h in (0, 1):
        m, acc = state[2 * h], state[2 * h + 1]
        total = acc[HEAD:HEAD + 1]
        outs.append(acc[:HEAD] / total)
        rows.append(-(m + jnp.log(total)))
    o_ref[...] = jnp.concatenate(outs, axis=0).T.astype(bf16)
    parts = [p for r in rows for p in split3(r)]
    pad = jnp.zeros((PAIR - 4 - len(parts), bq), f32)
    st = jnp.concatenate([jnp.zeros((4, bq), f32)] + parts + [pad], axis=0).T
    stat_ref[...] = (st + mq_ref[...].astype(f32)).astype(bf16)

def attn_fwd(qkv, pk, pv, mq, mk, pm):
    s_len = qkv.shape[0]
    bq, bk = min(2048, s_len), min(512, s_len)
    full = lambda c: pl.BlockSpec((s_len, PAIR), lambda i: (0, c))
    few = pl.BlockSpec((PREFIX_ROWS, PAIR), lambda i: (0, 0))
    row = pl.BlockSpec((bq, PAIR), lambda i: (i, 0))
    return pl.pallas_call(
        functools.partial(fwd_body, bq, bk),
        grid=(s_len // bq,),
        in_specs=[row, full(1), full(2), few, few, row, full(0), few],
        out_specs=[row, row],
        out_shape=[jax.ShapeDtypeStruct((s_len, PAIR), bf16)] * 2,
        scratch_shapes=[
            pltpu.VMEM((s_len, 2 * PAIR), bf16),
            pltpu.VMEM((2, VT_ROWS, s_len), bf16),
            pltpu.VMEM((PREFIX_ROWS, 2 * PAIR), bf16),
            pltpu.VMEM((2, VT_ROWS, PREFIX_ROWS), bf16),
            pltpu.VMEM((2, bq, 2 * PAIR), bf16),
        ],
        compiler_params=pltpu.CompilerParams(vmem_limit_bytes=48 << 20),
        cost_estimate=pl.CostEstimate(
            flops=2 * s_len * s_len * 512, bytes_accessed=s_len * PAIR * 16,
            transcendentals=s_len * s_len,
        ),
        name="attn_fwd",
    )(qkv, qkv, qkv, pk, pv, mq, mk, pm)


def bwd_body(bq, bk, q_ref, k_ref, v_ref, pk_ref, pv_ref, stat_ref, mk_ref, pm_ref, o_ref, do_ref,
             grad_ref, dp_ref, ka, va, kt, pka, pva, pkt, qh, dh, dk_acc, dv_acc, dpk_acc, dpv_acc):
    i = pl.program_id(0)
    s_len = k_ref.shape[0]

    @pl.when(i == 0)
    def _():
        ones = jnp.where(lane((s_len, PAIR)) < 3, 1.0, 0.0).astype(bf16)
        for h in (0, 1):
            l = lane((s_len, PAIR))
            mine = (l >= 4 + 3 * h) & (l < 7 + 3 * h)
            ka[h, :, :PAIR] = k_ref[...]
            ka[h, :, PAIR:] = jnp.where(mine, bf16(1), mk_ref[...])
            pka[h, :, :PAIR] = pk_ref[...]
            pka[h, :, PAIR:] = jnp.where(mine[:PREFIX_ROWS], bf16(1), pm_ref[...])
        va[:, :PAIR] = v_ref[...]
        va[:, PAIR:] = ones
        pva[:, :PAIR] = pv_ref[...]
        pva[:, PAIR:] = ones[:PREFIX_ROWS]
        kt[...] = k_ref[...].T
        pkt[...] = pk_ref[...].T
        dk_acc[...] = jnp.zeros_like(dk_acc)
        dv_acc[...] = jnp.zeros_like(dv_acc)
        dpk_acc[...] = jnp.zeros_like(dpk_acc)
        dpv_acc[...] = jnp.zeros_like(dpv_acc)

    q = q_ref[...] * bf16(0.125)
    do = do_ref[...]
    prod = do.astype(f32) * o_ref[...].astype(f32)
    for h in (0, 1):
        half = head_half(h, q.shape)
        qh[h, :, :PAIR] = jnp.where(half, q, bf16(0))
        qh[h, :, PAIR:] = stat_ref[...]
        dh[h, :, :PAIR] = jnp.where(half, do, bf16(0))
        delta = -jnp.sum(jnp.where(half, prod, 0.0), axis=1, keepdims=True)
        hi, mid, lo = split3(delta)
        l = lane((bq, PAIR))
        dh[h, :, PAIR:] = jnp.where(l == 0, hi, jnp.where(l == 1, mid, jnp.where(l == 2, lo, 0.0))).astype(bf16)

    dq_state = []
    for h in (0, 1):
        p = jnp.exp(dot(pka[h], qh[h], 1, 1))
        ds = (p * dot(pva[...], dh[h], 1, 1)).astype(bf16)
        dpv_acc[...] += dot(p.astype(bf16), dh[h, :, :PAIR], 1, 0)
        dpk_acc[...] += dot(ds, qh[h, :, :PAIR], 1, 0)
        dq_state.append(dot(pkt[h * HEAD:(h + 1) * HEAD, :], ds, 1, 0))

    def block(start, state, first, causal):
        start = pl.multiple_of(start, bk)
        at = pl.ds(start, bk)
        out = []
        dv = dk = None
        ss = [dot(ka[h, at, :], qh[h, first:, :], 1, 1) for h in (0, 1)]
        dps = [dot(va[at, :], dh[h, first:, :], 1, 1) for h in (0, 1)]
        for h in (0, 1):
            s = ss[h]
            p = jnp.exp(s)
            if causal:
                ok = lax.broadcasted_iota(jnp.int32, s.shape, 0) <= lane(s.shape)
                p = jnp.where(ok, p, 0.0)
            ds = (p * dps[h]).astype(bf16)
            a = dot(p.astype(bf16), dh[h, first:, :PAIR], 1, 0)
            b = dot(ds, qh[h, first:, :PAIR], 1, 0)
            dv = a if dv is None else dv + a
            dk = b if dk is None else dk + b
            c = dot(kt[h * HEAD:(h + 1) * HEAD, at], ds, 1, 0)
            if first:
                out.append(jnp.concatenate([state[h][:, :first], state[h][:, first:] + c], axis=1))
            else:
                out.append(state[h] + c)
        dv_acc[at, :] += dv
        dk_acc[at, :] += dk
        return tuple(out)

    state = lax.fori_loop(
        0, i * (bq // bk), lambda j, st: block(j * bk, st, 0, False), tuple(dq_state)
    )
    for jj in range(bq // bk):
        state = block(i * bq + jj * bk, state, jj * bk, True)
    grad_ref[pl.ds(pl.multiple_of(i * bq, bq), bq), :PAIR] = (
        (jnp.concatenate(state, axis=0) * 0.125).T.astype(bf16)
    )

    @pl.when(i == pl.num_programs(0) - 1)
    def _():
        grad_ref[:, PAIR : 2 * PAIR] = dk_acc[...].astype(bf16)
        grad_ref[:, 2 * PAIR :] = dv_acc[...].astype(bf16)
        dp_ref[0] = dpk_acc[...]
        dp_ref[1] = dpv_acc[...]

def attn_bwd(qkv, pk, pv, stat, mk, pm, o, do):
    s_len = qkv.shape[0]
    bq, bk = min(2048, s_len), min(256, s_len)
    full = lambda c: pl.BlockSpec((s_len, PAIR), lambda i: (0, c))
    few = pl.BlockSpec((PREFIX_ROWS, PAIR), lambda i: (0, 0))
    row = pl.BlockSpec((bq, PAIR), lambda i: (i, 0))
    return pl.pallas_call(
        functools.partial(bwd_body, bq, bk),
        grid=(s_len // bq,),
        in_specs=[row, full(1), full(2), few, few, row, full(0), few, row, row],
        out_specs=[
            pl.BlockSpec((s_len, 3 * PAIR), lambda i: (0, 0)),
            pl.BlockSpec((2, PREFIX_ROWS, PAIR), lambda i: (0, 0, 0)),
        ],
        out_shape=[
            jax.ShapeDtypeStruct((s_len, 3 * PAIR), bf16),
            jax.ShapeDtypeStruct((2, PREFIX_ROWS, PAIR), f32),
        ],
        scratch_shapes=[
            pltpu.VMEM((2, s_len, 2 * PAIR), bf16),
            pltpu.VMEM((s_len, 2 * PAIR), bf16),
            pltpu.VMEM((PAIR, s_len), bf16),
            pltpu.VMEM((2, PREFIX_ROWS, 2 * PAIR), bf16),
            pltpu.VMEM((PREFIX_ROWS, 2 * PAIR), bf16),
            pltpu.VMEM((PAIR, PREFIX_ROWS), bf16),
            pltpu.VMEM((2, bq, 2 * PAIR), bf16),
            pltpu.VMEM((2, bq, 2 * PAIR), bf16),
            pltpu.VMEM((s_len, PAIR), f32),
            pltpu.VMEM((s_len, PAIR), f32),
            pltpu.VMEM((PREFIX_ROWS, PAIR), f32),
            pltpu.VMEM((PREFIX_ROWS, PAIR), f32),
        ],
        compiler_params=pltpu.CompilerParams(vmem_limit_bytes=48 << 20),
        cost_estimate=pl.CostEstimate(
            flops=5 * s_len * s_len * 512, bytes_accessed=s_len * PAIR * 24,
            transcendentals=s_len * s_len,
        ),
        name="attn_bwd",
    )(qkv, qkv, qkv, pk, pv, stat, mk, pm, o, do)


def masks(lengths, s_len):
    e0 = lengths[0]; e1 = e0 + lengths[1]; e2 = e1 + lengths[2]
    pos = jnp.arange(s_len, dtype=jnp.int32)
    doc = sum((pos >= e).astype(jnp.int32) for e in (e0, e1, e2))
    l = lax.broadcasted_iota(jnp.int32, (s_len, PAIR), 1)
    same = l == doc[:, None]
    mq = jnp.where((l < 4) & ~same, blocked, 0.0).astype(bf16)
    mk = jnp.where((l < 4) & same, 1.0, 0.0).astype(bf16)
    r = lax.broadcasted_iota(jnp.int32, (PREFIX_ROWS, PAIR), 0)
    lp = lax.broadcasted_iota(jnp.int32, (PREFIX_ROWS, PAIR), 1)
    pm = jnp.where((r >= PREFIX) & (lp == 3), 1.0, 0.0).astype(bf16)
    return mq, mk, pm


def layer_norm(hidden):
    centered = hidden - jnp.mean(hidden, axis=-1, keepdims=True)
    return centered * lax.rsqrt(
        jnp.mean(centered * centered, axis=-1, keepdims=True) + norm_epsilon
    )


def gelu_tanh(values):
    return (
        0.5
        * values
        * (1.0 + jnp.tanh(0.7978845608028654 * (values + 0.044715 * values * values * values)))
    )


def reparam(embedding, inner_matrix, inner_shift, outer_matrix, outer_shift):
    hidden = jnp.tanh(
        jnp.dot(embedding, inner_matrix, precision=highest, preferred_element_type=f32)
        + inner_shift
    )
    return (
        jnp.dot(hidden, outer_matrix, precision=highest, preferred_element_type=f32) + outer_shift
    )


def halvings(count):
    steps = []
    while count > 1:
        count //= 2
        steps.append(count)
    return steps


def swap(value, axis, size, mask):
    return lax.ppermute(value, axis, [(i, i ^ mask) for i in range(size)])


def put(buffer, piece, starts):
    return lax.dynamic_update_slice(buffer, piece, starts)


def gather_dp(piece, dp):
    me = lax.axis_index("dp")
    near = 2 if dp % 2 == 0 else 1
    far = dp // near
    mine = me // near
    zero = (0,) * piece.ndim
    line = put(jnp.zeros((far,) + piece.shape, piece.dtype), piece[None], (mine,) + zero)
    for k in range(1, far):
        got = lax.ppermute(piece, "dp", [(i, (i + near * k) % dp) for i in range(dp)])
        line = put(line, got[None], (lax.rem(mine - k + far, far),) + zero)
    if near == 1:
        return line
    other = swap(line, "dp", dp, 1)
    side = lax.rem(me, 2)
    both = jnp.zeros((far, 2) + piece.shape, piece.dtype)
    both = put(both, line[:, None], (0, side) + zero)
    both = put(both, other[:, None], (0, 1 - side) + zero)
    return both.reshape((dp,) + piece.shape)


def spread_seq(value, seq):
    held = {0: value}
    for mask in halvings(seq):
        for r in list(held):
            held[r ^ mask] = swap(held[r], "seq", seq, mask)
    return [held[r] for r in range(seq)]


def exchange_seq(pieces, seq):
    return [pieces[0]] + [swap(pieces[r], "seq", seq, r) for r in range(1, seq)]


def shards(seq, dp, tokens, lengths, attend_weight, output_weight, expand_weight, shrink_weight,
           prefix_embed, inner_weight, inner_bias, outer_weight, outer_bias, cotangent):
    s = lax.axis_index("seq")
    rows, width = tokens.shape[1:]
    s_len = rows * seq
    cols = width // seq
    pairs = cols // PAIR
    token_rows = tokens[0].astype(f32)
    upstream = cotangent[0]

    normed_full, input_norm_back = jax.vjp(layer_norm, token_rows)
    normed_all = jnp.zeros((s_len, width), bf16)
    for r, got in enumerate(spread_seq(normed_full.astype(bf16), seq)):
        normed_all = put(normed_all, got, ((s ^ r) * rows, 0))

    shard_rows = attend_weight.shape[0]
    parts = attend_weight.reshape(shard_rows, 3, seq, pairs, PAIR)
    mine = lax.dynamic_index_in_dim(parts, s, 2, keepdims=False)
    attend_pairs = [
        gather_dp(mine[:, :, p].reshape(shard_rows, 3 * PAIR), dp).reshape(width, 3 * PAIR)
        for p in range(pairs)
    ]
    quarter = output_weight.shape[0] // seq
    got = spread_seq(
        gather_dp(lax.dynamic_slice_in_dim(output_weight, s * quarter, quarter, 0), dp), seq
    )
    full_output = jnp.zeros((dp, seq, quarter, width), bf16)
    for r in range(seq):
        full_output = put(full_output, got[r][:, None], (0, s ^ r, 0, 0))
    full_output = full_output.reshape(width, width)
    hidden = expand_weight.shape[1]
    chunk = hidden // dp // seq
    piece = lax.dynamic_index_in_dim(
        expand_weight.reshape(shard_rows, dp, seq, chunk), s, 2, keepdims=False
    ).reshape(shard_rows, dp * chunk)
    expand_parts = [w.reshape(width, dp * chunk) for w in spread_seq(gather_dp(piece, dp), seq)]
    piece = lax.dynamic_slice_in_dim(shrink_weight, s * chunk, chunk, 0)
    shrink_parts = [w.reshape(dp * chunk, width) for w in spread_seq(gather_dp(piece, dp), seq)]

    prefix_kv, reparam_back = jax.vjp(
        reparam, prefix_embed, inner_weight, inner_bias, outer_weight, outer_bias
    )
    padded = jnp.pad(prefix_kv.astype(bf16), ((0, PREFIX_ROWS - PREFIX), (0, 0)))
    prefix_mine = lax.dynamic_index_in_dim(
        padded.reshape(PREFIX_ROWS, 2, seq, pairs, PAIR), s, 2, keepdims=False
    )
    mask_q, mask_k, mask_p = masks(lengths[0], s_len)

    qkv, attended, stats, own_heads = [], [], [], []
    for p in range(pairs):
        projected = jnp.dot(normed_all, attend_pairs[p], preferred_element_type=f32).astype(bf16)
        out, stat = attn_fwd(projected, prefix_mine[:, 0, p], prefix_mine[:, 1, p], mask_q, mask_k, mask_p)
        qkv.append(projected)
        attended.append(out)
        stats.append(stat)
        own_heads.append(
            exchange_seq(
                [lax.dynamic_slice_in_dim(out, (s ^ r) * rows, rows, 0) for r in range(seq)], seq
            )
        )
    merged = jnp.zeros((rows, width), bf16)
    for p in range(pairs):
        for r in range(seq):
            merged = put(merged, own_heads[p][r], (0, (s ^ r) * cols + p * PAIR))
    residual_mid = token_rows + jnp.dot(merged, full_output, preferred_element_type=f32)
    normed_mid, mid_norm_back = jax.vjp(layer_norm, residual_mid)
    normed_mid = normed_mid.astype(bf16)
    outputs = residual_mid
    normed_grad = jnp.zeros((rows, width), f32)
    for up, down in zip(expand_parts, shrink_parts):
        expanded = jnp.dot(normed_mid, up, preferred_element_type=f32)
        activated, gelu_back = jax.vjp(gelu_tanh, expanded)
        outputs = outputs + jnp.dot(activated.astype(bf16), down, preferred_element_type=f32)
        expand_grad = gelu_back(dot(upstream, down, 1, 1))[0].astype(bf16)
        normed_grad = normed_grad + dot(expand_grad, up, 1, 1)
    mid_grad = upstream.astype(f32) + mid_norm_back(normed_grad)[0]
    out_grad = dot(mid_grad.astype(bf16), full_output, 1, 1).astype(bf16)

    partial = jnp.zeros((s_len, width), f32)
    prefix_terms = []
    for p in range(pairs):
        sent = [
            lax.dynamic_slice(out_grad, (0, (s ^ r) * cols + p * PAIR), (rows, PAIR))
            for r in range(seq)
        ]
        out_all = jnp.zeros((s_len, PAIR), bf16)
        for r, got in enumerate(exchange_seq(sent, seq)):
            out_all = put(out_all, got, ((s ^ r) * rows, 0))
        grads, prefix_part = attn_bwd(
            qkv[p], prefix_mine[:, 0, p], prefix_mine[:, 1, p], stats[p], mask_k, mask_p,
            attended[p], out_all,
        )
        partial = partial + dot(grads, attend_pairs[p], 1, 1)
        prefix_terms.append(prefix_part)

    blocks = {r: lax.dynamic_slice_in_dim(partial, (s ^ r) * rows, rows, 0) for r in range(seq)}
    for mask in reversed(halvings(seq)):
        keep = {r: blocks[r] for r in blocks if not r & mask}
        for r in keep:
            got = swap(blocks[r ^ mask].astype(bf16), "seq", seq, mask)
            keep[r] = blocks[r] + got.astype(f32)
        blocks = keep
    input_grad = mid_grad + input_norm_back(blocks[0])[0]

    prefix_sum = jnp.stack(prefix_terms, axis=2)
    for mask in halvings(dp):
        prefix_sum = prefix_sum + swap(prefix_sum, "dp", dp, mask)
    prefix_grad = jnp.zeros((2, PREFIX_ROWS, seq, pairs, PAIR), f32)
    for r, got in enumerate(spread_seq(prefix_sum, seq)):
        prefix_grad = put(prefix_grad, got[:, :, None], (0, 0, s ^ r, 0, 0))
    prefix_grad = prefix_grad[:, :PREFIX].reshape(2, PREFIX, width)
    back = reparam_back(jnp.concatenate([prefix_grad[0], prefix_grad[1]], axis=1))
    return (outputs.astype(bf16)[None], input_grad.astype(bf16)[None], *back, prefix_kv)


def solution(mesh):
    placed = (
        P("dp", "seq", None),
        P("dp", None),
        P("dp", None),
        P("dp", None),
        P("dp", None),
        P("dp", None),
        P(),
        P(),
        P(),
        P(),
        P(),
        P("dp", "seq", None),
    )
    return jax.shard_map(
        functools.partial(shards, mesh.shape["seq"], mesh.shape["dp"]),
        mesh=mesh,
        in_specs=placed,
        out_specs=(P("dp", "seq", None), P("dp", "seq", None), P(), P(), P(), P(), P(), P()),
        check_vma=False,
    )
```

```python
import functools

import jax
import jax.numpy as jnp
from jax import lax
from jax.experimental import pallas as pl
from jax.experimental.pallas import tpu as pltpu
from jax.sharding import PartitionSpec as P

PREFIX = 10
HEAD = 64
PAIR = 128
PREFIX_ROWS = 16
VT_ROWS = 80
blocked = -1e30
norm_epsilon = 1e-05
highest = lax.Precision.HIGHEST
f32, bf16 = jnp.float32, jnp.bfloat16
VMEM_LIMIT = 56 << 20
in_vmem = pl.BlockSpec(memory_space=pltpu.VMEM)
in_smem = pl.BlockSpec(memory_space=pltpu.SMEM)
in_place = pl.BlockSpec(memory_space=pl.ANY)


def params():
    return pltpu.CompilerParams(vmem_limit_bytes=VMEM_LIMIT)


def cost(flops, moved, special=0):
    return pl.CostEstimate(flops=int(flops), bytes_accessed=int(moved), transcendentals=int(special))


def like(shape, dtype=bf16):
    return jax.ShapeDtypeStruct(shape, dtype)


def dot(a, b, ca, cb):
    return lax.dot_general(a, b, (((ca,), (cb,)), ((), ())), preferred_element_type=f32)


def lane(shape):
    return lax.broadcasted_iota(jnp.int32, shape, len(shape) - 1)


def head_half(h, shape):
    l = lane(shape)
    return (l < HEAD) if h == 0 else (l >= HEAD)


def split3(v):
    hi = v.astype(bf16)
    r = v - hi.astype(f32)
    mid = r.astype(bf16)
    lo = (r - mid.astype(f32)).astype(bf16)
    return hi.astype(f32), mid.astype(f32), lo.astype(f32)


def at(index, size):
    return pl.ds(pl.multiple_of(index * size, size), size)


def normalize(hidden):
    centered = hidden - jnp.mean(hidden, axis=-1, keepdims=True)
    scale = lax.rsqrt(jnp.mean(centered * centered, axis=-1, keepdims=True) + norm_epsilon)
    return centered * scale, scale


def normalize_back(normed, scale, grad):
    return scale * (
        grad
        - jnp.mean(grad, axis=-1, keepdims=True)
        - normed * jnp.mean(grad * normed, axis=-1, keepdims=True)
    )


def cut_attend_body(seq, pairs, place, attend_ref, *outs):
    width = attend_ref.shape[1] // 3
    for p in range(pairs):
        for t in range(3):
            column = t * width + (place[0] * pairs + p) * PAIR
            outs[p][:, t * PAIR : (t + 1) * PAIR] = attend_ref[
                :, pl.ds(pl.multiple_of(column, PAIR), PAIR)
            ]


def cut_attend(seq, pairs, place, attend_weight):
    rows = attend_weight.shape[0]
    return pl.pallas_call(
        functools.partial(cut_attend_body, seq, pairs),
        in_specs=[in_smem, in_vmem],
        out_specs=[in_vmem] * pairs,
        out_shape=[like((rows, 3 * PAIR))] * pairs,
        cost_estimate=cost(0, attend_weight.size * 3),
        compiler_params=params(),
        name="cut_attend",
    )(place, attend_weight)


def cut_rest_body(seq, place, output_ref, expand_ref, shrink_ref, up_ref, down_ref):
    s = place[0]
    wide = output_ref.shape[1] // seq
    up_ref[:, :wide] = output_ref[:, at(s, wide)]
    up_ref[:, wide:] = expand_ref[:, at(s, expand_ref.shape[1] // seq)]
    part = shrink_ref.shape[0] // seq
    for x in range(seq // 2):
        down_ref[x * part : (x + 1) * part, :] = shrink_ref[at(2 * x + lax.rem(s, 2), part), :]


def cut_rest(seq, place, output_weight, expand_weight, shrink_weight):
    rows, width = output_weight.shape
    up_shape = (rows, (width + expand_weight.shape[1]) // seq)
    return pl.pallas_call(
        functools.partial(cut_rest_body, seq),
        in_specs=[in_smem, in_vmem, in_vmem, in_vmem],
        out_specs=[in_vmem] * 2,
        out_shape=[like(up_shape), like((shrink_weight.shape[0] // 2, width))],
        cost_estimate=cost(0, expand_weight.size * 6),
        compiler_params=params(),
        name="cut_rest",
    )(place, output_weight, expand_weight, shrink_weight)


def forward_body(seq, bq, bk, place, *refs):
    normed, (line, other, pk_ref, pv_ref, mq_ref, mk_ref, pm_ref) = refs[:seq], refs[seq : seq + 7]
    qkv_ref, stat_ref, weight_ref = refs[seq + 7 : seq + 10]
    outs, (ka, vt, pka, pvt, qh, o_all) = refs[seq + 10 : 2 * seq + 10], refs[2 * seq + 10 :]
    s = place[0]
    s_len = qkv_ref.shape[0]
    rows = s_len // seq
    count = line.shape[0]
    shard = line.shape[1]
    for j in range(count):
        weight_ref[at(place[1 + j], shard), :] = line[j]
        weight_ref[at(place[1 + count + j], shard), :] = other[j]
    for r in range(seq):
        got = jnp.dot(normed[r][...], weight_ref[...], preferred_element_type=f32)
        qkv_ref[at(lax.bitwise_xor(s, r), rows), :] = got.astype(bf16)
    ka[:, :PAIR] = qkv_ref[:, PAIR : 2 * PAIR]
    ka[:, PAIR:] = mk_ref[...]
    pka[:, :PAIR] = pk_ref[...]
    pka[:, PAIR:] = pm_ref[...]
    first_row = lax.broadcasted_iota(jnp.int32, (VT_ROWS - HEAD, s_len), 0) == 0
    ones = jnp.where(first_row, 1.0, 0.0).astype(bf16)
    vtr = qkv_ref[:, 2 * PAIR :].T
    pvr = pv_ref[...].T
    for h in (0, 1):
        vt[h, :HEAD, :] = vtr[h * HEAD : (h + 1) * HEAD, :]
        vt[h, HEAD:, :] = ones
        pvt[h, :HEAD, :] = pvr[h * HEAD : (h + 1) * HEAD, :]
        pvt[h, HEAD:, :] = ones[:, :PREFIX_ROWS]

    def block(start, state, first, causal):
        out = []
        start = pl.multiple_of(start, bk)
        scores = [dot(ka[pl.ds(start, bk), :], qh[h, first:, :], 1, 1) for h in (0, 1)]
        for h in (0, 1):
            m, acc = state[2 * h], state[2 * h + 1]
            x = scores[h]
            if causal:
                ok = lax.broadcasted_iota(jnp.int32, x.shape, 0) <= lane(x.shape)
                x = jnp.where(ok, x, blocked)
            if first:
                keep_m, keep_acc = m[:, :first], acc[:, :first]
                m, acc = m[:, first:], acc[:, first:]
            new = jnp.maximum(m, jnp.max(x, axis=0, keepdims=True))
            p = jnp.exp(x - new)
            acc = acc * jnp.exp(m - new) + dot(vt[h, :, pl.ds(start, bk)], p.astype(bf16), 1, 0)
            if first:
                new = jnp.concatenate([keep_m, new], axis=1)
                acc = jnp.concatenate([keep_acc, acc], axis=1)
            out += [new, acc]
        return tuple(out)

    for i in range(s_len // bq):
        span = slice(i * bq, (i + 1) * bq)
        q = qkv_ref[span, :PAIR] * bf16(0.125)
        for h in (0, 1):
            qh[h, :, :PAIR] = jnp.where(head_half(h, q.shape), q, bf16(0))
            qh[h, :, PAIR:] = mq_ref[span, :]
        state = []
        for h in (0, 1):
            x = dot(pka[...], qh[h], 1, 1)
            m = jnp.max(x, axis=0, keepdims=True)
            state += [m, dot(pvt[h], jnp.exp(x - m).astype(bf16), 1, 0)]
        state = tuple(state)
        if i:
            state = lax.fori_loop(
                0, i * (bq // bk), lambda j, st: block(j * bk, st, 0, False), state
            )
        for j in range(bq // bk):
            state = block(i * bq + j * bk, state, j * bk, True)
        tops, parts = [], []
        for h in (0, 1):
            m, acc = state[2 * h], state[2 * h + 1]
            total = acc[HEAD : HEAD + 1]
            tops.append(acc[:HEAD] / total)
            parts += split3(-(m + jnp.log(total)))
        o_all[span, :] = jnp.concatenate(tops, axis=0).T.astype(bf16)
        pad = jnp.zeros((PAIR - 4 - len(parts), bq), f32)
        logs = jnp.concatenate([jnp.zeros((4, bq), f32)] + parts + [pad], axis=0).T
        stat_ref[span, :] = (logs + mq_ref[span, :].astype(f32)).astype(bf16)
    for r in range(seq):
        outs[r][...] = o_all[at(lax.bitwise_xor(s, r), rows), :]


def attend_forward(place, normed, line, other, pk, pv, mq, mk, pm):
    seq = len(normed)
    rows, width = normed[0].shape
    s_len = rows * seq
    bq, bk = min(2048, s_len), min(512, s_len)
    return pl.pallas_call(
        functools.partial(forward_body, seq, bq, bk),
        in_specs=[in_smem] + [in_vmem] * (seq + 7),
        out_specs=[in_vmem] * (3 + seq),
        out_shape=[like((s_len, 3 * PAIR)), like((s_len, PAIR)), like((width, 3 * PAIR))]
        + [like((rows, PAIR))] * seq,
        scratch_shapes=[
            pltpu.VMEM((s_len, 2 * PAIR), bf16),
            pltpu.VMEM((2, VT_ROWS, s_len), bf16),
            pltpu.VMEM((PREFIX_ROWS, 2 * PAIR), bf16),
            pltpu.VMEM((2, VT_ROWS, PREFIX_ROWS), bf16),
            pltpu.VMEM((2, bq, 2 * PAIR), bf16),
            pltpu.VMEM((s_len, PAIR), bf16),
        ],
        compiler_params=params(),
        cost_estimate=cost(
            2 * s_len * s_len * 512 + 2 * s_len * width * 3 * PAIR, s_len * width * 3, s_len * s_len
        ),
        name="attend_forward",
    )(place, *normed, line, other, pk, pv, mq, mk, pm)


def backward_body(seq, bq, bk, place, *refs):
    (qkv_ref, pk_ref, pv_ref, stat_ref, mk_ref, pm_ref), refs = refs[:6], refs[6:]
    o_parts, do_parts, refs = refs[:seq], refs[seq : 2 * seq], refs[2 * seq :]
    grad_refs, (dp_ref,), refs = refs[:seq], refs[seq : seq + 1], refs[seq + 1 :]
    ka, va, kt, pka, pva, pkt, qh, dh, dk_acc, dv_acc, o_all, do_all, dq_all = refs
    s = place[0]
    s_len = qkv_ref.shape[0]
    rows = s_len // seq
    for r in range(seq):
        o_all[at(lax.bitwise_xor(s, r), rows), :] = o_parts[r][...]
        do_all[at(lax.bitwise_xor(s, r), rows), :] = do_parts[r][...]
    ones = jnp.where(lane((s_len, PAIR)) < 3, 1.0, 0.0).astype(bf16)
    l = lane((s_len, PAIR))
    k = qkv_ref[:, PAIR : 2 * PAIR]
    for h in (0, 1):
        mine = (l >= 4 + 3 * h) & (l < 7 + 3 * h)
        ka[h, :, :PAIR] = k
        ka[h, :, PAIR:] = jnp.where(mine, bf16(1), mk_ref[...])
        pka[h, :, :PAIR] = pk_ref[...]
        pka[h, :, PAIR:] = jnp.where(mine[:PREFIX_ROWS], bf16(1), pm_ref[...])
    va[:, :PAIR] = qkv_ref[:, 2 * PAIR :]
    va[:, PAIR:] = ones
    pva[:, :PAIR] = pv_ref[...]
    pva[:, PAIR:] = ones[:PREFIX_ROWS]
    kt[...] = k.T
    pkt[...] = pk_ref[...].T
    dk_acc[...] = jnp.zeros_like(dk_acc)
    dv_acc[...] = jnp.zeros_like(dv_acc)

    def block(start, state, first, causal):
        start = pl.multiple_of(start, bk)
        here = pl.ds(start, bk)
        out = []
        dv = dk = None
        scores = [dot(ka[h, here, :], qh[h, first:, :], 1, 1) for h in (0, 1)]
        dps = [dot(va[here, :], dh[h, first:, :], 1, 1) for h in (0, 1)]
        for h in (0, 1):
            p = jnp.exp(scores[h])
            if causal:
                ok = lax.broadcasted_iota(jnp.int32, p.shape, 0) <= lane(p.shape)
                p = jnp.where(ok, p, 0.0)
            ds = (p * dps[h]).astype(bf16)
            a = dot(p.astype(bf16), dh[h, first:, :PAIR], 1, 0)
            b = dot(ds, qh[h, first:, :PAIR], 1, 0)
            dv = a if dv is None else dv + a
            dk = b if dk is None else dk + b
            c = dot(kt[h * HEAD : (h + 1) * HEAD, here], ds, 1, 0)
            if first:
                out.append(jnp.concatenate([state[h][:, :first], state[h][:, first:] + c], axis=1))
            else:
                out.append(state[h] + c)
        dv_acc[here, :] += dv
        dk_acc[here, :] += dk
        return tuple(out)

    for i in range(s_len // bq):
        span = slice(i * bq, (i + 1) * bq)
        q = qkv_ref[span, :PAIR] * bf16(0.125)
        do = do_all[span, :]
        prod = do.astype(f32) * o_all[span, :].astype(f32)
        for h in (0, 1):
            half = head_half(h, q.shape)
            qh[h, :, :PAIR] = jnp.where(half, q, bf16(0))
            qh[h, :, PAIR:] = stat_ref[span, :]
            dh[h, :, :PAIR] = jnp.where(half, do, bf16(0))
            delta = -jnp.sum(jnp.where(half, prod, 0.0), axis=1, keepdims=True)
            hi, mid, lo = split3(delta)
            n = lane((bq, PAIR))
            dh[h, :, PAIR:] = jnp.where(
                n == 0, hi, jnp.where(n == 1, mid, jnp.where(n == 2, lo, 0.0))
            ).astype(bf16)
        state = []
        dpk = dpv = jnp.zeros((PREFIX_ROWS, PAIR), f32)
        for h in (0, 1):
            p = jnp.exp(dot(pka[h], qh[h], 1, 1))
            ds = (p * dot(pva[...], dh[h], 1, 1)).astype(bf16)
            dpv = dpv + dot(p.astype(bf16), dh[h, :, :PAIR], 1, 0)
            dpk = dpk + dot(ds, qh[h, :, :PAIR], 1, 0)
            state.append(dot(pkt[h * HEAD : (h + 1) * HEAD, :], ds, 1, 0))
        dp_ref[0] = dpk if i == 0 else dp_ref[0] + dpk
        dp_ref[1] = dpv if i == 0 else dp_ref[1] + dpv
        state = tuple(state)
        if i:
            state = lax.fori_loop(
                0, i * (bq // bk), lambda j, st: block(j * bk, st, 0, False), state
            )
        for j in range(bq // bk):
            state = block(i * bq + j * bk, state, j * bk, True)
        dq_all[span, :] = (jnp.concatenate(state, axis=0) * 0.125).T.astype(bf16)
    for r in range(seq):
        here = at(lax.bitwise_xor(s, r), rows)
        grad_refs[r][:, :PAIR] = dq_all[here, :]
        grad_refs[r][:, PAIR : 2 * PAIR] = dk_acc[here, :].astype(bf16)
        grad_refs[r][:, 2 * PAIR :] = dv_acc[here, :].astype(bf16)


def attend_backward(place, qkv, pk, pv, stat, mk, pm, o_parts, do_parts):
    seq = len(o_parts)
    s_len = qkv.shape[0]
    rows = s_len // seq
    bq, bk = min(2048, s_len), min(256, s_len)
    return pl.pallas_call(
        functools.partial(backward_body, seq, bq, bk),
        in_specs=[in_smem] + [in_vmem] * (6 + 2 * seq),
        out_specs=[in_vmem] * (seq + 1),
        out_shape=[like((rows, 3 * PAIR))] * seq + [like((2, PREFIX_ROWS, PAIR), f32)],
        scratch_shapes=[
            pltpu.VMEM((2, s_len, 2 * PAIR), bf16),
            pltpu.VMEM((s_len, 2 * PAIR), bf16),
            pltpu.VMEM((PAIR, s_len), bf16),
            pltpu.VMEM((2, PREFIX_ROWS, 2 * PAIR), bf16),
            pltpu.VMEM((PREFIX_ROWS, 2 * PAIR), bf16),
            pltpu.VMEM((PAIR, PREFIX_ROWS), bf16),
            pltpu.VMEM((2, bq, 2 * PAIR), bf16),
            pltpu.VMEM((2, bq, 2 * PAIR), bf16),
            pltpu.VMEM((s_len, PAIR), f32),
            pltpu.VMEM((s_len, PAIR), f32),
            pltpu.VMEM((s_len, PAIR), bf16),
            pltpu.VMEM((s_len, PAIR), bf16),
            pltpu.VMEM((s_len, PAIR), bf16),
        ],
        compiler_params=params(),
        cost_estimate=cost(5 * s_len * s_len * 512, s_len * PAIR * 24, s_len * s_len),
        name="attend_backward",
    )(place, qkv, pk, pv, stat, mk, pm, *o_parts, *do_parts)


def middle_body(seq, pairs, count, place, *refs):
    tokens_ref, cot_ref, refs = refs[0], refs[1], refs[2:]
    heads, refs = refs[: seq * pairs], refs[seq * pairs :]
    ups, refs = refs[: 2 * seq], refs[2 * seq :]
    downs, refs = refs[:4], refs[4:]
    out_ref, mid_grad_ref, refs = refs[0], refs[1], refs[2:]
    grads, refs = refs[: seq * pairs], refs[seq * pairs :]
    up, down, merged, mid, normed, out_acc, back_acc, sem_u, sem_d = refs
    s = place[0]
    rows, width = tokens_ref.shape
    shard = up.shape[1] // (2 * count)
    wide = width // seq
    part = down.shape[0] // (2 * count * seq)

    copies_u, copies_d = [], []
    for r in range(seq):
        owner = lax.bitwise_xor(s, r)
        for t in (0, 1):
            for j in range(count):
                copies_u.append(
                    pltpu.make_async_copy(
                        ups[2 * r + t].at[j],
                        up.at[owner, at(place[1 + t * count + j], shard)],
                        sem_u.at[(r * 2 + t) * count + j],
                    )
                )
    for c in (0, 1):
        owner = lax.bitwise_xor(lax.rem(s, 2), c)
        for t in (0, 1):
            for j in range(count):
                d = place[1 + t * count + j]
                for x in range(seq // 2):
                    n = ((c * 2 + t) * count + j) * (seq // 2) + x
                    first = (d * seq + 2 * x + owner) * part
                    copies_d.append(
                        pltpu.make_async_copy(
                            downs[2 * c + t].at[j, pl.ds(x * part, part)],
                            down.at[pl.ds(pl.multiple_of(first, part), part)],
                            sem_d.at[n],
                        )
                    )
    for copy in copies_u + copies_d:
        copy.start()
    for r in range(seq):
        for p in range(pairs):
            column = lax.bitwise_xor(s, r) * (pairs * PAIR) + p * PAIR
            merged[:, pl.ds(pl.multiple_of(column, PAIR), PAIR)] = heads[p * seq + r][...]
    for copy in copies_u:
        copy.wait()
    acc = tokens_ref[...].astype(f32) + jnp.concatenate(
        [dot(merged[...], up[o, :, :wide], 1, 0) for o in range(seq)], axis=1
    )
    mid[...] = acc
    normed[...] = normalize(acc)[0].astype(bf16)
    out_acc[...] = acc
    back_acc[...] = jnp.zeros_like(back_acc)
    for copy in copies_d:
        copy.wait()
    chunk = min(512, up.shape[2] - wide)
    inner = (up.shape[2] - wide) // chunk

    def step(h, carry):
        block, piece = h // inner, lax.rem(h, inner)
        w_up = up[block, :, pl.ds(pl.multiple_of(wide + piece * chunk, PAIR), chunk)]
        w_down = down[at(h, chunk), :]
        u = jnp.dot(normed[...], w_up, preferred_element_type=f32)
        gelu_grad = dot(cot_ref[...], w_down, 1, 1)
        square = u * u
        t = jnp.tanh(0.7978845608028654 * u * (1.0 + 0.044715 * square))
        half = 0.5 * (1.0 + t)
        slope = half + (0.5 * 0.7978845608028654) * u * (1.0 - t * t) * (
            1.0 + 3 * 0.044715 * square
        )
        activated = (u * half).astype(bf16)
        expand_grad = (gelu_grad * slope).astype(bf16)
        out_acc[...] += jnp.dot(activated, w_down, preferred_element_type=f32)
        back_acc[...] += dot(expand_grad, w_up, 1, 1)
        return carry

    lax.fori_loop(0, seq * inner, step, 0)
    out_ref[...] = out_acc[...].astype(bf16)
    again, scale = normalize(mid[...])
    mid_grad = cot_ref[...].astype(f32) + normalize_back(again, scale, back_acc[...])
    mid_grad_ref[...] = mid_grad
    rounded = mid_grad.astype(bf16)
    grad = sum(
        dot(rounded[:, o * wide : (o + 1) * wide], up[o, :, :wide], 1, 1) for o in range(seq)
    )
    merged[...] = grad.astype(bf16)
    for r in range(seq):
        for p in range(pairs):
            column = lax.bitwise_xor(s, r) * (pairs * PAIR) + p * PAIR
            grads[p * seq + r][...] = merged[:, pl.ds(pl.multiple_of(column, PAIR), PAIR)]


def middle(pairs, place, tokens, cot, heads, ups, downs, hidden):
    seq = len(heads) // pairs
    rows, width = tokens.shape
    count = ups[0].shape[0]
    dp = 2 * count
    return pl.pallas_call(
        functools.partial(middle_body, seq, pairs, count),
        in_specs=[in_smem, in_vmem, in_vmem]
        + [in_vmem] * len(heads)
        + [in_place] * (len(ups) + len(downs)),
        out_specs=[in_vmem] * (2 + len(heads)),
        out_shape=[like((rows, width)), like((rows, width), f32)]
        + [like((rows, PAIR))] * len(heads),
        scratch_shapes=[
            pltpu.VMEM((seq, width, (width + hidden) // seq), bf16),
            pltpu.VMEM((hidden, width), bf16),
            pltpu.VMEM((rows, width), bf16),
            pltpu.VMEM((rows, width), f32),
            pltpu.VMEM((rows, width), bf16),
            pltpu.VMEM((rows, width), f32),
            pltpu.VMEM((rows, width), f32),
            pltpu.SemaphoreType.DMA((seq * dp,)),
            pltpu.SemaphoreType.DMA((seq * dp,)),
        ],
        compiler_params=params(),
        cost_estimate=cost(
            8 * rows * width * hidden + 4 * rows * width * width,
            4 * width * hidden + 12 * rows * width,
            rows * hidden,
        ),
        name="middle",
    )(place, tokens, cot, *heads, *ups, *downs)


def finish_body(tokens_ref, mid_grad_ref, own_ref, got_ref, out_ref):
    normed, scale = normalize(tokens_ref[...].astype(f32))
    grad = own_ref[...] + got_ref[...].astype(f32)
    out_ref[...] = (mid_grad_ref[...] + normalize_back(normed, scale, grad)).astype(bf16)


def finish(tokens, mid_grad, own, got):
    return pl.pallas_call(
        finish_body,
        in_specs=[in_vmem] * 4,
        out_specs=in_vmem,
        out_shape=like(tokens.shape),
        compiler_params=params(),
        cost_estimate=cost(tokens.size * 20, tokens.size * 14),
        name="finish",
    )(tokens, mid_grad, own, got)


def masks(lengths, s_len):
    e0 = lengths[0]
    e1 = e0 + lengths[1]
    e2 = e1 + lengths[2]
    pos = jnp.arange(s_len, dtype=jnp.int32)
    doc = sum((pos >= e).astype(jnp.int32) for e in (e0, e1, e2))
    l = lax.broadcasted_iota(jnp.int32, (s_len, PAIR), 1)
    same = l == doc[:, None]
    mq = jnp.where((l < 4) & ~same, blocked, 0.0).astype(bf16)
    mk = jnp.where((l < 4) & same, 1.0, 0.0).astype(bf16)
    r = lax.broadcasted_iota(jnp.int32, (PREFIX_ROWS, PAIR), 0)
    lp = lax.broadcasted_iota(jnp.int32, (PREFIX_ROWS, PAIR), 1)
    pm = jnp.where((r >= PREFIX) & (lp == 3), 1.0, 0.0).astype(bf16)
    return mq, mk, pm


def reparam(embedding, inner_matrix, inner_shift, outer_matrix, outer_shift):
    hidden = jnp.tanh(
        jnp.dot(embedding, inner_matrix, precision=highest, preferred_element_type=f32)
        + inner_shift
    )
    return (
        jnp.dot(hidden, outer_matrix, precision=highest, preferred_element_type=f32) + outer_shift
    )


def halvings(count):
    steps = []
    while count > 1:
        count //= 2
        steps.append(count)
    return steps


def swap(value, axis, size, mask):
    return lax.ppermute(value, axis, [(i, i ^ mask) for i in range(size)])


def gather_dp(piece, dp):
    far = dp // 2
    line = [piece] + [
        lax.ppermute(piece, "dp", [(i, (i + 2 * k) % dp) for i in range(dp)]) for k in range(1, far)
    ]
    line = jnp.stack(line)
    return [line, swap(line, "dp", dp, 1)]


def places(dp):
    me = lax.axis_index("dp")
    far = dp // 2
    row, side = me // 2, lax.rem(me, 2)
    steps = lax.rem(row - jnp.arange(far, dtype=jnp.int32) + far, far) * 2
    head = jnp.reshape(lax.axis_index("seq"), (1,))
    return jnp.concatenate([head, steps + side, steps + 1 - side]).astype(jnp.int32)


def spread_seq(values, seq):
    held = {0: values}
    for mask in halvings(seq):
        for r in list(held):
            held[r ^ mask] = [swap(v, "seq", seq, mask) for v in held[r]]
    return [held[r] for r in range(seq)]


def exchange_seq(pieces, seq):
    return [pieces[0]] + [swap(pieces[r], "seq", seq, r) for r in range(1, seq)]


def shards(seq, dp, tokens, lengths, attend_weight, output_weight, expand_weight, shrink_weight,
           prefix_embed, inner_weight, inner_bias, outer_weight, outer_bias, cotangent):
    s = lax.axis_index("seq")
    rows, width = tokens.shape[1:]
    s_len = rows * seq
    pairs = width // seq // PAIR
    token_rows = tokens[0]
    place = places(dp)

    normed = normalize(token_rows.astype(f32))[0].astype(bf16)
    normed = [v[0] for v in spread_seq([normed], seq)]
    attend_pairs = [gather_dp(w, dp) for w in cut_attend(seq, pairs, place, attend_weight)]
    up, down = cut_rest(seq, place, output_weight, expand_weight, shrink_weight)
    ups = [w for pair in spread_seq(gather_dp(up, dp), seq) for w in pair]
    down = gather_dp(down, dp)
    downs = down + [swap(w, "seq", seq, 1) for w in down]

    prefix_kv, reparam_back = jax.vjp(
        reparam, prefix_embed, inner_weight, inner_bias, outer_weight, outer_bias
    )
    padded = jnp.pad(prefix_kv.astype(bf16), ((0, PREFIX_ROWS - PREFIX), (0, 0)))
    prefix_mine = lax.dynamic_index_in_dim(
        padded.reshape(PREFIX_ROWS, 2, seq, pairs, PAIR), s, 2, keepdims=False
    )
    prefix_pairs = [(prefix_mine[:, 0, p], prefix_mine[:, 1, p]) for p in range(pairs)]
    mask_q, mask_k, mask_p = masks(lengths[0], s_len)

    saved, heads = [], []
    for p in range(pairs):
        qkv, stat, weight, *outs = attend_forward(
            place, normed, *attend_pairs[p], *prefix_pairs[p], mask_q, mask_k, mask_p
        )
        saved.append((qkv, stat, weight, outs))
        heads += exchange_seq(outs, seq)
    outputs, mid_grad, *out_grads = middle(
        pairs, place, token_rows, cotangent[0], heads, ups, downs, expand_weight.shape[1]
    )
    grads, prefix_terms = [], []
    for p in range(pairs):
        qkv, stat, weight, outs = saved[p]
        got = exchange_seq(out_grads[p * seq : (p + 1) * seq], seq)
        *parts, prefix_part = attend_backward(
            place, qkv, *prefix_pairs[p], stat, mask_k, mask_p, outs, got
        )
        grads.append(parts)
        prefix_terms.append(prefix_part)

    blocks = {
        r: sum(dot(grads[p][r], saved[p][2], 1, 1) for p in range(pairs)) for r in range(seq)
    }
    got = None
    for mask in reversed(halvings(seq)):
        keep = {}
        for r in [r for r in blocks if not r & mask]:
            got = swap(blocks[r ^ mask].astype(bf16), "seq", seq, mask)
            keep[r] = blocks[r] if len(blocks) == 2 else blocks[r] + got.astype(f32)
        blocks = keep
    input_grad = finish(token_rows, mid_grad, blocks[0], got)

    prefix_sum = jnp.stack(prefix_terms, axis=2)
    for mask in halvings(dp):
        prefix_sum = prefix_sum + swap(prefix_sum, "dp", dp, mask)
    prefix_grad = jnp.zeros((2, PREFIX_ROWS, seq, pairs, PAIR), f32)
    for r, (got,) in enumerate(spread_seq([prefix_sum], seq)):
        prefix_grad = lax.dynamic_update_slice(prefix_grad, got[:, :, None], (0, 0, s ^ r, 0, 0))
    prefix_grad = prefix_grad[:, :PREFIX].reshape(2, PREFIX, width)
    back = reparam_back(jnp.concatenate([prefix_grad[0], prefix_grad[1]], axis=1))
    return (outputs[None], input_grad[None], *back, prefix_kv)


def solution(mesh):
    placed = (
        P("dp", "seq", None),
        P("dp", None),
        P("dp", None),
        P("dp", None),
        P("dp", None),
        P("dp", None),
        P(),
        P(),
        P(),
        P(),
        P(),
        P("dp", "seq", None),
    )
    return jax.shard_map(
        functools.partial(shards, mesh.shape["seq"], mesh.shape["dp"]),
        mesh=mesh,
        in_specs=placed,
        out_specs=(P("dp", "seq", None), P("dp", "seq", None), P(), P(), P(), P(), P(), P()),
        check_vma=False,
    )
```

```python
import functools

import jax
import jax.numpy as jnp
from jax import lax
from jax.experimental import pallas as pl
from jax.experimental.pallas import tpu as pltpu
from jax.sharding import PartitionSpec as P

PREFIX = 10
HEAD = 64
PAIR = 128
PREFIX_ROWS = 16
VT_ROWS = 80
blocked = -1e30
norm_epsilon = 1e-05
highest = lax.Precision.HIGHEST
f32, bf16 = jnp.float32, jnp.bfloat16
in_vmem = pl.BlockSpec(memory_space=pltpu.VMEM)
in_smem = pl.BlockSpec(memory_space=pltpu.SMEM)
in_place = pl.BlockSpec(memory_space=pl.ANY)


def params(mib):
    return pltpu.CompilerParams(vmem_limit_bytes=mib << 20)


def cost(flops, moved, special=0):
    return pl.CostEstimate(flops=int(flops), bytes_accessed=int(moved), transcendentals=int(special))


def like(shape, dtype=bf16):
    return jax.ShapeDtypeStruct(shape, dtype)


def dot(a, b, ca, cb):
    return lax.dot_general(a, b, (((ca,), (cb,)), ((), ())), preferred_element_type=f32)


def lane(shape):
    return lax.broadcasted_iota(jnp.int32, shape, len(shape) - 1)


def head_half(h, shape):
    l = lane(shape)
    return (l < HEAD) if h == 0 else (l >= HEAD)


def split3(v):
    hi = v.astype(bf16)
    r = v - hi.astype(f32)
    mid = r.astype(bf16)
    lo = (r - mid.astype(f32)).astype(bf16)
    return hi.astype(f32), mid.astype(f32), lo.astype(f32)


def at(index, size):
    return pl.ds(pl.multiple_of(index * size, size), size)


def normalize(hidden):
    centered = hidden - jnp.mean(hidden, axis=-1, keepdims=True)
    scale = lax.rsqrt(jnp.mean(centered * centered, axis=-1, keepdims=True) + norm_epsilon)
    return centered * scale, scale


def normalize_back(normed, scale, grad):
    return scale * (
        grad
        - jnp.mean(grad, axis=-1, keepdims=True)
        - normed * jnp.mean(grad * normed, axis=-1, keepdims=True)
    )


def cut_attend_body(seq, pairs, place, attend_ref, *outs):
    width = attend_ref.shape[1] // 3
    for p in range(pairs):
        for t in range(3):
            column = t * width + (place[0] * pairs + p) * PAIR
            outs[p][:, t * PAIR : (t + 1) * PAIR] = attend_ref[
                :, pl.ds(pl.multiple_of(column, PAIR), PAIR)
            ]


def cut_attend(seq, pairs, place, attend_weight):
    rows = attend_weight.shape[0]
    return pl.pallas_call(
        functools.partial(cut_attend_body, seq, pairs),
        in_specs=[in_smem, in_vmem],
        out_specs=[in_vmem] * pairs,
        out_shape=[like((rows, 3 * PAIR))] * pairs,
        cost_estimate=cost(0, attend_weight.size * 3),
        compiler_params=params(4),
        name="cut_attend",
    )(place, attend_weight)


def cut_rest_body(seq, place, output_ref, expand_ref, shrink_ref, first_ref, second_ref, down_ref):
    s = place[0]
    wide = output_ref.shape[1] // seq
    part = shrink_ref.shape[0] // seq
    half = second_ref.shape[1] // part
    first_ref[:, :wide] = output_ref[:, at(s, wide)]
    for d in range(2 * half):
        piece = expand_ref[:, at(d * seq + s, part)]
        if d < half:
            first_ref[:, wide + d * part : wide + (d + 1) * part] = piece
        else:
            second_ref[:, (d - half) * part : (d - half + 1) * part] = piece
    for x in range(seq // 2):
        down_ref[x * part : (x + 1) * part, :] = shrink_ref[at(2 * x + lax.rem(s, 2), part), :]


def cut_rest(seq, place, output_weight, expand_weight, shrink_weight):
    rows, width = output_weight.shape
    hidden = expand_weight.shape[1]
    part = shrink_weight.shape[0] // seq
    wide, half = width // seq, hidden // seq // 2
    if part % PAIR:
        s = lax.axis_index("seq")
        up = lax.dynamic_index_in_dim(
            expand_weight.reshape(rows, -1, seq, part), s, 2, keepdims=False
        ).reshape(rows, 2 * half)
        out = lax.dynamic_slice_in_dim(output_weight, s * wide, wide, 1)
        down = lax.dynamic_index_in_dim(
            shrink_weight.reshape(seq // 2, 2, part, width), lax.rem(s, 2), 1, keepdims=False
        ).reshape(seq // 2 * part, width)
        return jnp.concatenate([out, up[:, :half]], axis=1), up[:, half:], down
    return pl.pallas_call(
        functools.partial(cut_rest_body, seq),
        in_specs=[in_smem, in_vmem, in_vmem, in_vmem],
        out_specs=[in_vmem] * 3,
        out_shape=[
            like((rows, wide + half)),
            like((rows, half)),
            like((shrink_weight.shape[0] // 2, width)),
        ],
        cost_estimate=cost(0, expand_weight.size * 6),
        compiler_params=params(8),
        name="cut_rest",
    )(place, output_weight, expand_weight, shrink_weight)


def forward_body(seq, dp, bq, bk, place, *refs):
    normed, (line, other, pk_ref, pv_ref, mq_ref, mk_ref, pm_ref) = refs[:seq], refs[seq : seq + 7]
    qkv_ref, stat_ref, weight_ref = refs[seq + 7 : seq + 10]
    groups = seq // 2
    outs, refs = refs[seq + 10 : seq + 10 + groups], refs[seq + 10 + groups :]
    ka, vt, pka, pvt, qh, o_all = refs
    s = place[0]
    s_len = qkv_ref.shape[0]
    rows = s_len // seq
    count = line.shape[0]
    shard = line.shape[1]
    order = dp_masks(dp, False)[1]
    for j in range(count):
        weight_ref[at(lax.bitwise_xor(place[1], order[j]), shard), :] = line[j]
        weight_ref[at(lax.bitwise_xor(place[1], order[count + j]), shard), :] = other[j]
    for r in range(seq):
        got = jnp.dot(normed[r][...], weight_ref[...], preferred_element_type=f32)
        qkv_ref[at(lax.bitwise_xor(s, r), rows), :] = got.astype(bf16)
    ka[:, :PAIR] = qkv_ref[:, PAIR : 2 * PAIR]
    ka[:, PAIR:] = mk_ref[...]
    pka[:, :PAIR] = pk_ref[...]
    pka[:, PAIR:] = pm_ref[...]
    first_row = lax.broadcasted_iota(jnp.int32, (VT_ROWS - HEAD, s_len), 0) == 0
    ones = jnp.where(first_row, 1.0, 0.0).astype(bf16)
    vtr = qkv_ref[:, 2 * PAIR :].T
    pvr = pv_ref[...].T
    for h in (0, 1):
        vt[h, :HEAD, :] = vtr[h * HEAD : (h + 1) * HEAD, :]
        vt[h, HEAD:, :] = ones
        pvt[h, :HEAD, :] = pvr[h * HEAD : (h + 1) * HEAD, :]
        pvt[h, HEAD:, :] = ones[:, :PREFIX_ROWS]

    def block(start, state, first, causal):
        out = []
        start = pl.multiple_of(start, bk)
        scores = [dot(ka[pl.ds(start, bk), :], qh[h, first:, :], 1, 1) for h in (0, 1)]
        for h in (0, 1):
            m, acc = state[2 * h], state[2 * h + 1]
            x = scores[h]
            if causal:
                ok = lax.broadcasted_iota(jnp.int32, x.shape, 0) <= lane(x.shape)
                x = jnp.where(ok, x, blocked)
            if first:
                keep_m, keep_acc = m[:, :first], acc[:, :first]
                m, acc = m[:, first:], acc[:, first:]
            new = jnp.maximum(m, jnp.max(x, axis=0, keepdims=True))
            p = jnp.exp(x - new)
            acc = acc * jnp.exp(m - new) + dot(vt[h, :, pl.ds(start, bk)], p.astype(bf16), 1, 0)
            if first:
                new = jnp.concatenate([keep_m, new], axis=1)
                acc = jnp.concatenate([keep_acc, acc], axis=1)
            out += [new, acc]
        return tuple(out)

    for i in range(s_len // bq):
        span = slice(i * bq, (i + 1) * bq)
        q = qkv_ref[span, :PAIR] * bf16(0.125)
        for h in (0, 1):
            qh[h, :, :PAIR] = jnp.where(head_half(h, q.shape), q, bf16(0))
            qh[h, :, PAIR:] = mq_ref[span, :]
        state = []
        for h in (0, 1):
            x = dot(pka[...], qh[h], 1, 1)
            m = jnp.max(x, axis=0, keepdims=True)
            state += [m, dot(pvt[h], jnp.exp(x - m).astype(bf16), 1, 0)]
        state = tuple(state)
        if i:
            state = lax.fori_loop(
                0, i * (bq // bk), lambda j, st: block(j * bk, st, 0, False), state
            )
        for j in range(bq // bk):
            state = block(i * bq + j * bk, state, j * bk, True)
        tops, parts = [], []
        for h in (0, 1):
            m, acc = state[2 * h], state[2 * h + 1]
            total = acc[HEAD : HEAD + 1]
            tops.append(acc[:HEAD] / total)
            parts += split3(-(m + jnp.log(total)))
        o_all[span, :] = jnp.concatenate(tops, axis=0).T.astype(bf16)
        pad = jnp.zeros((PAIR - 4 - len(parts), bq), f32)
        logs = jnp.concatenate([jnp.zeros((4, bq), f32)] + parts + [pad], axis=0).T
        stat_ref[span, :] = (logs + mq_ref[span, :].astype(f32)).astype(bf16)
    for r in range(seq):
        outs[r // 2][r % 2 * rows : (r % 2 + 1) * rows, :] = o_all[at(lax.bitwise_xor(s, r), rows), :]


def attend_forward(place, normed, line, other, pk, pv, mq, mk, pm):
    seq = len(normed)
    rows, width = normed[0].shape
    s_len = rows * seq
    bq, bk = min(2048, s_len), min(512, s_len)
    return pl.pallas_call(
        functools.partial(forward_body, seq, 2 * line.shape[0], bq, bk),
        in_specs=[in_smem] + [in_vmem] * (seq + 7),
        out_specs=[in_vmem] * (3 + seq // 2),
        out_shape=[like((s_len, 3 * PAIR)), like((s_len, PAIR)), like((width, 3 * PAIR))]
        + [like((2 * rows, PAIR))] * (seq // 2),
        scratch_shapes=[
            pltpu.VMEM((s_len, 2 * PAIR), bf16),
            pltpu.VMEM((2, VT_ROWS, s_len), bf16),
            pltpu.VMEM((PREFIX_ROWS, 2 * PAIR), bf16),
            pltpu.VMEM((2, VT_ROWS, PREFIX_ROWS), bf16),
            pltpu.VMEM((2, bq, 2 * PAIR), bf16),
            pltpu.VMEM((s_len, PAIR), bf16),
        ],
        compiler_params=params(40),
        cost_estimate=cost(
            2 * s_len * s_len * 512 + 2 * s_len * width * 3 * PAIR, s_len * width * 3, s_len * s_len
        ),
        name="attend_forward",
    )(place, *normed, line, other, pk, pv, mq, mk, pm)


def backward_body(seq, bq, bk, place, *refs):
    (qkv_ref, pk_ref, pv_ref, stat_ref, mk_ref, pm_ref), refs = refs[:6], refs[6:]
    groups = seq // 2
    o_parts, do_parts, refs = refs[:groups], refs[groups : groups + seq], refs[groups + seq :]
    grad_refs, (dp_ref,), refs = refs[:seq], refs[seq : seq + 1], refs[seq + 1 :]
    ka, va, kt, pka, pva, pkt, qh, dh, dk_acc, dv_acc, o_all, do_all, dq_all = refs
    s = place[0]
    s_len = qkv_ref.shape[0]
    rows = s_len // seq
    for r in range(seq):
        o_all[at(lax.bitwise_xor(s, r), rows), :] = o_parts[r // 2][
            r % 2 * rows : (r % 2 + 1) * rows, :
        ]
        do_all[at(lax.bitwise_xor(s, r), rows), :] = do_parts[r][...]
    ones = jnp.where(lane((s_len, PAIR)) < 3, 1.0, 0.0).astype(bf16)
    l = lane((s_len, PAIR))
    k = qkv_ref[:, PAIR : 2 * PAIR]
    for h in (0, 1):
        mine = (l >= 4 + 3 * h) & (l < 7 + 3 * h)
        ka[h, :, :PAIR] = k
        ka[h, :, PAIR:] = jnp.where(mine, bf16(1), mk_ref[...])
        pka[h, :, :PAIR] = pk_ref[...]
        pka[h, :, PAIR:] = jnp.where(mine[:PREFIX_ROWS], bf16(1), pm_ref[...])
    va[:, :PAIR] = qkv_ref[:, 2 * PAIR :]
    va[:, PAIR:] = ones
    pva[:, :PAIR] = pv_ref[...]
    pva[:, PAIR:] = ones[:PREFIX_ROWS]
    kt[...] = k.T
    pkt[...] = pk_ref[...].T
    dk_acc[...] = jnp.zeros_like(dk_acc)
    dv_acc[...] = jnp.zeros_like(dv_acc)

    def block(start, state, first, causal):
        start = pl.multiple_of(start, bk)
        here = pl.ds(start, bk)
        out = []
        dv = dk = None
        scores = [dot(ka[h, here, :], qh[h, first:, :], 1, 1) for h in (0, 1)]
        dps = [dot(va[here, :], dh[h, first:, :], 1, 1) for h in (0, 1)]
        for h in (0, 1):
            p = jnp.exp(scores[h])
            if causal:
                ok = lax.broadcasted_iota(jnp.int32, p.shape, 0) <= lane(p.shape)
                p = jnp.where(ok, p, 0.0)
            ds = (p * dps[h]).astype(bf16)
            a = dot(p.astype(bf16), dh[h, first:, :PAIR], 1, 0)
            b = dot(ds, qh[h, first:, :PAIR], 1, 0)
            dv = a if dv is None else dv + a
            dk = b if dk is None else dk + b
            c = dot(kt[h * HEAD : (h + 1) * HEAD, here], ds, 1, 0)
            if first:
                out.append(jnp.concatenate([state[h][:, :first], state[h][:, first:] + c], axis=1))
            else:
                out.append(state[h] + c)
        dv_acc[here, :] += dv
        dk_acc[here, :] += dk
        return tuple(out)

    for i in range(s_len // bq):
        span = slice(i * bq, (i + 1) * bq)
        q = qkv_ref[span, :PAIR] * bf16(0.125)
        do = do_all[span, :]
        prod = do.astype(f32) * o_all[span, :].astype(f32)
        for h in (0, 1):
            half = head_half(h, q.shape)
            qh[h, :, :PAIR] = jnp.where(half, q, bf16(0))
            qh[h, :, PAIR:] = stat_ref[span, :]
            dh[h, :, :PAIR] = jnp.where(half, do, bf16(0))
            delta = -jnp.sum(jnp.where(half, prod, 0.0), axis=1, keepdims=True)
            hi, mid, lo = split3(delta)
            n = lane((bq, PAIR))
            dh[h, :, PAIR:] = jnp.where(
                n == 0, hi, jnp.where(n == 1, mid, jnp.where(n == 2, lo, 0.0))
            ).astype(bf16)
        state = []
        dpk = dpv = jnp.zeros((PREFIX_ROWS, PAIR), f32)
        for h in (0, 1):
            p = jnp.exp(dot(pka[h], qh[h], 1, 1))
            ds = (p * dot(pva[...], dh[h], 1, 1)).astype(bf16)
            dpv = dpv + dot(p.astype(bf16), dh[h, :, :PAIR], 1, 0)
            dpk = dpk + dot(ds, qh[h, :, :PAIR], 1, 0)
            state.append(dot(pkt[h * HEAD : (h + 1) * HEAD, :], ds, 1, 0))
        dp_ref[0] = dpk if i == 0 else dp_ref[0] + dpk
        dp_ref[1] = dpv if i == 0 else dp_ref[1] + dpv
        state = tuple(state)
        if i:
            state = lax.fori_loop(
                0, i * (bq // bk), lambda j, st: block(j * bk, st, 0, False), state
            )
        for j in range(bq // bk):
            state = block(i * bq + j * bk, state, j * bk, True)
        dq_all[span, :] = (jnp.concatenate(state, axis=0) * 0.125).T.astype(bf16)
    for r in range(seq):
        here = at(lax.bitwise_xor(s, r), rows)
        grad_refs[r][:, :PAIR] = dq_all[here, :]
        grad_refs[r][:, PAIR : 2 * PAIR] = dk_acc[here, :].astype(bf16)
        grad_refs[r][:, 2 * PAIR :] = dv_acc[here, :].astype(bf16)


def attend_backward(place, qkv, pk, pv, stat, mk, pm, o_parts, do_parts):
    seq = len(do_parts)
    s_len = qkv.shape[0]
    rows = s_len // seq
    bq, bk = min(2048, s_len), min(256, s_len)
    return pl.pallas_call(
        functools.partial(backward_body, seq, bq, bk),
        in_specs=[in_smem] + [in_vmem] * (6 + seq // 2 + seq),
        out_specs=[in_vmem] * (seq + 1),
        out_shape=[like((rows, 3 * PAIR))] * seq + [like((2, PREFIX_ROWS, PAIR), f32)],
        scratch_shapes=[
            pltpu.VMEM((2, s_len, 2 * PAIR), bf16),
            pltpu.VMEM((s_len, 2 * PAIR), bf16),
            pltpu.VMEM((PAIR, s_len), bf16),
            pltpu.VMEM((2, PREFIX_ROWS, 2 * PAIR), bf16),
            pltpu.VMEM((PREFIX_ROWS, 2 * PAIR), bf16),
            pltpu.VMEM((PAIR, PREFIX_ROWS), bf16),
            pltpu.VMEM((2, bq, 2 * PAIR), bf16),
            pltpu.VMEM((2, bq, 2 * PAIR), bf16),
            pltpu.VMEM((s_len, PAIR), f32),
            pltpu.VMEM((s_len, PAIR), f32),
            pltpu.VMEM((s_len, PAIR), bf16),
            pltpu.VMEM((s_len, PAIR), bf16),
            pltpu.VMEM((s_len, PAIR), bf16),
        ],
        compiler_params=params(44),
        cost_estimate=cost(5 * s_len * s_len * 512, s_len * PAIR * 24, s_len * s_len),
        name="attend_backward",
    )(place, qkv, pk, pv, stat, mk, pm, *o_parts, *do_parts)


def dp_masks(dp, near_first):
    masks = [1] + halvings(dp)[:-1] if near_first else halvings(dp)
    order = [0]
    for mask in masks:
        order += [i ^ mask for i in order]
    return masks, order


def middle_body(seq, pairs, dp, rows, place, *refs):
    groups = seq // 2
    tokens, cots, refs = refs[:2], refs[2:4], refs[4:]
    heads, refs = refs[: 2 * groups * pairs], refs[2 * groups * pairs :]
    firsts, seconds, refs = refs[: 2 * groups], refs[2 * groups : 4 * groups], refs[4 * groups :]
    across, (few, many), refs = refs[0], (refs[1:3], refs[3:5]), refs[5:]
    mid_ref, out_ref, out_give_ref, back_ref, back_give_ref, wo = refs[:6]
    up, down, merged, normed, active, grads, cot, sem_o, sem_u, sem_d = refs[6:]
    s, me = place[0], place[1]
    width = tokens[0].shape[1]
    shard = width // dp
    wide = width // seq
    half = seconds[0].shape[2]
    part = down.shape[1] // dp
    far_order = dp_masks(dp, False)[1]
    near_order = dp_masks(dp, True)[1]
    per_array = dp // 2

    copies_o, copies_u, copies_d = [], [], []

    def add(copies, sems, source, target):
        copies.append(pltpu.make_async_copy(source, target, sems.at[len(copies)]))

    for g in range(groups):
        owner = lax.bitwise_xor(s, 2 * g)
        for t in (0, 1):
            for j in range(per_array):
                d = lax.bitwise_xor(me, far_order[t * per_array + j])
                first, second = firsts[2 * g + t].at[j], seconds[2 * g + t].at[j]
                add(copies_o, sem_o, first.at[:, pl.ds(0, wide)], wo.at[owner, at(d, shard)])
                add(
                    copies_o,
                    sem_o,
                    across.at[2 * g + t, j],
                    wo.at[lax.bitwise_xor(owner, 1), at(d, shard)],
                )
                place_up = up.at[owner // 2, at(d, shard)]
                add(copies_u, sem_u, first.at[:, pl.ds(wide, half)], place_up.at[:, pl.ds(0, half)])
                add(copies_u, sem_u, second, place_up.at[:, pl.ds(half, half)])
    start = 0
    for arrays, order in ((few, near_order), (many, far_order)):
        size = arrays[0].shape[1]
        for t in (0, 1):
            for j in range(per_array):
                d = lax.bitwise_xor(me, order[t * per_array + j])
                done = 0
                while done < size:
                    x, row = (start + done) // part, (start + done) % part
                    take = min(part - row, size - done)
                    to = pl.multiple_of(d * part + row, min(take, part))
                    add(
                        copies_d,
                        sem_d,
                        arrays[t].at[j, pl.ds(done, take)],
                        down.at[x, pl.ds(to, take)],
                    )
                    done += take
        start += size
    for copy in copies_o + copies_u + copies_d:
        copy.start()
    for p in range(pairs):
        for g in range(groups):
            for flip in (0, 1):
                source = heads[(p * groups + g) * 2 + flip]
                owner = lax.bitwise_xor(s, 2 * g + flip)
                column = pl.ds(pl.multiple_of(owner * (pairs * PAIR) + p * PAIR, PAIR), PAIR)
                for k in (0, 1):
                    here = k ^ flip
                    merged[k * rows : (k + 1) * rows, column] = source[
                        here * rows : (here + 1) * rows, :
                    ]
    for k in (0, 1):
        cot[k * rows : (k + 1) * rows, :] = cots[k][...]
    for copy in copies_o:
        copy.wait()
    both = jnp.concatenate([dot(merged[...], wo[o], 1, 0) for o in range(seq)], axis=1)
    for k in (0, 1):
        acc = tokens[k][...].astype(f32) + both[k * rows : (k + 1) * rows]
        if k == 0:
            mid_ref[...] = acc
        normed[k * rows : (k + 1) * rows, :] = normalize(acc)[0].astype(bf16)
    for copy in copies_u + copies_d:
        copy.wait()
    chunk = min(512, 2 * half)
    inner = 2 * half // chunk

    def step(h, carry):
        block, piece = h // inner, lax.rem(h, inner)
        w_up = up[block, :, at(piece, chunk)]
        w_down = down[block, at(piece, chunk), :]
        u = jnp.dot(normed[...], w_up, preferred_element_type=f32)
        gelu_grad = dot(cot[...], w_down, 1, 1)
        square = u * u
        t = jnp.tanh(0.7978845608028654 * u * (1.0 + 0.044715 * square))
        side = 0.5 * (1.0 + t)
        slope = side + (0.5 * 0.7978845608028654) * u * (1.0 - t * t) * (
            1.0 + 3 * 0.044715 * square
        )
        active[block, :, at(piece, chunk)] = (u * side).astype(bf16)
        grads[block, :, at(piece, chunk)] = (gelu_grad * slope).astype(bf16)
        return carry

    lax.fori_loop(0, groups * inner, step, 0)
    first, last = slice(0, rows), slice(rows, 2 * rows)
    for give_ref, own_ref, left, right, side in (
        (back_give_ref, back_ref, grads, up, 1),
        (out_give_ref, out_ref, active, down, 0),
    ):
        give_ref[...] = sum(
            dot(left[g, last, :], right[g], 1, side) for g in range(groups)
        ).astype(bf16)
        total = sum(dot(left[g, first, :], right[g], 1, side) for g in range(groups))
        own_ref[...] = total if side else mid_ref[...] + total


def middle(seq, dp, pairs, place, tokens, cots, heads, firsts, seconds, across, few, many):
    rows, width = tokens[0].shape
    groups = seq // 2
    half = seconds[0].shape[2]
    part = (few[0].shape[1] + many[0].shape[1]) // groups
    spans = 0
    start = 0
    for arrays in (few, many):
        size = arrays[0].shape[1]
        spans += (start + size - 1) // part - start // part + 1
        start += size
    hidden = groups * 2 * half
    return pl.pallas_call(
        functools.partial(middle_body, seq, pairs, dp, rows),
        in_specs=[in_smem]
        + [in_vmem] * (4 + len(heads))
        + [in_place] * (len(firsts) + len(seconds) + 5),
        out_specs=[in_vmem] * 6,
        out_shape=[
            like((rows, width), f32),
            like((rows, width), f32),
            like((rows, width)),
            like((rows, width), f32),
            like((rows, width)),
            like((seq, width, width // seq)),
        ],
        scratch_shapes=[
            pltpu.VMEM((groups, width, 2 * half), bf16),
            pltpu.VMEM((groups, dp * part, width), bf16),
            pltpu.VMEM((2 * rows, width), bf16),
            pltpu.VMEM((2 * rows, width), bf16),
            pltpu.VMEM((groups, 2 * rows, 2 * half), bf16),
            pltpu.VMEM((groups, 2 * rows, 2 * half), bf16),
            pltpu.VMEM((2 * rows, width), bf16),
            pltpu.SemaphoreType.DMA((seq * dp,)),
            pltpu.SemaphoreType.DMA((seq * dp,)),
            pltpu.SemaphoreType.DMA((spans * dp,)),
        ],
        compiler_params=params(58),
        cost_estimate=cost(
            16 * rows * width * hidden + 4 * rows * width * width,
            4 * width * hidden + 20 * rows * width,
            2 * rows * hidden,
        ),
        name="middle",
    )(place, *tokens, *cots, *heads, *firsts, *seconds, across, *few, *many)


def turn_body(seq, pairs, place, mid_ref, cot_ref, own_ref, got_ref, wo, *refs):
    mid_grad_ref, grads, (merged,) = refs[0], refs[1:-1], refs[-1:]
    s = place[0]
    wide = wo.shape[2]
    normed, scale = normalize(mid_ref[...])
    grad = own_ref[...] + got_ref[...].astype(f32)
    mid_grad = cot_ref[...].astype(f32) + normalize_back(normed, scale, grad)
    mid_grad_ref[...] = mid_grad
    rounded = mid_grad.astype(bf16)
    grad = sum(dot(rounded[:, o * wide : (o + 1) * wide], wo[o], 1, 1) for o in range(seq))
    merged[...] = grad.astype(bf16)
    for r in range(seq):
        for p in range(pairs):
            column = lax.bitwise_xor(s, r) * (pairs * PAIR) + p * PAIR
            grads[p * seq + r][...] = merged[:, pl.ds(pl.multiple_of(column, PAIR), PAIR)]


def turn(seq, pairs, place, mid, cot, own, got, wo):
    rows, width = mid.shape
    return pl.pallas_call(
        functools.partial(turn_body, seq, pairs),
        in_specs=[in_smem] + [in_vmem] * 5,
        out_specs=[in_vmem] * (1 + seq * pairs),
        out_shape=[like((rows, width), f32)] + [like((rows, PAIR))] * (seq * pairs),
        scratch_shapes=[pltpu.VMEM((rows, width), bf16)],
        compiler_params=params(24),
        cost_estimate=cost(2 * rows * width * width, 16 * rows * width),
        name="turn",
    )(place, mid, cot, own, got, wo)


def finish_body(tokens_ref, mid_grad_ref, own_ref, got_ref, out_ref):
    normed, scale = normalize(tokens_ref[...].astype(f32))
    grad = own_ref[...] + got_ref[...].astype(f32)
    out_ref[...] = (mid_grad_ref[...] + normalize_back(normed, scale, grad)).astype(bf16)


def finish(tokens, mid_grad, own, got):
    return pl.pallas_call(
        finish_body,
        in_specs=[in_vmem] * 4,
        out_specs=in_vmem,
        out_shape=like(tokens.shape),
        compiler_params=params(24),
        cost_estimate=cost(tokens.size * 20, tokens.size * 14),
        name="finish",
    )(tokens, mid_grad, own, got)


def masks(lengths, s_len):
    e0 = lengths[0]
    e1 = e0 + lengths[1]
    e2 = e1 + lengths[2]
    pos = jnp.arange(s_len, dtype=jnp.int32)
    doc = sum((pos >= e).astype(jnp.int32) for e in (e0, e1, e2))
    l = lax.broadcasted_iota(jnp.int32, (s_len, PAIR), 1)
    same = l == doc[:, None]
    mq = jnp.where((l < 4) & ~same, blocked, 0.0).astype(bf16)
    mk = jnp.where((l < 4) & same, 1.0, 0.0).astype(bf16)
    r = lax.broadcasted_iota(jnp.int32, (PREFIX_ROWS, PAIR), 0)
    lp = lax.broadcasted_iota(jnp.int32, (PREFIX_ROWS, PAIR), 1)
    pm = jnp.where((r >= PREFIX) & (lp == 3), 1.0, 0.0).astype(bf16)
    return mq, mk, pm


def precise(a, b, ca, cb):
    return lax.dot_general(
        a, b, (((ca,), (cb,)), ((), ())), precision=highest, preferred_element_type=f32
    )


def norm_body(rows_ref, out_ref):
    out_ref[...] = normalize(rows_ref[...].astype(f32))[0].astype(bf16)


def norm(rows):
    return pl.pallas_call(
        norm_body,
        in_specs=[in_vmem],
        out_specs=in_vmem,
        out_shape=like(rows.shape),
        compiler_params=params(8),
        cost_estimate=cost(rows.size * 8, rows.size * 4),
        name="norm",
    )(rows)


def reparam_body(seq, pairs, place, embed, inner, inner_bias, outer, outer_bias, kv, hidden, *parts):
    s = place[0]
    half = outer.shape[1] // 2
    hidden[...] = jnp.tanh(precise(embed[...], inner[...], 1, 0) + inner_bias[...])
    both = precise(hidden[...], outer[...], 1, 0) + outer_bias[...]
    kv[...] = both[:PREFIX]
    *parts, held = parts
    row = lax.broadcasted_iota(jnp.int32, both.shape, 0)
    held[...] = jnp.where(row < PREFIX, both, 0.0)
    for t in (0, 1):
        for p in range(pairs):
            column = pl.multiple_of(t * half + (s * pairs + p) * PAIR, PAIR)
            parts[t * pairs + p][...] = held[:, pl.ds(column, PAIR)].astype(bf16)


def reparam(seq, pairs, place, embed, inner, inner_bias, outer, outer_bias):
    width = outer.shape[1]
    return pl.pallas_call(
        functools.partial(reparam_body, seq, pairs),
        in_specs=[in_smem] + [in_vmem] * 5,
        out_specs=[in_vmem] * (2 + 2 * pairs),
        out_shape=[like((PREFIX, width), f32), like((PREFIX_ROWS, inner.shape[1]), f32)]
        + [like((PREFIX_ROWS, PAIR))] * (2 * pairs),
        scratch_shapes=[pltpu.VMEM((PREFIX_ROWS, width), f32)],
        compiler_params=params(20),
        cost_estimate=cost(12 * PREFIX_ROWS * (inner.size + outer.size), 4 * (inner.size + outer.size)),
        name="reparam",
    )(place, embed, inner, inner_bias[None], outer, outer_bias[None])


def reparam_back_body(seq, pairs, place, embed, inner, outer, hidden, *refs):
    got, (d_embed, d_inner, d_inner_bias, d_outer, d_outer_bias, grad) = refs[:seq], refs[seq:]
    s = place[0]
    half = outer.shape[1] // 2
    for r in range(seq):
        for t in (0, 1):
            for p in range(pairs):
                column = t * half + (lax.bitwise_xor(s, r) * pairs + p) * PAIR
                grad[:, pl.ds(pl.multiple_of(column, PAIR), PAIR)] = got[r][p, t]
    d_outer_bias[...] = jnp.sum(grad[...], axis=0, keepdims=True)
    d_outer[...] = precise(hidden[...].T, grad[...], 1, 0)
    back = precise(grad[...], outer[...], 1, 1) * (1.0 - hidden[...] * hidden[...])
    d_inner_bias[...] = jnp.sum(back, axis=0, keepdims=True)
    d_inner[...] = precise(embed[...].T, back, 1, 0)
    d_embed[...] = precise(back, inner[...], 1, 1)[:PREFIX]


def reparam_back(pairs, place, embed, inner, outer, hidden, got):
    seq = len(got)
    wide, (deep, width) = inner.shape[0], outer.shape
    outs = pl.pallas_call(
        functools.partial(reparam_back_body, seq, pairs),
        in_specs=[in_smem] + [in_vmem] * (4 + seq),
        out_specs=[in_vmem] * 5,
        out_shape=[
            like((PREFIX, wide), f32),
            like((wide, deep), f32),
            like((1, deep), f32),
            like((deep, width), f32),
            like((1, width), f32),
        ],
        scratch_shapes=[pltpu.VMEM((PREFIX_ROWS, width), f32)],
        compiler_params=params(28),
        cost_estimate=cost(24 * PREFIX_ROWS * (inner.size + outer.size), 8 * (inner.size + outer.size)),
        name="reparam_back",
    )(place, embed, inner, outer, hidden, *got)
    return outs[0], outs[1], outs[2][0], outs[3], outs[4][0]


def product_body(pairs, adds, out_dtype, *refs):
    weights, refs = refs[:pairs], refs[pairs:]
    count = len(refs) // (pairs + adds + 1)
    rows, refs = refs[: count * pairs], refs[count * pairs :]
    extra, outs = refs[: count * adds], refs[count * adds :]
    for i in range(count):
        total = sum(dot(rows[i * pairs + p][...], weights[p][...], 1, 1) for p in range(pairs))
        if adds:
            total = total + extra[i][...].astype(f32)
        outs[i][...] = total.astype(out_dtype)


def product(weights, rows, extra, out_dtype):
    pairs = len(weights)
    height, width = rows[0][0].shape[0], weights[0].shape[0]
    flat = [w for entry in rows for w in entry]
    return pl.pallas_call(
        functools.partial(product_body, pairs, int(bool(extra)), out_dtype),
        in_specs=[in_vmem] * (pairs + len(flat) + len(extra)),
        out_specs=[in_vmem] * len(rows),
        out_shape=[like((height, width), out_dtype)] * len(rows),
        compiler_params=params(24),
        cost_estimate=cost(
            2 * len(flat) * height * width * flat[0].shape[1], 4 * len(rows) * height * width
        ),
        name="product",
    )(*weights, *flat, *extra)


def halvings(count):
    steps = []
    while count > 1:
        count //= 2
        steps.append(count)
    return steps


def swap(value, axis, size, mask):
    return lax.ppermute(value, axis, [(i, i ^ mask) for i in range(size)])


def after(value, *events):
    return lax.optimization_barrier((value, *events))[0] if events else value


def spread_seq(value, seq):
    held = {0: value}
    for mask in halvings(seq):
        for r in list(held):
            held[r ^ mask] = swap(held[r], "seq", seq, mask)
    return [held[r] for r in range(seq)]


def exchange_seq(pieces, seq):
    return [pieces[0]] + [swap(pieces[r], "seq", seq, r) for r in range(1, seq)]


def shards(seq, dp, tokens, lengths, attend_weight, output_weight, expand_weight, shrink_weight,
           prefix_embed, inner_weight, inner_bias, outer_weight, outer_bias, cotangent):
    s = lax.axis_index("seq")
    rows, width = tokens.shape[1:]
    s_len = rows * seq
    pairs = width // seq // PAIR
    groups = seq // 2
    token_rows, cot_rows = tokens[0], cotangent[0]
    place = jnp.stack([s, lax.axis_index("dp")]).astype(jnp.int32)
    near_mask, far_masks = dp_masks(dp, False)[0][-1], dp_masks(dp, False)[0][:-1]

    def over(value, mask, *events):
        return swap(after(value, *events), "dp", dp, mask)

    def other_core(value, *events):
        return swap(after(value, *events), "seq", seq, 1)

    def line(piece, begin=(), later=()):
        held, arrived = piece, []
        for mask in far_masks:
            arrived.append(over(held, mask, *(later if arrived else begin)))
            held = jnp.concatenate([held, arrived[-1]])
        return held, arrived

    def spread(value, *events):
        held = {0: after(value, *events)}
        for mask in halvings(seq)[:-1]:
            for g in list(held):
                held[g ^ mask // 2] = swap(held[g], "seq", seq, mask)
        return [held[g] for g in range(groups)]

    token_far = spread(token_rows)
    token_pair = (token_rows, other_core(token_rows))
    cot_pair = (cot_rows, other_core(cot_rows))
    attend_lines = [
        line(w[None], later=(token_pair[1], cot_pair[1]))
        for w in cut_attend(seq, pairs, place, attend_weight)
    ]
    first, second, down = cut_rest(seq, place, output_weight, expand_weight, shrink_weight)
    quarter = down.shape[0] // 4
    few = over(down[None, :quarter], near_mask, attend_lines[0][1][0])
    few = jnp.concatenate([down[None, :quarter], few])
    attend_pairs = [(w, over(w, near_mask)) for w, _ in attend_lines]
    normed_rows = [norm(w) for w in token_pair]
    line_a, steps_a = line(
        first[None],
        (few, *[steps[-1] for _, steps in attend_lines]),
        (attend_pairs[0][1],),
    )
    for w in token_far[1:]:
        normed_rows += [norm(w), norm(other_core(w))]
    line_b, steps_b = line(second[None], (steps_a[0], attend_pairs[0][1]), (attend_pairs[-1][1],))

    embed = after(prefix_embed, attend_lines[-1][1][-1])
    embed = jnp.pad(embed, ((0, PREFIX_ROWS - PREFIX), (0, 0)))
    prefix_kv, prefix_hidden, *prefix_parts = reparam(
        seq, pairs, place, embed, inner_weight, inner_bias, outer_weight, outer_bias
    )
    prefix_pairs = [(prefix_parts[p], prefix_parts[pairs + p]) for p in range(pairs)]
    mask_q, mask_k, mask_p = masks(lengths[0], s_len)
    saved, heads = [], []

    def attend(p, *events):
        qkv, stat, weight, *outs = attend_forward(
            after(place, *events), normed_rows, *attend_pairs[p], *prefix_pairs[p],
            mask_q, mask_k, mask_p,
        )
        saved.append((qkv, stat, weight, outs))
        for g in range(groups):
            got = outs[0] if g == 0 else swap(outs[g], "seq", seq, 2 * g)
            heads.extend((got, other_core(got)))

    attend(0, attend_pairs[-1][1], steps_a[-1], steps_b[0])
    other_a = over(line_a, near_mask, attend_pairs[-1][1])
    near_a = spread(line_a, normed_rows[-1])
    many = over(down[None, quarter:], far_masks[0], steps_b[0])
    many = jnp.concatenate([down[None, quarter:], many])
    begun = saved[0][1]
    other_b = over(line_b, near_mask, begun, other_a)
    far_a = spread(other_a, begun, *near_a)
    for mask in far_masks[1:]:
        many = jnp.concatenate([many, over(many, mask, begun, steps_b[-1])])
    for p in range(1, pairs):
        attend(p, other_a, *near_a, steps_b[-1])
    ended = saved[-1][1]
    many = (many, over(many, near_mask, ended, other_b, *far_a, *heads[: 2 * groups]))
    near_b = spread(line_b, ended, *far_a)
    far_b = spread(other_b, ended, *far_a)
    for mask in far_masks[:-1]:
        few = jnp.concatenate([few, over(few, mask, ended)])
    few = (few, over(few, far_masks[-1], *heads, *near_b))
    ups = [
        [w for g in range(groups) for w in (a[g], b[g])]
        for a, b in ((near_a, far_a), (near_b, far_b))
    ]
    wide = width // seq
    across = other_core(jnp.stack([w[..., :wide] for w in ups[0]]))
    mid, out_own, out_give, back_own, back_give, wo = middle(
        seq, dp, pairs, place, token_pair, cot_pair, heads, *ups, across, few, many
    )
    mid_grad, *out_grads = turn(
        seq, pairs, place, mid, cot_rows, back_own, other_core(back_give), wo
    )
    outputs = (out_own + other_core(out_give).astype(f32)).astype(bf16)
    grads, prefix_terms = [], []
    for p in range(pairs):
        qkv, stat, weight, outs = saved[p]
        got = exchange_seq(out_grads[p * seq : (p + 1) * seq], seq)
        *parts, prefix_part = attend_backward(
            place, qkv, *prefix_pairs[p], stat, mask_k, mask_p, outs, got
        )
        grads.append(parts)
        prefix_terms.append(prefix_part)

    weights = [entry[2] for entry in saved]
    block = lambda r: [grads[p][r] for p in range(pairs)]
    sent = product(weights, [block(r) for r in range(1, seq, 2)], [], bf16)
    got = [other_core(v) for v in sent]
    evens = product(weights, [block(r) for r in range(2, seq, 2)], got[1:], bf16)
    (own,) = product(weights, [block(0)], got[:1], f32)
    left = dict(zip(range(2, seq, 2), evens))
    for mask in reversed(halvings(seq)[:-1]):
        keep = {}
        for r in [0, *left]:
            if r & mask:
                continue
            arrived = swap(left[r ^ mask], "seq", seq, mask)
            if r:
                keep[r] = left[r] + arrived
            elif len(left) > 1:
                own = own + arrived.astype(f32)
        left = keep
    input_grad = finish(token_rows, mid_grad, own, arrived)

    prefix_sum = jnp.stack(prefix_terms)
    for mask in halvings(dp):
        prefix_sum = prefix_sum + swap(prefix_sum, "dp", dp, mask)
    back = reparam_back(
        pairs, place, embed, inner_weight, outer_weight, prefix_hidden, spread_seq(prefix_sum, seq)
    )
    return (outputs[None], input_grad[None], *back, prefix_kv)


def solution(mesh):
    placed = (
        P("dp", "seq", None),
        P("dp", None),
        P("dp", None),
        P("dp", None),
        P("dp", None),
        P("dp", None),
        P(),
        P(),
        P(),
        P(),
        P(),
        P("dp", "seq", None),
    )
    return jax.shard_map(
        functools.partial(shards, mesh.shape["seq"], mesh.shape["dp"]),
        mesh=mesh,
        in_specs=placed,
        out_specs=(P("dp", "seq", None), P("dp", "seq", None), P(), P(), P(), P(), P(), P()),
        check_vma=False,
    )
```

```python
import functools

import jax
import jax.numpy as jnp
from jax import lax
from jax.experimental import pallas as pl
from jax.experimental.pallas import tpu as pltpu
from jax.sharding import PartitionSpec as P

PREFIX = 10
HEAD = 64
PAIR = 128
PREFIX_ROWS = 16
VT_ROWS = 80
blocked = -1e30
norm_epsilon = 1e-05
f32, bf16 = jnp.float32, jnp.bfloat16
in_vmem = pl.BlockSpec(memory_space=pltpu.VMEM)
in_smem = pl.BlockSpec(memory_space=pltpu.SMEM)
in_place = pl.BlockSpec(memory_space=pl.ANY)


def params(mib):
    return pltpu.CompilerParams(vmem_limit_bytes=mib << 20)


def cost(flops, moved, special=0):
    return pl.CostEstimate(flops=int(flops), bytes_accessed=int(moved), transcendentals=int(special))


def like(shape, dtype=bf16):
    return jax.ShapeDtypeStruct(shape, dtype)


def dot(a, b, ca, cb):
    return lax.dot_general(a, b, (((ca,), (cb,)), ((), ())), preferred_element_type=f32)


def lane(shape):
    return lax.broadcasted_iota(jnp.int32, shape, len(shape) - 1)


def head_half(h, shape):
    l = lane(shape)
    return (l < HEAD) if h == 0 else (l >= HEAD)


def split3(v):
    hi = v.astype(bf16)
    r = v - hi.astype(f32)
    mid = r.astype(bf16)
    lo = (r - mid.astype(f32)).astype(bf16)
    return hi.astype(f32), mid.astype(f32), lo.astype(f32)


def at(index, size):
    return pl.ds(pl.multiple_of(index * size, size), size)


def normalize(hidden):
    centered = hidden - jnp.mean(hidden, axis=-1, keepdims=True)
    scale = lax.rsqrt(jnp.mean(centered * centered, axis=-1, keepdims=True) + norm_epsilon)
    return centered * scale, scale


def normalize_back(normed, scale, grad):
    return scale * (
        grad
        - jnp.mean(grad, axis=-1, keepdims=True)
        - normed * jnp.mean(grad * normed, axis=-1, keepdims=True)
    )


def cut_attend_body(seq, pairs, place, attend_ref, *outs):
    width = attend_ref.shape[1] // 3
    for p in range(pairs):
        for t in range(3):
            column = t * width + (place[0] * pairs + p) * PAIR
            outs[p][:, t * PAIR : (t + 1) * PAIR] = attend_ref[
                :, pl.ds(pl.multiple_of(column, PAIR), PAIR)
            ]


def cut_attend(seq, pairs, place, attend_weight):
    rows = attend_weight.shape[0]
    return pl.pallas_call(
        functools.partial(cut_attend_body, seq, pairs),
        in_specs=[in_smem, in_vmem],
        out_specs=[in_vmem] * pairs,
        out_shape=[like((rows, 3 * PAIR))] * pairs,
        cost_estimate=cost(0, attend_weight.size * 3),
        compiler_params=params(4),
        name="cut_attend",
    )(place, attend_weight)


def cut_rest_body(seq, place, output_ref, expand_ref, shrink_ref, first_ref, second_ref, down_ref):
    s = place[0]
    wide = output_ref.shape[1] // seq
    part = shrink_ref.shape[0] // seq
    half = second_ref.shape[1] // part
    first_ref[:, :wide] = output_ref[:, at(s, wide)]
    for d in range(2 * half):
        piece = expand_ref[:, at(d * seq + s, part)]
        if d < half:
            first_ref[:, wide + d * part : wide + (d + 1) * part] = piece
        else:
            second_ref[:, (d - half) * part : (d - half + 1) * part] = piece
    for x in range(seq // 2):
        down_ref[x * part : (x + 1) * part, :] = shrink_ref[at(2 * x + lax.rem(s, 2), part), :]


def cut_rest(seq, place, output_weight, expand_weight, shrink_weight):
    rows, width = output_weight.shape
    hidden = expand_weight.shape[1]
    part = shrink_weight.shape[0] // seq
    wide, half = width // seq, hidden // seq // 2
    if part % PAIR:
        s = lax.axis_index("seq")
        up = lax.dynamic_index_in_dim(
            expand_weight.reshape(rows, -1, seq, part), s, 2, keepdims=False
        ).reshape(rows, 2 * half)
        out = lax.dynamic_slice_in_dim(output_weight, s * wide, wide, 1)
        down = lax.dynamic_index_in_dim(
            shrink_weight.reshape(seq // 2, 2, part, width), lax.rem(s, 2), 1, keepdims=False
        ).reshape(seq // 2 * part, width)
        return jnp.concatenate([out, up[:, :half]], axis=1), up[:, half:], down
    return pl.pallas_call(
        functools.partial(cut_rest_body, seq),
        in_specs=[in_smem, in_vmem, in_vmem, in_vmem],
        out_specs=[in_vmem] * 3,
        out_shape=[
            like((rows, wide + half)),
            like((rows, half)),
            like((shrink_weight.shape[0] // 2, width)),
        ],
        cost_estimate=cost(0, expand_weight.size * 6),
        compiler_params=params(8),
        name="cut_rest",
    )(place, output_weight, expand_weight, shrink_weight)


def forward_body(seq, dp, bq, bk, place, *refs):
    normed, (line, other, pk_ref, pv_ref, mq_ref, mk_ref, pm_ref) = refs[:seq], refs[seq : seq + 7]
    qkv_ref, stat_ref, weight_ref = refs[seq + 7 : seq + 10]
    groups = seq // 2
    outs, refs = refs[seq + 10 : seq + 10 + groups], refs[seq + 10 + groups :]
    ka, vt, pka, pvt, qh, o_all = refs
    s = place[0]
    s_len = qkv_ref.shape[0]
    rows = s_len // seq
    count = line.shape[0]
    shard = line.shape[1]
    order = dp_masks(dp, False)[1]
    for j in range(count):
        weight_ref[at(lax.bitwise_xor(place[1], order[j]), shard), :] = line[j]
        weight_ref[at(lax.bitwise_xor(place[1], order[count + j]), shard), :] = other[j]
    for r in range(seq):
        got = jnp.dot(normed[r][...], weight_ref[...], preferred_element_type=f32)
        qkv_ref[at(lax.bitwise_xor(s, r), rows), :] = got.astype(bf16)
    ka[:, :PAIR] = qkv_ref[:, PAIR : 2 * PAIR]
    ka[:, PAIR:] = mk_ref[...]
    pka[:, :PAIR] = pk_ref[...]
    pka[:, PAIR:] = pm_ref[...]
    first_row = lax.broadcasted_iota(jnp.int32, (VT_ROWS - HEAD, s_len), 0) == 0
    ones = jnp.where(first_row, 1.0, 0.0).astype(bf16)
    vtr = qkv_ref[:, 2 * PAIR :].T
    pvr = pv_ref[...].T
    for h in (0, 1):
        vt[h, :HEAD, :] = vtr[h * HEAD : (h + 1) * HEAD, :]
        vt[h, HEAD:, :] = ones
        pvt[h, :HEAD, :] = pvr[h * HEAD : (h + 1) * HEAD, :]
        pvt[h, HEAD:, :] = ones[:, :PREFIX_ROWS]

    def block(start, state, first, causal):
        out = []
        start = pl.multiple_of(start, bk)
        scores = [dot(ka[pl.ds(start, bk), :], qh[h, first:, :], 1, 1) for h in (0, 1)]
        for h in (0, 1):
            m, acc = state[2 * h], state[2 * h + 1]
            x = scores[h]
            if causal:
                ok = lax.broadcasted_iota(jnp.int32, x.shape, 0) <= lane(x.shape)
                x = jnp.where(ok, x, blocked)
            if first:
                keep_m, keep_acc = m[:, :first], acc[:, :first]
                m, acc = m[:, first:], acc[:, first:]
            new = jnp.maximum(m, jnp.max(x, axis=0, keepdims=True))
            p = jnp.exp(x - new)
            acc = acc * jnp.exp(m - new) + dot(vt[h, :, pl.ds(start, bk)], p.astype(bf16), 1, 0)
            if first:
                new = jnp.concatenate([keep_m, new], axis=1)
                acc = jnp.concatenate([keep_acc, acc], axis=1)
            out += [new, acc]
        return tuple(out)

    for i in range(s_len // bq):
        span = slice(i * bq, (i + 1) * bq)
        q = qkv_ref[span, :PAIR] * bf16(0.125)
        for h in (0, 1):
            qh[h, :, :PAIR] = jnp.where(head_half(h, q.shape), q, bf16(0))
            qh[h, :, PAIR:] = mq_ref[span, :]
        state = []
        for h in (0, 1):
            x = dot(pka[...], qh[h], 1, 1)
            m = jnp.max(x, axis=0, keepdims=True)
            state += [m, dot(pvt[h], jnp.exp(x - m).astype(bf16), 1, 0)]
        state = tuple(state)
        if i:
            state = lax.fori_loop(
                0, i * (bq // bk), lambda j, st: block(j * bk, st, 0, False), state
            )
        for j in range(bq // bk):
            state = block(i * bq + j * bk, state, j * bk, True)
        tops, parts = [], []
        for h in (0, 1):
            m, acc = state[2 * h], state[2 * h + 1]
            total = acc[HEAD : HEAD + 1]
            tops.append(acc[:HEAD] / total)
            parts += split3(-(m + jnp.log(total)))
        o_all[span, :] = jnp.concatenate(tops, axis=0).T.astype(bf16)
        pad = jnp.zeros((PAIR - 4 - len(parts), bq), f32)
        logs = jnp.concatenate([jnp.zeros((4, bq), f32)] + parts + [pad], axis=0).T
        stat_ref[span, :] = (logs + mq_ref[span, :].astype(f32)).astype(bf16)
    for r in range(seq):
        outs[r // 2][r % 2 * rows : (r % 2 + 1) * rows, :] = o_all[at(lax.bitwise_xor(s, r), rows), :]


def attend_forward(place, normed, line, other, pk, pv, mq, mk, pm):
    seq = len(normed)
    rows, width = normed[0].shape
    s_len = rows * seq
    bq, bk = min(2048, s_len), min(512, s_len)
    return pl.pallas_call(
        functools.partial(forward_body, seq, 2 * line.shape[0], bq, bk),
        in_specs=[in_smem] + [in_vmem] * (seq + 7),
        out_specs=[in_vmem] * (3 + seq // 2),
        out_shape=[like((s_len, 3 * PAIR)), like((s_len, PAIR)), like((width, 3 * PAIR))]
        + [like((2 * rows, PAIR))] * (seq // 2),
        scratch_shapes=[
            pltpu.VMEM((s_len, 2 * PAIR), bf16),
            pltpu.VMEM((2, VT_ROWS, s_len), bf16),
            pltpu.VMEM((PREFIX_ROWS, 2 * PAIR), bf16),
            pltpu.VMEM((2, VT_ROWS, PREFIX_ROWS), bf16),
            pltpu.VMEM((2, bq, 2 * PAIR), bf16),
            pltpu.VMEM((s_len, PAIR), bf16),
        ],
        compiler_params=params(40),
        cost_estimate=cost(
            2 * s_len * s_len * 512 + 2 * s_len * width * 3 * PAIR, s_len * width * 3, s_len * s_len
        ),
        name="attend_forward",
    )(place, *normed, line, other, pk, pv, mq, mk, pm)


def backward_body(seq, bq, bk, place, *refs):
    (qkv_ref, pk_ref, pv_ref, stat_ref, mk_ref, pm_ref), refs = refs[:6], refs[6:]
    groups = seq // 2
    o_parts, do_parts, refs = refs[:groups], refs[groups : groups + seq], refs[groups + seq :]
    grad_refs, (dp_ref,), refs = refs[:seq], refs[seq : seq + 1], refs[seq + 1 :]
    ka, va, kt, pka, pva, pkt, qh, dh, dk_acc, dv_acc, o_all, do_all, dq_all = refs
    s = place[0]
    s_len = qkv_ref.shape[0]
    rows = s_len // seq
    for r in range(seq):
        o_all[at(lax.bitwise_xor(s, r), rows), :] = o_parts[r // 2][
            r % 2 * rows : (r % 2 + 1) * rows, :
        ]
        do_all[at(lax.bitwise_xor(s, r), rows), :] = do_parts[r][...]
    ones = jnp.where(lane((s_len, PAIR)) < 3, 1.0, 0.0).astype(bf16)
    l = lane((s_len, PAIR))
    k = qkv_ref[:, PAIR : 2 * PAIR]
    for h in (0, 1):
        mine = (l >= 4 + 3 * h) & (l < 7 + 3 * h)
        ka[h, :, :PAIR] = k
        ka[h, :, PAIR:] = jnp.where(mine, bf16(1), mk_ref[...])
        pka[h, :, :PAIR] = pk_ref[...]
        pka[h, :, PAIR:] = jnp.where(mine[:PREFIX_ROWS], bf16(1), pm_ref[...])
    va[:, :PAIR] = qkv_ref[:, 2 * PAIR :]
    va[:, PAIR:] = ones
    pva[:, :PAIR] = pv_ref[...]
    pva[:, PAIR:] = ones[:PREFIX_ROWS]
    kt[...] = k.T
    pkt[...] = pk_ref[...].T
    dk_acc[...] = jnp.zeros_like(dk_acc)
    dv_acc[...] = jnp.zeros_like(dv_acc)

    def block(start, state, first, causal):
        start = pl.multiple_of(start, bk)
        here = pl.ds(start, bk)
        out = []
        dv = dk = None
        scores = [dot(ka[h, here, :], qh[h, first:, :], 1, 1) for h in (0, 1)]
        dps = [dot(va[here, :], dh[h, first:, :], 1, 1) for h in (0, 1)]
        for h in (0, 1):
            p = jnp.exp(scores[h])
            if causal:
                ok = lax.broadcasted_iota(jnp.int32, p.shape, 0) <= lane(p.shape)
                p = jnp.where(ok, p, 0.0)
            ds = (p * dps[h]).astype(bf16)
            a = dot(p.astype(bf16), dh[h, first:, :PAIR], 1, 0)
            b = dot(ds, qh[h, first:, :PAIR], 1, 0)
            dv = a if dv is None else dv + a
            dk = b if dk is None else dk + b
            c = dot(kt[h * HEAD : (h + 1) * HEAD, here], ds, 1, 0)
            if first:
                out.append(jnp.concatenate([state[h][:, :first], state[h][:, first:] + c], axis=1))
            else:
                out.append(state[h] + c)
        dv_acc[here, :] += dv
        dk_acc[here, :] += dk
        return tuple(out)

    for i in range(s_len // bq):
        span = slice(i * bq, (i + 1) * bq)
        q = qkv_ref[span, :PAIR] * bf16(0.125)
        do = do_all[span, :]
        prod = do.astype(f32) * o_all[span, :].astype(f32)
        for h in (0, 1):
            half = head_half(h, q.shape)
            qh[h, :, :PAIR] = jnp.where(half, q, bf16(0))
            qh[h, :, PAIR:] = stat_ref[span, :]
            dh[h, :, :PAIR] = jnp.where(half, do, bf16(0))
            delta = -jnp.sum(jnp.where(half, prod, 0.0), axis=1, keepdims=True)
            hi, mid, lo = split3(delta)
            n = lane((bq, PAIR))
            dh[h, :, PAIR:] = jnp.where(
                n == 0, hi, jnp.where(n == 1, mid, jnp.where(n == 2, lo, 0.0))
            ).astype(bf16)
        state = []
        dpk = dpv = jnp.zeros((PREFIX_ROWS, PAIR), f32)
        for h in (0, 1):
            p = jnp.exp(dot(pka[h], qh[h], 1, 1))
            ds = (p * dot(pva[...], dh[h], 1, 1)).astype(bf16)
            dpv = dpv + dot(p.astype(bf16), dh[h, :, :PAIR], 1, 0)
            dpk = dpk + dot(ds, qh[h, :, :PAIR], 1, 0)
            state.append(dot(pkt[h * HEAD : (h + 1) * HEAD, :], ds, 1, 0))
        dp_ref[0] = dpk if i == 0 else dp_ref[0] + dpk
        dp_ref[1] = dpv if i == 0 else dp_ref[1] + dpv
        state = tuple(state)
        if i:
            state = lax.fori_loop(
                0, i * (bq // bk), lambda j, st: block(j * bk, st, 0, False), state
            )
        for j in range(bq // bk):
            state = block(i * bq + j * bk, state, j * bk, True)
        dq_all[span, :] = (jnp.concatenate(state, axis=0) * 0.125).T.astype(bf16)
    for r in range(seq):
        here = at(lax.bitwise_xor(s, r), rows)
        grad_refs[r][:, :PAIR] = dq_all[here, :]
        grad_refs[r][:, PAIR : 2 * PAIR] = dk_acc[here, :].astype(bf16)
        grad_refs[r][:, 2 * PAIR :] = dv_acc[here, :].astype(bf16)


def attend_backward(place, qkv, pk, pv, stat, mk, pm, o_parts, do_parts):
    seq = len(do_parts)
    s_len = qkv.shape[0]
    rows = s_len // seq
    bq, bk = min(2048, s_len), min(256, s_len)
    return pl.pallas_call(
        functools.partial(backward_body, seq, bq, bk),
        in_specs=[in_smem] + [in_vmem] * (6 + seq // 2 + seq),
        out_specs=[in_vmem] * (seq + 1),
        out_shape=[like((rows, 3 * PAIR))] * seq + [like((2, PREFIX_ROWS, PAIR), f32)],
        scratch_shapes=[
            pltpu.VMEM((2, s_len, 2 * PAIR), bf16),
            pltpu.VMEM((s_len, 2 * PAIR), bf16),
            pltpu.VMEM((PAIR, s_len), bf16),
            pltpu.VMEM((2, PREFIX_ROWS, 2 * PAIR), bf16),
            pltpu.VMEM((PREFIX_ROWS, 2 * PAIR), bf16),
            pltpu.VMEM((PAIR, PREFIX_ROWS), bf16),
            pltpu.VMEM((2, bq, 2 * PAIR), bf16),
            pltpu.VMEM((2, bq, 2 * PAIR), bf16),
            pltpu.VMEM((s_len, PAIR), f32),
            pltpu.VMEM((s_len, PAIR), f32),
            pltpu.VMEM((s_len, PAIR), bf16),
            pltpu.VMEM((s_len, PAIR), bf16),
            pltpu.VMEM((s_len, PAIR), bf16),
        ],
        compiler_params=params(44),
        cost_estimate=cost(5 * s_len * s_len * 512, s_len * PAIR * 24, s_len * s_len),
        name="attend_backward",
    )(place, qkv, pk, pv, stat, mk, pm, *o_parts, *do_parts)


def dp_masks(dp, near_first):
    masks = [1] + halvings(dp)[:-1] if near_first else halvings(dp)
    order = [0]
    for mask in masks:
        order += [i ^ mask for i in order]
    return masks, order


def middle_body(seq, pairs, dp, rows, place, *refs):
    groups = seq // 2
    tokens, cots, refs = refs[:2], refs[2:4], refs[4:]
    heads, refs = refs[: 2 * groups * pairs], refs[2 * groups * pairs :]
    firsts, seconds, refs = refs[: 2 * groups], refs[2 * groups : 4 * groups], refs[4 * groups :]
    across, (few, many), refs = refs[0], (refs[1:3], refs[3:5]), refs[5:]
    mid_ref, out_ref, out_give_ref, back_ref, back_give_ref, wo = refs[:6]
    up, down, merged, normed, active, grads, cot, sem_o, sem_u, sem_d = refs[6:]
    s, me = place[0], place[1]
    width = tokens[0].shape[1]
    shard = width // dp
    wide = width // seq
    half = seconds[0].shape[2]
    part = down.shape[1] // dp
    far_order = dp_masks(dp, False)[1]
    near_order = dp_masks(dp, True)[1]
    per_array = dp // 2

    copies_o, copies_u, copies_d = [], [], []

    def add(copies, sems, source, target):
        copies.append(pltpu.make_async_copy(source, target, sems.at[len(copies)]))

    for g in range(groups):
        owner = lax.bitwise_xor(s, 2 * g)
        for t in (0, 1):
            for j in range(per_array):
                d = lax.bitwise_xor(me, far_order[t * per_array + j])
                first, second = firsts[2 * g + t].at[j], seconds[2 * g + t].at[j]
                add(copies_o, sem_o, first.at[:, pl.ds(0, wide)], wo.at[owner, at(d, shard)])
                add(
                    copies_o,
                    sem_o,
                    across.at[2 * g + t, j],
                    wo.at[lax.bitwise_xor(owner, 1), at(d, shard)],
                )
                place_up = up.at[owner // 2, at(d, shard)]
                add(copies_u, sem_u, first.at[:, pl.ds(wide, half)], place_up.at[:, pl.ds(0, half)])
                add(copies_u, sem_u, second, place_up.at[:, pl.ds(half, half)])
    start = 0
    for arrays, order in ((few, near_order), (many, far_order)):
        size = arrays[0].shape[1]
        for t in (0, 1):
            for j in range(per_array):
                d = lax.bitwise_xor(me, order[t * per_array + j])
                done = 0
                while done < size:
                    x, row = (start + done) // part, (start + done) % part
                    take = min(part - row, size - done)
                    to = pl.multiple_of(d * part + row, min(take, part))
                    add(
                        copies_d,
                        sem_d,
                        arrays[t].at[j, pl.ds(done, take)],
                        down.at[x, pl.ds(to, take)],
                    )
                    done += take
        start += size
    for copy in copies_o + copies_u + copies_d:
        copy.start()
    for p in range(pairs):
        for g in range(groups):
            for flip in (0, 1):
                source = heads[(p * groups + g) * 2 + flip]
                owner = lax.bitwise_xor(s, 2 * g + flip)
                column = pl.ds(pl.multiple_of(owner * (pairs * PAIR) + p * PAIR, PAIR), PAIR)
                for k in (0, 1):
                    here = k ^ flip
                    merged[k * rows : (k + 1) * rows, column] = source[
                        here * rows : (here + 1) * rows, :
                    ]
    for k in (0, 1):
        cot[k * rows : (k + 1) * rows, :] = cots[k][...]
    for copy in copies_o:
        copy.wait()
    both = jnp.concatenate([dot(merged[...], wo[o], 1, 0) for o in range(seq)], axis=1)
    for k in (0, 1):
        acc = tokens[k][...].astype(f32) + both[k * rows : (k + 1) * rows]
        if k == 0:
            mid_ref[...] = acc
        normed[k * rows : (k + 1) * rows, :] = normalize(acc)[0].astype(bf16)
    for copy in copies_u + copies_d:
        copy.wait()
    chunk = min(512, 2 * half)
    inner = 2 * half // chunk

    def step(h, carry):
        block, piece = h // inner, lax.rem(h, inner)
        w_up = up[block, :, at(piece, chunk)]
        w_down = down[block, at(piece, chunk), :]
        u = jnp.dot(normed[...], w_up, preferred_element_type=f32)
        gelu_grad = dot(cot[...], w_down, 1, 1)
        square = u * u
        t = jnp.tanh(0.7978845608028654 * u * (1.0 + 0.044715 * square))
        side = 0.5 * (1.0 + t)
        slope = side + (0.5 * 0.7978845608028654) * u * (1.0 - t * t) * (
            1.0 + 3 * 0.044715 * square
        )
        active[block, :, at(piece, chunk)] = (u * side).astype(bf16)
        grads[block, :, at(piece, chunk)] = (gelu_grad * slope).astype(bf16)
        return carry

    lax.fori_loop(0, groups * inner, step, 0)
    first, last = slice(0, rows), slice(rows, 2 * rows)
    for give_ref, own_ref, left, right, side in (
        (back_give_ref, back_ref, grads, up, 1),
        (out_give_ref, out_ref, active, down, 0),
    ):
        give_ref[...] = sum(
            dot(left[g, last, :], right[g], 1, side) for g in range(groups)
        ).astype(bf16)
        total = sum(dot(left[g, first, :], right[g], 1, side) for g in range(groups))
        own_ref[...] = total if side else mid_ref[...] + total


def middle(seq, dp, pairs, place, tokens, cots, heads, firsts, seconds, across, few, many):
    rows, width = tokens[0].shape
    groups = seq // 2
    half = seconds[0].shape[2]
    part = (few[0].shape[1] + many[0].shape[1]) // groups
    spans = 0
    start = 0
    for arrays in (few, many):
        size = arrays[0].shape[1]
        spans += (start + size - 1) // part - start // part + 1
        start += size
    hidden = groups * 2 * half
    return pl.pallas_call(
        functools.partial(middle_body, seq, pairs, dp, rows),
        in_specs=[in_smem]
        + [in_vmem] * (4 + len(heads))
        + [in_place] * (len(firsts) + len(seconds) + 5),
        out_specs=[in_vmem] * 6,
        out_shape=[
            like((rows, width), f32),
            like((rows, width), f32),
            like((rows, width)),
            like((rows, width), f32),
            like((rows, width)),
            like((seq, width, width // seq)),
        ],
        scratch_shapes=[
            pltpu.VMEM((groups, width, 2 * half), bf16),
            pltpu.VMEM((groups, dp * part, width), bf16),
            pltpu.VMEM((2 * rows, width), bf16),
            pltpu.VMEM((2 * rows, width), bf16),
            pltpu.VMEM((groups, 2 * rows, 2 * half), bf16),
            pltpu.VMEM((groups, 2 * rows, 2 * half), bf16),
            pltpu.VMEM((2 * rows, width), bf16),
            pltpu.SemaphoreType.DMA((seq * dp,)),
            pltpu.SemaphoreType.DMA((seq * dp,)),
            pltpu.SemaphoreType.DMA((spans * dp,)),
        ],
        compiler_params=params(58),
        cost_estimate=cost(
            16 * rows * width * hidden + 4 * rows * width * width,
            4 * width * hidden + 20 * rows * width,
            2 * rows * hidden,
        ),
        name="middle",
    )(place, *tokens, *cots, *heads, *firsts, *seconds, across, *few, *many)


def turn_body(seq, pairs, place, mid_ref, cot_ref, own_ref, got_ref, wo, *refs):
    mid_grad_ref, grads, (merged,) = refs[0], refs[1:-1], refs[-1:]
    s = place[0]
    wide = wo.shape[2]
    normed, scale = normalize(mid_ref[...])
    grad = own_ref[...] + got_ref[...].astype(f32)
    mid_grad = cot_ref[...].astype(f32) + normalize_back(normed, scale, grad)
    mid_grad_ref[...] = mid_grad
    rounded = mid_grad.astype(bf16)
    grad = sum(dot(rounded[:, o * wide : (o + 1) * wide], wo[o], 1, 1) for o in range(seq))
    merged[...] = grad.astype(bf16)
    for r in range(seq):
        for p in range(pairs):
            column = lax.bitwise_xor(s, r) * (pairs * PAIR) + p * PAIR
            grads[p * seq + r][...] = merged[:, pl.ds(pl.multiple_of(column, PAIR), PAIR)]


def turn(seq, pairs, place, mid, cot, own, got, wo):
    rows, width = mid.shape
    return pl.pallas_call(
        functools.partial(turn_body, seq, pairs),
        in_specs=[in_smem] + [in_vmem] * 5,
        out_specs=[in_vmem] * (1 + seq * pairs),
        out_shape=[like((rows, width), f32)] + [like((rows, PAIR))] * (seq * pairs),
        scratch_shapes=[pltpu.VMEM((rows, width), bf16)],
        compiler_params=params(24),
        cost_estimate=cost(2 * rows * width * width, 16 * rows * width),
        name="turn",
    )(place, mid, cot, own, got, wo)


def finish_body(tokens_ref, mid_grad_ref, own_ref, got_ref, out_ref):
    normed, scale = normalize(tokens_ref[...].astype(f32))
    grad = own_ref[...] + got_ref[...].astype(f32)
    out_ref[...] = (mid_grad_ref[...] + normalize_back(normed, scale, grad)).astype(bf16)


def finish(tokens, mid_grad, own, got):
    return pl.pallas_call(
        finish_body,
        in_specs=[in_vmem] * 4,
        out_specs=in_vmem,
        out_shape=like(tokens.shape),
        compiler_params=params(24),
        cost_estimate=cost(tokens.size * 20, tokens.size * 14),
        name="finish",
    )(tokens, mid_grad, own, got)


def masks(lengths, s_len):
    e0 = lengths[0]
    e1 = e0 + lengths[1]
    e2 = e1 + lengths[2]
    pos = jnp.arange(s_len, dtype=jnp.int32)
    doc = sum((pos >= e).astype(jnp.int32) for e in (e0, e1, e2))
    l = lax.broadcasted_iota(jnp.int32, (s_len, PAIR), 1)
    same = l == doc[:, None]
    mq = jnp.where((l < 4) & ~same, blocked, 0.0).astype(bf16)
    mk = jnp.where((l < 4) & same, 1.0, 0.0).astype(bf16)
    r = lax.broadcasted_iota(jnp.int32, (PREFIX_ROWS, PAIR), 0)
    lp = lax.broadcasted_iota(jnp.int32, (PREFIX_ROWS, PAIR), 1)
    pm = jnp.where((r >= PREFIX) & (lp == 3), 1.0, 0.0).astype(bf16)
    return mq, mk, pm


def parts_of(v):
    return [p.astype(bf16) for p in split3(v)]


def precise(a, b, side):
    high, mid, low = parts_of(a)
    few = a.shape[0]
    total = None
    for stack, part in zip(([high, mid, low], [high, mid], [high]), parts_of(b)):
        got = dot(jnp.concatenate(stack, axis=0), part, 1, side)
        for k in reversed(range(len(stack))):
            piece = got[k * few : (k + 1) * few]
            total = piece if total is None else total + piece
    return total


def full(a, b):
    return jnp.dot(a, b, precision=lax.Precision.HIGHEST, preferred_element_type=f32)


def precise_outer(a, b):
    high, mid, low = parts_of(a)
    high_b, mid_b, low_b = parts_of(b)
    left = jnp.concatenate([low, mid, high, mid, high, high], axis=0)
    right = jnp.concatenate([high_b, mid_b, low_b, high_b, mid_b, high_b], axis=0)
    return dot(left.astype(f32).T.astype(bf16), right, 1, 0)


def norm_body(rows_ref, out_ref):
    out_ref[...] = normalize(rows_ref[...].astype(f32))[0].astype(bf16)


def norm(rows):
    return pl.pallas_call(
        norm_body,
        in_specs=[in_vmem],
        out_specs=in_vmem,
        out_shape=like(rows.shape),
        compiler_params=params(8),
        cost_estimate=cost(rows.size * 8, rows.size * 4),
        name="norm",
    )(rows)


def reparam_body(seq, pairs, place, embed, inner, inner_bias, outer, outer_bias, kv, hidden, *parts):
    s = place[0]
    half = outer.shape[1] // 2
    hidden[...] = jnp.tanh(full(embed[...], inner[...]) + inner_bias[...])
    both = full(hidden[...], outer[...]) + outer_bias[...]
    kv[...] = both[:PREFIX]
    *parts, held = parts
    row = lax.broadcasted_iota(jnp.int32, both.shape, 0)
    held[...] = jnp.where(row < PREFIX, both, 0.0)
    for t in (0, 1):
        for p in range(pairs):
            column = pl.multiple_of(t * half + (s * pairs + p) * PAIR, PAIR)
            parts[t * pairs + p][...] = held[:, pl.ds(column, PAIR)].astype(bf16)


def reparam(seq, pairs, place, embed, inner, inner_bias, outer, outer_bias):
    width = outer.shape[1]
    return pl.pallas_call(
        functools.partial(reparam_body, seq, pairs),
        in_specs=[in_smem] + [in_vmem] * 5,
        out_specs=[in_vmem] * (2 + 2 * pairs),
        out_shape=[like((PREFIX, width), f32), like((PREFIX_ROWS, inner.shape[1]), f32)]
        + [like((PREFIX_ROWS, PAIR))] * (2 * pairs),
        scratch_shapes=[pltpu.VMEM((PREFIX_ROWS, width), f32)],
        compiler_params=params(20),
        cost_estimate=cost(12 * PREFIX_ROWS * (inner.size + outer.size), 4 * (inner.size + outer.size)),
        name="reparam",
    )(place, embed, inner, inner_bias[None], outer, outer_bias[None])


def reparam_back_body(seq, pairs, place, embed, inner, outer, hidden, *refs):
    got, (d_embed, d_inner, d_inner_bias, d_outer, d_outer_bias, grad) = refs[:2], refs[2:]
    s = place[0]
    half = outer.shape[1] // 2
    for r in range(seq):
        for t in (0, 1):
            for p in range(pairs):
                column = t * half + (lax.bitwise_xor(s, r) * pairs + p) * PAIR
                grad[:, pl.ds(pl.multiple_of(column, PAIR), PAIR)] = got[r % 2][r // 2, p, t]
    d_outer_bias[...] = jnp.sum(grad[...], axis=0, keepdims=True)
    d_outer[...] = precise_outer(hidden[...], grad[...])
    back = precise(grad[...], outer[...], 1) * (1.0 - hidden[...] * hidden[...])
    d_inner_bias[...] = jnp.sum(back, axis=0, keepdims=True)
    d_inner[...] = precise_outer(embed[...], back)
    d_embed[...] = precise(back, inner[...], 1)[:PREFIX]


def reparam_back(pairs, place, embed, inner, outer, hidden, got):
    seq = 2 * got[0].shape[0]
    wide, (deep, width) = inner.shape[0], outer.shape
    outs = pl.pallas_call(
        functools.partial(reparam_back_body, seq, pairs),
        in_specs=[in_smem] + [in_vmem] * 6,
        out_specs=[in_vmem] * 5,
        out_shape=[
            like((PREFIX, wide), f32),
            like((wide, deep), f32),
            like((1, deep), f32),
            like((deep, width), f32),
            like((1, width), f32),
        ],
        scratch_shapes=[pltpu.VMEM((PREFIX_ROWS, width), f32)],
        compiler_params=params(28),
        cost_estimate=cost(24 * PREFIX_ROWS * (inner.size + outer.size), 8 * (inner.size + outer.size)),
        name="reparam_back",
    )(place, embed, inner, outer, hidden, *got)
    return outs[0], outs[1], outs[2][0], outs[3], outs[4][0]


def product_body(pairs, adds, out_dtype, *refs):
    weights, refs = refs[:pairs], refs[pairs:]
    count = len(refs) // (pairs + adds + 1)
    rows, refs = refs[: count * pairs], refs[count * pairs :]
    extra, outs = refs[: count * adds], refs[count * adds :]
    for i in range(count):
        total = sum(dot(rows[i * pairs + p][...], weights[p][...], 1, 1) for p in range(pairs))
        if adds:
            total = total + extra[i][...].astype(f32)
        outs[i][...] = total.astype(out_dtype)


def product(weights, rows, extra, out_dtype):
    pairs = len(weights)
    height, width = rows[0][0].shape[0], weights[0].shape[0]
    flat = [w for entry in rows for w in entry]
    return pl.pallas_call(
        functools.partial(product_body, pairs, int(bool(extra)), out_dtype),
        in_specs=[in_vmem] * (pairs + len(flat) + len(extra)),
        out_specs=[in_vmem] * len(rows),
        out_shape=[like((height, width), out_dtype)] * len(rows),
        compiler_params=params(24),
        cost_estimate=cost(
            2 * len(flat) * height * width * flat[0].shape[1], 4 * len(rows) * height * width
        ),
        name="product",
    )(*weights, *flat, *extra)


def halvings(count):
    steps = []
    while count > 1:
        count //= 2
        steps.append(count)
    return steps


def swap(value, axis, size, mask):
    return lax.ppermute(value, axis, [(i, i ^ mask) for i in range(size)])


def after(value, *events):
    return lax.optimization_barrier((value, *events))[0] if events else value


def spread_seq(value, seq):
    held = {0: value}
    for mask in halvings(seq):
        for r in list(held):
            held[r ^ mask] = swap(held[r], "seq", seq, mask)
    return [held[r] for r in range(seq)]


def exchange_seq(pieces, seq):
    return [pieces[0]] + [swap(pieces[r], "seq", seq, r) for r in range(1, seq)]


def shards(seq, dp, tokens, lengths, attend_weight, output_weight, expand_weight, shrink_weight,
           prefix_embed, inner_weight, inner_bias, outer_weight, outer_bias, cotangent):
    s = lax.axis_index("seq")
    rows, width = tokens.shape[1:]
    s_len = rows * seq
    pairs = width // seq // PAIR
    groups = seq // 2
    token_rows, cot_rows = tokens[0], cotangent[0]
    place = jnp.stack([s, lax.axis_index("dp")]).astype(jnp.int32)
    near_mask, far_masks = dp_masks(dp, False)[0][-1], dp_masks(dp, False)[0][:-1]

    def over(value, mask, *events):
        return swap(after(value, *events), "dp", dp, mask)

    def other_core(value, *events):
        return swap(after(value, *events), "seq", seq, 1)

    def line(piece, begin=(), later=()):
        held, arrived = piece, []
        for mask in far_masks:
            arrived.append(over(held, mask, *(later if arrived else begin)))
            held = jnp.concatenate([held, arrived[-1]])
        return held, arrived

    def spread(value, *events):
        held = {0: after(value, *events)}
        for mask in halvings(seq)[:-1]:
            for g in list(held):
                held[g ^ mask // 2] = swap(held[g], "seq", seq, mask)
        return [held[g] for g in range(groups)]

    token_far = spread(token_rows)
    token_pair = (token_rows, other_core(token_rows))
    cot_pair = (cot_rows, other_core(cot_rows))
    attend_lines = [
        line(w[None], later=(token_pair[1], cot_pair[1]))
        for w in cut_attend(seq, pairs, place, attend_weight)
    ]
    first, second, down = cut_rest(seq, place, output_weight, expand_weight, shrink_weight)
    quarter = down.shape[0] // 4
    few = over(down[None, :quarter], near_mask, attend_lines[0][1][0])
    few = jnp.concatenate([down[None, :quarter], few])
    attend_pairs = [(w, over(w, near_mask)) for w, _ in attend_lines]
    normed_rows = [norm(w) for w in token_pair]
    line_a, steps_a = line(
        first[None],
        (few, *[steps[-1] for _, steps in attend_lines]),
        (attend_pairs[0][1],),
    )
    for w in token_far[1:]:
        normed_rows += [norm(w), norm(other_core(w))]
    line_b, steps_b = line(second[None], (steps_a[0], attend_pairs[0][1]), (attend_pairs[-1][1],))

    embed = after(prefix_embed, attend_lines[-1][1][-1])
    embed = jnp.pad(embed, ((0, PREFIX_ROWS - PREFIX), (0, 0)))
    prefix_kv, prefix_hidden, *prefix_parts = reparam(
        seq, pairs, place, embed, inner_weight, inner_bias, outer_weight, outer_bias
    )
    prefix_pairs = [(prefix_parts[p], prefix_parts[pairs + p]) for p in range(pairs)]
    mask_q, mask_k, mask_p = masks(lengths[0], s_len)
    saved, heads = [], []

    def attend(p, *events):
        qkv, stat, weight, *outs = attend_forward(
            after(place, *events), normed_rows, *attend_pairs[p], *prefix_pairs[p],
            mask_q, mask_k, mask_p,
        )
        saved.append((qkv, stat, weight, outs))
        for g in range(groups):
            got = outs[0] if g == 0 else swap(outs[g], "seq", seq, 2 * g)
            heads.extend((got, other_core(got)))

    attend(0, attend_pairs[-1][1], steps_a[-1], steps_b[0])
    other_a = over(line_a, near_mask, attend_pairs[-1][1])
    near_a = spread(line_a, normed_rows[-1])
    many = over(down[None, quarter:], far_masks[0], steps_b[0])
    many = jnp.concatenate([down[None, quarter:], many])
    begun = saved[0][1]
    other_b = over(line_b, near_mask, begun, other_a)
    far_a = spread(other_a, begun, *near_a)
    for mask in far_masks[1:]:
        many = jnp.concatenate([many, over(many, mask, begun, steps_b[-1])])
    for p in range(1, pairs):
        attend(p, other_a, *near_a, steps_b[-1])
    ended = saved[-1][1]
    many = (many, over(many, near_mask, ended, other_b, *far_a, *heads[: 2 * groups]))
    near_b = spread(line_b, ended, *far_a)
    far_b = spread(other_b, ended, *far_a)
    for mask in far_masks[:-1]:
        few = jnp.concatenate([few, over(few, mask, ended)])
    few = (few, over(few, far_masks[-1], *heads, *near_b))
    ups = [
        [w for g in range(groups) for w in (a[g], b[g])]
        for a, b in ((near_a, far_a), (near_b, far_b))
    ]
    wide = width // seq
    across = other_core(jnp.stack([w[..., :wide] for w in ups[0]]))
    mid, out_own, out_give, back_own, back_give, wo = middle(
        seq, dp, pairs, place, token_pair, cot_pair, heads, *ups, across, few, many
    )
    mid_grad, *out_grads = turn(
        seq, pairs, place, mid, cot_rows, back_own, other_core(back_give), wo
    )
    outputs = (out_own + other_core(out_give).astype(f32)).astype(bf16)
    grads, prefix_terms = [], []
    for p in range(pairs):
        qkv, stat, weight, outs = saved[p]
        got = exchange_seq(out_grads[p * seq : (p + 1) * seq], seq)
        *parts, prefix_part = attend_backward(
            place, qkv, *prefix_pairs[p], stat, mask_k, mask_p, outs, got
        )
        grads.append(parts)
        prefix_terms.append(prefix_part)

    prefix_sum = jnp.stack(spread(jnp.stack(prefix_terms)))

    weights = [entry[2] for entry in saved]
    block = lambda r: [grads[p][r] for p in range(pairs)]
    sent = product(weights, [block(r) for r in range(1, seq, 2)], [], bf16)
    got = [other_core(v, prefix_sum) for v in sent]
    evens = product(weights, [block(r) for r in range(2, seq, 2)], got[1:], bf16)
    (own,) = product(weights, [block(0)], got[:1], f32)
    left = dict(zip(range(2, seq, 2), evens))
    for mask in reversed(halvings(seq)[:-1]):
        keep = {}
        for r in [0, *left]:
            if r & mask:
                continue
            arrived = swap(left[r ^ mask], "seq", seq, mask)
            if r:
                keep[r] = left[r] + arrived
            elif len(left) > 1:
                own = own + arrived.astype(f32)
        left = keep
    input_grad = finish(token_rows, mid_grad, own, arrived)

    prefix_sum = after(prefix_sum, *evens)
    reach = [0]
    for mask in far_masks:
        reach += [mask ^ other for other in reach]
    terms = [prefix_sum] + [swap(prefix_sum, "dp", dp, mask) for mask in reach[1:]]
    while len(terms) > 1:
        half = len(terms) // 2
        terms = [terms[i] + terms[i + half] for i in range(half)]
    prefix_sum = terms[0] + swap(terms[0], "dp", dp, near_mask)
    prefix_all = (prefix_sum, other_core(prefix_sum))
    back = reparam_back(
        pairs, place, embed, inner_weight, outer_weight, prefix_hidden, prefix_all
    )
    return (outputs[None], input_grad[None], *back, prefix_kv)


def solution(mesh):
    placed = (
        P("dp", "seq", None),
        P("dp", None),
        P("dp", None),
        P("dp", None),
        P("dp", None),
        P("dp", None),
        P(),
        P(),
        P(),
        P(),
        P(),
        P("dp", "seq", None),
    )
    return jax.shard_map(
        functools.partial(shards, mesh.shape["seq"], mesh.shape["dp"]),
        mesh=mesh,
        in_specs=placed,
        out_specs=(P("dp", "seq", None), P("dp", "seq", None), P(), P(), P(), P(), P(), P()),
        check_vma=False,
    )
```

```python
import functools

import jax
import jax.numpy as jnp
from jax import lax
from jax.experimental import pallas as pl
from jax.experimental.pallas import tpu as pltpu
from jax.sharding import PartitionSpec as P

PREFIX = 10
HEAD = 64
PAIR = 128
PREFIX_ROWS = 16
VT_ROWS = 80
blocked = -1e30
norm_epsilon = 1e-05
f32, bf16 = jnp.float32, jnp.bfloat16
in_vmem = pl.BlockSpec(memory_space=pltpu.VMEM)
in_smem = pl.BlockSpec(memory_space=pltpu.SMEM)
in_place = pl.BlockSpec(memory_space=pl.ANY)


def params(mib):
    return pltpu.CompilerParams(vmem_limit_bytes=mib << 20)


def cost(flops, moved, special=0):
    return pl.CostEstimate(flops=int(flops), bytes_accessed=int(moved), transcendentals=int(special))


def like(shape, dtype=bf16):
    return jax.ShapeDtypeStruct(shape, dtype)


def dot(a, b, ca, cb):
    return lax.dot_general(a, b, (((ca,), (cb,)), ((), ())), preferred_element_type=f32)


def lane(shape):
    return lax.broadcasted_iota(jnp.int32, shape, len(shape) - 1)


def head_half(h, shape):
    l = lane(shape)
    return (l < HEAD) if h == 0 else (l >= HEAD)


def split3(v):
    hi = v.astype(bf16)
    r = v - hi.astype(f32)
    mid = r.astype(bf16)
    lo = (r - mid.astype(f32)).astype(bf16)
    return hi.astype(f32), mid.astype(f32), lo.astype(f32)


def at(index, size):
    return pl.ds(pl.multiple_of(index * size, size), size)


def normalize(hidden):
    centered = hidden - jnp.mean(hidden, axis=-1, keepdims=True)
    scale = lax.rsqrt(jnp.mean(centered * centered, axis=-1, keepdims=True) + norm_epsilon)
    return centered * scale, scale


def normalize_back(normed, scale, grad):
    return scale * (
        grad
        - jnp.mean(grad, axis=-1, keepdims=True)
        - normed * jnp.mean(grad * normed, axis=-1, keepdims=True)
    )


def cut_attend_body(seq, pairs, place, attend_ref, *outs):
    width = attend_ref.shape[1] // 3
    for p in range(pairs):
        for t in range(3):
            column = t * width + (place[0] * pairs + p) * PAIR
            outs[p][:, t * PAIR : (t + 1) * PAIR] = attend_ref[
                :, pl.ds(pl.multiple_of(column, PAIR), PAIR)
            ]


def cut_attend(seq, pairs, place, attend_weight):
    rows = attend_weight.shape[0]
    return pl.pallas_call(
        functools.partial(cut_attend_body, seq, pairs),
        in_specs=[in_smem, in_vmem],
        out_specs=[in_vmem] * pairs,
        out_shape=[like((rows, 3 * PAIR))] * pairs,
        cost_estimate=cost(0, attend_weight.size * 3),
        compiler_params=params(4),
        name="cut_attend",
    )(place, attend_weight)


def cut_rest_body(seq, place, output_ref, expand_ref, shrink_ref, first_ref, second_ref, down_ref):
    s = place[0]
    wide = output_ref.shape[1] // seq
    part = shrink_ref.shape[0] // seq
    half = second_ref.shape[1] // part
    first_ref[:, :wide] = output_ref[:, at(s, wide)]
    for d in range(2 * half):
        piece = expand_ref[:, at(d * seq + s, part)]
        if d < half:
            first_ref[:, wide + d * part : wide + (d + 1) * part] = piece
        else:
            second_ref[:, (d - half) * part : (d - half + 1) * part] = piece
    for x in range(seq // 2):
        down_ref[x * part : (x + 1) * part, :] = shrink_ref[at(2 * x + lax.rem(s, 2), part), :]


def cut_rest(seq, place, output_weight, expand_weight, shrink_weight):
    rows, width = output_weight.shape
    hidden = expand_weight.shape[1]
    part = shrink_weight.shape[0] // seq
    wide, half = width // seq, hidden // seq // 2
    if part % PAIR:
        s = lax.axis_index("seq")
        up = lax.dynamic_index_in_dim(
            expand_weight.reshape(rows, -1, seq, part), s, 2, keepdims=False
        ).reshape(rows, 2 * half)
        out = lax.dynamic_slice_in_dim(output_weight, s * wide, wide, 1)
        down = lax.dynamic_index_in_dim(
            shrink_weight.reshape(seq // 2, 2, part, width), lax.rem(s, 2), 1, keepdims=False
        ).reshape(seq // 2 * part, width)
        return jnp.concatenate([out, up[:, :half]], axis=1), up[:, half:], down
    return pl.pallas_call(
        functools.partial(cut_rest_body, seq),
        in_specs=[in_smem, in_vmem, in_vmem, in_vmem],
        out_specs=[in_vmem] * 3,
        out_shape=[
            like((rows, wide + half)),
            like((rows, half)),
            like((shrink_weight.shape[0] // 2, width)),
        ],
        cost_estimate=cost(0, expand_weight.size * 6),
        compiler_params=params(8),
        name="cut_rest",
    )(place, output_weight, expand_weight, shrink_weight)


def forward_body(seq, dp, bq, bk, place, *refs):
    normed, (line, other, pk_ref, pv_ref, mq_ref, mk_ref, pm_ref) = refs[:seq], refs[seq : seq + 7]
    qkv_ref, stat_ref, weight_ref = refs[seq + 7 : seq + 10]
    groups = seq // 2
    outs, refs = refs[seq + 10 : seq + 10 + groups], refs[seq + 10 + groups :]
    ka, vt, pka, pvt, qh, o_all = refs
    s = place[0]
    s_len = qkv_ref.shape[0]
    rows = s_len // seq
    count = line.shape[0]
    shard = line.shape[1]
    order = dp_masks(dp, False)[1]
    for j in range(count):
        weight_ref[at(lax.bitwise_xor(place[1], order[j]), shard), :] = line[j]
        weight_ref[at(lax.bitwise_xor(place[1], order[count + j]), shard), :] = other[j]
    for r in range(seq):
        got = jnp.dot(normed[r][...], weight_ref[...], preferred_element_type=f32)
        qkv_ref[at(lax.bitwise_xor(s, r), rows), :] = got.astype(bf16)
    ka[:, :PAIR] = qkv_ref[:, PAIR : 2 * PAIR]
    ka[:, PAIR:] = mk_ref[...]
    pka[:, :PAIR] = pk_ref[...]
    pka[:, PAIR:] = pm_ref[...]
    first_row = lax.broadcasted_iota(jnp.int32, (VT_ROWS - HEAD, s_len), 0) == 0
    ones = jnp.where(first_row, 1.0, 0.0).astype(bf16)
    vtr = qkv_ref[:, 2 * PAIR :].T
    pvr = pv_ref[...].T
    for h in (0, 1):
        vt[h, :HEAD, :] = vtr[h * HEAD : (h + 1) * HEAD, :]
        vt[h, HEAD:, :] = ones
        pvt[h, :HEAD, :] = pvr[h * HEAD : (h + 1) * HEAD, :]
        pvt[h, HEAD:, :] = ones[:, :PREFIX_ROWS]

    def block(start, state, first, causal):
        out = []
        start = pl.multiple_of(start, bk)
        scores = [dot(ka[pl.ds(start, bk), :], qh[h, first:, :], 1, 1) for h in (0, 1)]
        for h in (0, 1):
            m, acc = state[2 * h], state[2 * h + 1]
            x = scores[h]
            if causal:
                ok = lax.broadcasted_iota(jnp.int32, x.shape, 0) <= lane(x.shape)
                x = jnp.where(ok, x, blocked)
            if first:
                keep_m, keep_acc = m[:, :first], acc[:, :first]
                m, acc = m[:, first:], acc[:, first:]
            new = jnp.maximum(m, jnp.max(x, axis=0, keepdims=True))
            p = jnp.exp(x - new)
            acc = acc * jnp.exp(m - new) + dot(vt[h, :, pl.ds(start, bk)], p.astype(bf16), 1, 0)
            if first:
                new = jnp.concatenate([keep_m, new], axis=1)
                acc = jnp.concatenate([keep_acc, acc], axis=1)
            out += [new, acc]
        return tuple(out)

    for i in range(s_len // bq):
        span = slice(i * bq, (i + 1) * bq)
        q = qkv_ref[span, :PAIR] * bf16(0.125)
        for h in (0, 1):
            qh[h, :, :PAIR] = jnp.where(head_half(h, q.shape), q, bf16(0))
            qh[h, :, PAIR:] = mq_ref[span, :]
        state = []
        for h in (0, 1):
            x = dot(pka[...], qh[h], 1, 1)
            m = jnp.max(x, axis=0, keepdims=True)
            state += [m, dot(pvt[h], jnp.exp(x - m).astype(bf16), 1, 0)]
        state = tuple(state)
        if i:
            state = lax.fori_loop(
                0, i * (bq // bk), lambda j, st: block(j * bk, st, 0, False), state
            )
        for j in range(bq // bk):
            state = block(i * bq + j * bk, state, j * bk, True)
        tops, parts = [], []
        for h in (0, 1):
            m, acc = state[2 * h], state[2 * h + 1]
            total = acc[HEAD : HEAD + 1]
            tops.append(acc[:HEAD] / total)
            parts += split3(-(m + jnp.log(total)))
        o_all[span, :] = jnp.concatenate(tops, axis=0).T.astype(bf16)
        pad = jnp.zeros((PAIR - 4 - len(parts), bq), f32)
        logs = jnp.concatenate([jnp.zeros((4, bq), f32)] + parts + [pad], axis=0).T
        stat_ref[span, :] = (logs + mq_ref[span, :].astype(f32)).astype(bf16)
    for r in range(seq):
        outs[r // 2][r % 2 * rows : (r % 2 + 1) * rows, :] = o_all[at(lax.bitwise_xor(s, r), rows), :]


def attend_forward(place, normed, line, other, pk, pv, mq, mk, pm):
    seq = len(normed)
    rows, width = normed[0].shape
    s_len = rows * seq
    bq, bk = min(2048, s_len), min(512, s_len)
    return pl.pallas_call(
        functools.partial(forward_body, seq, 2 * line.shape[0], bq, bk),
        in_specs=[in_smem] + [in_vmem] * (seq + 7),
        out_specs=[in_vmem] * (3 + seq // 2),
        out_shape=[like((s_len, 3 * PAIR)), like((s_len, PAIR)), like((width, 3 * PAIR))]
        + [like((2 * rows, PAIR))] * (seq // 2),
        scratch_shapes=[
            pltpu.VMEM((s_len, 2 * PAIR), bf16),
            pltpu.VMEM((2, VT_ROWS, s_len), bf16),
            pltpu.VMEM((PREFIX_ROWS, 2 * PAIR), bf16),
            pltpu.VMEM((2, VT_ROWS, PREFIX_ROWS), bf16),
            pltpu.VMEM((2, bq, 2 * PAIR), bf16),
            pltpu.VMEM((s_len, PAIR), bf16),
        ],
        compiler_params=params(40),
        cost_estimate=cost(
            2 * s_len * s_len * 512 + 2 * s_len * width * 3 * PAIR, s_len * width * 3, s_len * s_len
        ),
        name="attend_forward",
    )(place, *normed, line, other, pk, pv, mq, mk, pm)


def backward_body(seq, bq, bk, place, *refs):
    (qkv_ref, pk_ref, pv_ref, stat_ref, mk_ref, pm_ref), refs = refs[:6], refs[6:]
    groups = seq // 2
    o_parts, do_parts, refs = refs[:groups], refs[groups : groups + seq], refs[groups + seq :]
    grad_refs, (dp_ref,), refs = refs[:seq], refs[seq : seq + 1], refs[seq + 1 :]
    ka, va, kt, pka, pva, pkt, qh, dh, dk_acc, dv_acc, o_all, do_all, dq_all = refs
    s = place[0]
    s_len = qkv_ref.shape[0]
    rows = s_len // seq
    for r in range(seq):
        o_all[at(lax.bitwise_xor(s, r), rows), :] = o_parts[r // 2][
            r % 2 * rows : (r % 2 + 1) * rows, :
        ]
        do_all[at(lax.bitwise_xor(s, r), rows), :] = do_parts[r][...]
    ones = jnp.where(lane((s_len, PAIR)) < 3, 1.0, 0.0).astype(bf16)
    l = lane((s_len, PAIR))
    k = qkv_ref[:, PAIR : 2 * PAIR]
    for h in (0, 1):
        mine = (l >= 4 + 3 * h) & (l < 7 + 3 * h)
        ka[h, :, :PAIR] = k
        ka[h, :, PAIR:] = jnp.where(mine, bf16(1), mk_ref[...])
        pka[h, :, :PAIR] = pk_ref[...]
        pka[h, :, PAIR:] = jnp.where(mine[:PREFIX_ROWS], bf16(1), pm_ref[...])
    va[:, :PAIR] = qkv_ref[:, 2 * PAIR :]
    va[:, PAIR:] = ones
    pva[:, :PAIR] = pv_ref[...]
    pva[:, PAIR:] = ones[:PREFIX_ROWS]
    kt[...] = k.T
    pkt[...] = pk_ref[...].T
    dk_acc[...] = jnp.zeros_like(dk_acc)
    dv_acc[...] = jnp.zeros_like(dv_acc)

    def block(start, state, first, causal):
        start = pl.multiple_of(start, bk)
        here = pl.ds(start, bk)
        out = []
        dv = dk = None
        scores = [dot(ka[h, here, :], qh[h, first:, :], 1, 1) for h in (0, 1)]
        dps = [dot(va[here, :], dh[h, first:, :], 1, 1) for h in (0, 1)]
        for h in (0, 1):
            p = jnp.exp(scores[h])
            if causal:
                ok = lax.broadcasted_iota(jnp.int32, p.shape, 0) <= lane(p.shape)
                p = jnp.where(ok, p, 0.0)
            ds = (p * dps[h]).astype(bf16)
            a = dot(p.astype(bf16), dh[h, first:, :PAIR], 1, 0)
            b = dot(ds, qh[h, first:, :PAIR], 1, 0)
            dv = a if dv is None else dv + a
            dk = b if dk is None else dk + b
            c = dot(kt[h * HEAD : (h + 1) * HEAD, here], ds, 1, 0)
            if first:
                out.append(jnp.concatenate([state[h][:, :first], state[h][:, first:] + c], axis=1))
            else:
                out.append(state[h] + c)
        dv_acc[here, :] += dv
        dk_acc[here, :] += dk
        return tuple(out)

    for i in range(s_len // bq):
        span = slice(i * bq, (i + 1) * bq)
        q = qkv_ref[span, :PAIR] * bf16(0.125)
        do = do_all[span, :]
        prod = do.astype(f32) * o_all[span, :].astype(f32)
        for h in (0, 1):
            half = head_half(h, q.shape)
            qh[h, :, :PAIR] = jnp.where(half, q, bf16(0))
            qh[h, :, PAIR:] = stat_ref[span, :]
            dh[h, :, :PAIR] = jnp.where(half, do, bf16(0))
            delta = -jnp.sum(jnp.where(half, prod, 0.0), axis=1, keepdims=True)
            hi, mid, lo = split3(delta)
            n = lane((bq, PAIR))
            dh[h, :, PAIR:] = jnp.where(
                n == 0, hi, jnp.where(n == 1, mid, jnp.where(n == 2, lo, 0.0))
            ).astype(bf16)
        state = []
        dpk = dpv = jnp.zeros((PREFIX_ROWS, PAIR), f32)
        for h in (0, 1):
            p = jnp.exp(dot(pka[h], qh[h], 1, 1))
            ds = (p * dot(pva[...], dh[h], 1, 1)).astype(bf16)
            dpv = dpv + dot(p.astype(bf16), dh[h, :, :PAIR], 1, 0)
            dpk = dpk + dot(ds, qh[h, :, :PAIR], 1, 0)
            state.append(dot(pkt[h * HEAD : (h + 1) * HEAD, :], ds, 1, 0))
        dp_ref[0] = dpk if i == 0 else dp_ref[0] + dpk
        dp_ref[1] = dpv if i == 0 else dp_ref[1] + dpv
        state = tuple(state)
        if i:
            state = lax.fori_loop(
                0, i * (bq // bk), lambda j, st: block(j * bk, st, 0, False), state
            )
        for j in range(bq // bk):
            state = block(i * bq + j * bk, state, j * bk, True)
        dq_all[span, :] = (jnp.concatenate(state, axis=0) * 0.125).T.astype(bf16)
    for r in range(seq):
        here = at(lax.bitwise_xor(s, r), rows)
        grad_refs[r][:, :PAIR] = dq_all[here, :]
        grad_refs[r][:, PAIR : 2 * PAIR] = dk_acc[here, :].astype(bf16)
        grad_refs[r][:, 2 * PAIR :] = dv_acc[here, :].astype(bf16)


def attend_backward(place, qkv, pk, pv, stat, mk, pm, o_parts, do_parts):
    seq = len(do_parts)
    s_len = qkv.shape[0]
    rows = s_len // seq
    bq, bk = min(2048, s_len), min(256, s_len)
    return pl.pallas_call(
        functools.partial(backward_body, seq, bq, bk),
        in_specs=[in_smem] + [in_vmem] * (6 + seq // 2 + seq),
        out_specs=[in_vmem] * (seq + 1),
        out_shape=[like((rows, 3 * PAIR))] * seq + [like((2, PREFIX_ROWS, PAIR), f32)],
        scratch_shapes=[
            pltpu.VMEM((2, s_len, 2 * PAIR), bf16),
            pltpu.VMEM((s_len, 2 * PAIR), bf16),
            pltpu.VMEM((PAIR, s_len), bf16),
            pltpu.VMEM((2, PREFIX_ROWS, 2 * PAIR), bf16),
            pltpu.VMEM((PREFIX_ROWS, 2 * PAIR), bf16),
            pltpu.VMEM((PAIR, PREFIX_ROWS), bf16),
            pltpu.VMEM((2, bq, 2 * PAIR), bf16),
            pltpu.VMEM((2, bq, 2 * PAIR), bf16),
            pltpu.VMEM((s_len, PAIR), f32),
            pltpu.VMEM((s_len, PAIR), f32),
            pltpu.VMEM((s_len, PAIR), bf16),
            pltpu.VMEM((s_len, PAIR), bf16),
            pltpu.VMEM((s_len, PAIR), bf16),
        ],
        compiler_params=params(44),
        cost_estimate=cost(5 * s_len * s_len * 512, s_len * PAIR * 24, s_len * s_len),
        name="attend_backward",
    )(place, qkv, pk, pv, stat, mk, pm, *o_parts, *do_parts)


def dp_masks(dp, near_first):
    masks = [1] + halvings(dp)[:-1] if near_first else halvings(dp)
    order = [0]
    for mask in masks:
        order += [i ^ mask for i in order]
    return masks, order


def middle_body(seq, pairs, dp, rows, place, *refs):
    groups = seq // 2
    tokens, cots, refs = refs[:2], refs[2:4], refs[4:]
    heads, refs = refs[: 2 * groups * pairs], refs[2 * groups * pairs :]
    firsts, seconds, refs = refs[: 2 * groups], refs[2 * groups : 4 * groups], refs[4 * groups :]
    across, (few, many), refs = refs[0], (refs[1:3], refs[3:5]), refs[5:]
    normed_ref, scale_ref, out_ref, out_give_ref, back_ref, back_give_ref, wo = refs[:7]
    up, down, normed, active, grads, cot = refs[7:]
    s, me = place[0], place[1]
    width = tokens[0].shape[1]
    shard = width // dp
    wide = width // seq
    half = seconds[0].shape[2]
    part = down.shape[1] // dp
    far_order = dp_masks(dp, False)[1]
    near_order = dp_masks(dp, True)[1]
    per_array = dp // 2

    for g in range(groups):
        owner = lax.bitwise_xor(s, 2 * g)
        for t in (0, 1):
            for j in range(per_array):
                here = at(lax.bitwise_xor(me, far_order[t * per_array + j]), shard)
                wo[owner, here, :] = firsts[2 * g + t][j, :, :wide]
                wo[lax.bitwise_xor(owner, 1), here, :] = across[2 * g + t, j]
                up[owner // 2, here, :half] = firsts[2 * g + t][j, :, wide:]
                up[owner // 2, here, half:] = seconds[2 * g + t][j]
    start = 0
    for arrays, order in ((few, near_order), (many, far_order)):
        size = arrays[0].shape[1]
        for t in (0, 1):
            for j in range(per_array):
                d = lax.bitwise_xor(me, order[t * per_array + j])
                done = 0
                while done < size:
                    x, row = (start + done) // part, (start + done) % part
                    take = min(part - row, size - done)
                    to = pl.multiple_of(d * part + row, min(take, part))
                    down[x, pl.ds(to, take), :] = arrays[t][j, done : done + take, :]
                    done += take
        start += size
    for p in range(pairs):
        for g in range(groups):
            for flip in (0, 1):
                source = heads[(p * groups + g) * 2 + flip]
                owner = lax.bitwise_xor(s, 2 * g + flip)
                column = pl.ds(pl.multiple_of(owner * (pairs * PAIR) + p * PAIR, PAIR), PAIR)
                for k in (0, 1):
                    here = k ^ flip
                    normed[k * rows : (k + 1) * rows, column] = source[
                        here * rows : (here + 1) * rows, :
                    ]
    for k in (0, 1):
        cot[k * rows : (k + 1) * rows, :] = cots[k][...]
    for k in (0, 1):
        merged = normed[k * rows : (k + 1) * rows, :]
        acc = tokens[k][...].astype(f32) + jnp.concatenate(
            [dot(merged, wo[o], 1, 0) for o in range(seq)], axis=1
        )
        unit, scale = normalize(acc)
        normed[k * rows : (k + 1) * rows, :] = unit.astype(bf16)
        if k == 0:
            out_ref[...] = acc
            normed_ref[...] = unit.astype(bf16)
            scale_ref[...] = jnp.broadcast_to(scale, scale_ref.shape)
    chunk = min(512, 2 * half)
    inner = 2 * half // chunk

    def step(h, carry):
        block, piece = h // inner, lax.rem(h, inner)
        w_up = up[block, :, at(piece, chunk)]
        w_down = down[block, at(piece, chunk), :]
        u = jnp.dot(normed[...], w_up, preferred_element_type=f32)
        gelu_grad = dot(cot[...], w_down, 1, 1)
        square = u * u
        side = 0.5 + 0.5 * jnp.tanh(u * (0.7978845608028654 + 0.7978845608028654 * 0.044715 * square))
        rise = 2 * 0.7978845608028654 + 6 * 0.7978845608028654 * 0.044715 * square
        slope = side + side * (1.0 - side) * (u * rise)
        active[block, :, at(piece, chunk)] = (u * side).astype(bf16)
        grads[block, :, at(piece, chunk)] = (gelu_grad * slope).astype(bf16)
        return carry

    lax.fori_loop(0, groups * inner, step, 0)
    for n in (0, 1):
        side = slice(n * width // 2, (n + 1) * width // 2)
        total = sum(dot(grads[g], up[g, side, :], 1, 1) for g in range(groups)).astype(bf16)
        back_ref[:, side] = total[:rows]
        back_give_ref[:, side] = total[rows:]
    for n in (0, 1):
        side = slice(n * width // 2, (n + 1) * width // 2)
        total = sum(dot(active[g], down[g, :, side], 1, 0) for g in range(groups))
        out_give_ref[:, side] = total[rows:].astype(bf16)
        out_ref[:, side] += total[:rows]


def middle(seq, dp, pairs, place, tokens, cots, heads, firsts, seconds, across, few, many):
    rows, width = tokens[0].shape
    groups = seq // 2
    half = seconds[0].shape[2]
    part = (few[0].shape[1] + many[0].shape[1]) // groups
    hidden = groups * 2 * half
    return pl.pallas_call(
        functools.partial(middle_body, seq, pairs, dp, rows),
        in_specs=[in_smem]
        + [in_vmem] * (9 + len(heads) + len(firsts) + len(seconds)),
        out_specs=[in_vmem] * 7,
        out_shape=[
            like((rows, width)),
            like((rows, PAIR), f32),
            like((rows, width), f32),
            like((rows, width)),
            like((rows, width)),
            like((rows, width)),
            like((seq, width, width // seq)),
        ],
        scratch_shapes=[
            pltpu.VMEM((groups, width, 2 * half), bf16),
            pltpu.VMEM((groups, dp * part, width), bf16),
            pltpu.VMEM((2 * rows, width), bf16),
            pltpu.VMEM((groups, 2 * rows, 2 * half), bf16),
            pltpu.VMEM((groups, 2 * rows, 2 * half), bf16),
            pltpu.VMEM((2 * rows, width), bf16),
        ],
        compiler_params=params(42),
        cost_estimate=cost(
            16 * rows * width * hidden + 4 * rows * width * width,
            4 * width * hidden + 20 * rows * width,
            2 * rows * hidden,
        ),
        name="middle",
    )(place, *tokens, *cots, *heads, *firsts, *seconds, across, *few, *many)


def turn_body(seq, pairs, place, unit_ref, scale_ref, cot_ref, own_ref, got_ref, wo, *refs):
    mid_grad_ref, grads, (merged,) = refs[0], refs[1:-1], refs[-1:]
    s = place[0]
    wide = wo.shape[2]
    grad = own_ref[...].astype(f32) + got_ref[...].astype(f32)
    mid_grad = cot_ref[...].astype(f32) + normalize_back(
        unit_ref[...].astype(f32), scale_ref[:, :1], grad
    )
    mid_grad_ref[...] = mid_grad
    rounded = mid_grad.astype(bf16)
    grad = sum(dot(rounded[:, o * wide : (o + 1) * wide], wo[o], 1, 1) for o in range(seq))
    merged[...] = grad.astype(bf16)
    for r in range(seq):
        for p in range(pairs):
            column = lax.bitwise_xor(s, r) * (pairs * PAIR) + p * PAIR
            grads[p * seq + r][...] = merged[:, pl.ds(pl.multiple_of(column, PAIR), PAIR)]


def turn(seq, pairs, place, unit, scale, cot, own, got, wo):
    rows, width = unit.shape
    return pl.pallas_call(
        functools.partial(turn_body, seq, pairs),
        in_specs=[in_smem] + [in_vmem] * 6,
        out_specs=[in_vmem] * (1 + seq * pairs),
        out_shape=[like((rows, width), f32)] + [like((rows, PAIR))] * (seq * pairs),
        scratch_shapes=[pltpu.VMEM((rows, width), bf16)],
        compiler_params=params(24),
        cost_estimate=cost(2 * rows * width * width, 16 * rows * width),
        name="turn",
    )(place, unit, scale, cot, own, got, wo)


def finish_body(tokens_ref, mid_grad_ref, own_ref, got_ref, out_ref):
    normed, scale = normalize(tokens_ref[...].astype(f32))
    grad = own_ref[...] + got_ref[...].astype(f32)
    out_ref[...] = (mid_grad_ref[...] + normalize_back(normed, scale, grad)).astype(bf16)


def finish(tokens, mid_grad, own, got):
    return pl.pallas_call(
        finish_body,
        in_specs=[in_vmem] * 4,
        out_specs=in_vmem,
        out_shape=like(tokens.shape),
        compiler_params=params(24),
        cost_estimate=cost(tokens.size * 20, tokens.size * 14),
        name="finish",
    )(tokens, mid_grad, own, got)


def masks(lengths, s_len):
    e0 = lengths[0]
    e1 = e0 + lengths[1]
    e2 = e1 + lengths[2]
    pos = jnp.arange(s_len, dtype=jnp.int32)
    doc = sum((pos >= e).astype(jnp.int32) for e in (e0, e1, e2))
    l = lax.broadcasted_iota(jnp.int32, (s_len, PAIR), 1)
    same = l == doc[:, None]
    mq = jnp.where((l < 4) & ~same, blocked, 0.0).astype(bf16)
    mk = jnp.where((l < 4) & same, 1.0, 0.0).astype(bf16)
    r = lax.broadcasted_iota(jnp.int32, (PREFIX_ROWS, PAIR), 0)
    lp = lax.broadcasted_iota(jnp.int32, (PREFIX_ROWS, PAIR), 1)
    pm = jnp.where((r >= PREFIX) & (lp == 3), 1.0, 0.0).astype(bf16)
    return mq, mk, pm


def parts_of(v):
    return [p.astype(bf16) for p in split3(v)]


def precise(a, b, side):
    high, mid, low = parts_of(a)
    few = a.shape[0]
    total = None
    for stack, part in zip(([high, mid, low], [high, mid], [high]), parts_of(b)):
        got = dot(jnp.concatenate(stack, axis=0), part, 1, side)
        for k in reversed(range(len(stack))):
            piece = got[k * few : (k + 1) * few]
            total = piece if total is None else total + piece
    return total


def full(a, b):
    return jnp.dot(a, b, precision=lax.Precision.HIGHEST, preferred_element_type=f32)


def precise_outer(a, b):
    high, mid, low = parts_of(a)
    high_b, mid_b, low_b = parts_of(b)
    left = jnp.concatenate([low, mid, high, mid, high, high], axis=0)
    right = jnp.concatenate([high_b, mid_b, low_b, high_b, mid_b, high_b], axis=0)
    return dot(left.astype(f32).T.astype(bf16), right, 1, 0)


def norm_body(rows_ref, out_ref):
    out_ref[...] = normalize(rows_ref[...].astype(f32))[0].astype(bf16)


def norm(rows):
    return pl.pallas_call(
        norm_body,
        in_specs=[in_vmem],
        out_specs=in_vmem,
        out_shape=like(rows.shape),
        compiler_params=params(8),
        cost_estimate=cost(rows.size * 8, rows.size * 4),
        name="norm",
    )(rows)


def reparam_body(seq, pairs, place, embed, inner, inner_bias, outer, outer_bias, kv, hidden, *parts):
    s = place[0]
    half = outer.shape[1] // 2
    hidden[...] = jnp.tanh(full(embed[...], inner[...]) + inner_bias[...])
    both = full(hidden[...], outer[...]) + outer_bias[...]
    kv[...] = both[:PREFIX]
    *parts, held = parts
    row = lax.broadcasted_iota(jnp.int32, both.shape, 0)
    held[...] = jnp.where(row < PREFIX, both, 0.0)
    for t in (0, 1):
        for p in range(pairs):
            column = pl.multiple_of(t * half + (s * pairs + p) * PAIR, PAIR)
            parts[t * pairs + p][...] = held[:, pl.ds(column, PAIR)].astype(bf16)


def reparam(seq, pairs, place, embed, inner, inner_bias, outer, outer_bias):
    width = outer.shape[1]
    return pl.pallas_call(
        functools.partial(reparam_body, seq, pairs),
        in_specs=[in_smem] + [in_vmem] * 5,
        out_specs=[in_vmem] * (2 + 2 * pairs),
        out_shape=[like((PREFIX, width), f32), like((PREFIX_ROWS, inner.shape[1]), f32)]
        + [like((PREFIX_ROWS, PAIR))] * (2 * pairs),
        scratch_shapes=[pltpu.VMEM((PREFIX_ROWS, width), f32)],
        compiler_params=params(20),
        cost_estimate=cost(12 * PREFIX_ROWS * (inner.size + outer.size), 4 * (inner.size + outer.size)),
        name="reparam",
    )(place, embed, inner, inner_bias[None], outer, outer_bias[None])


def reparam_back_body(seq, pairs, place, embed, inner, outer, hidden, *refs):
    got, (d_embed, d_inner, d_inner_bias, d_outer, d_outer_bias, grad) = refs[:2], refs[2:]
    s = place[0]
    half = outer.shape[1] // 2
    for r in range(seq):
        for t in (0, 1):
            for p in range(pairs):
                column = t * half + (lax.bitwise_xor(s, r) * pairs + p) * PAIR
                grad[:, pl.ds(pl.multiple_of(column, PAIR), PAIR)] = got[r % 2][r // 2, p, t]
    d_outer_bias[...] = jnp.sum(grad[...], axis=0, keepdims=True)
    d_outer[...] = precise_outer(hidden[...], grad[...])
    back = precise(grad[...], outer[...], 1) * (1.0 - hidden[...] * hidden[...])
    d_inner_bias[...] = jnp.sum(back, axis=0, keepdims=True)
    d_inner[...] = precise_outer(embed[...], back)
    d_embed[...] = precise(back, inner[...], 1)[:PREFIX]


def reparam_back(pairs, place, embed, inner, outer, hidden, got):
    seq = 2 * got[0].shape[0]
    wide, (deep, width) = inner.shape[0], outer.shape
    outs = pl.pallas_call(
        functools.partial(reparam_back_body, seq, pairs),
        in_specs=[in_smem] + [in_vmem] * 6,
        out_specs=[in_vmem] * 5,
        out_shape=[
            like((PREFIX, wide), f32),
            like((wide, deep), f32),
            like((1, deep), f32),
            like((deep, width), f32),
            like((1, width), f32),
        ],
        scratch_shapes=[pltpu.VMEM((PREFIX_ROWS, width), f32)],
        compiler_params=params(28),
        cost_estimate=cost(24 * PREFIX_ROWS * (inner.size + outer.size), 8 * (inner.size + outer.size)),
        name="reparam_back",
    )(place, embed, inner, outer, hidden, *got)
    return outs[0], outs[1], outs[2][0], outs[3], outs[4][0]


def product_body(pairs, adds, out_dtype, *refs):
    weights, refs = refs[:pairs], refs[pairs:]
    count = len(refs) // (pairs + adds + 1)
    rows, refs = refs[: count * pairs], refs[count * pairs :]
    extra, outs = refs[: count * adds], refs[count * adds :]
    for i in range(count):
        total = sum(dot(rows[i * pairs + p][...], weights[p][...], 1, 1) for p in range(pairs))
        if adds:
            total = total + extra[i][...].astype(f32)
        outs[i][...] = total.astype(out_dtype)


def product(weights, rows, extra, out_dtype):
    pairs = len(weights)
    height, width = rows[0][0].shape[0], weights[0].shape[0]
    flat = [w for entry in rows for w in entry]
    return pl.pallas_call(
        functools.partial(product_body, pairs, int(bool(extra)), out_dtype),
        in_specs=[in_vmem] * (pairs + len(flat) + len(extra)),
        out_specs=[in_vmem] * len(rows),
        out_shape=[like((height, width), out_dtype)] * len(rows),
        compiler_params=params(24),
        cost_estimate=cost(
            2 * len(flat) * height * width * flat[0].shape[1], 4 * len(rows) * height * width
        ),
        name="product",
    )(*weights, *flat, *extra)


def halvings(count):
    steps = []
    while count > 1:
        count //= 2
        steps.append(count)
    return steps


def swap(value, axis, size, mask):
    return lax.ppermute(value, axis, [(i, i ^ mask) for i in range(size)])


def after(value, *events):
    return lax.optimization_barrier((value, *events))[0] if events else value


def spread_seq(value, seq):
    held = {0: value}
    for mask in halvings(seq):
        for r in list(held):
            held[r ^ mask] = swap(held[r], "seq", seq, mask)
    return [held[r] for r in range(seq)]


def exchange_seq(pieces, seq):
    return [pieces[0]] + [swap(pieces[r], "seq", seq, r) for r in range(1, seq)]


def shards(seq, dp, tokens, lengths, attend_weight, output_weight, expand_weight, shrink_weight,
           prefix_embed, inner_weight, inner_bias, outer_weight, outer_bias, cotangent):
    s = lax.axis_index("seq")
    rows, width = tokens.shape[1:]
    s_len = rows * seq
    pairs = width // seq // PAIR
    groups = seq // 2
    token_rows, cot_rows = tokens[0], cotangent[0]
    place = jnp.stack([s, lax.axis_index("dp")]).astype(jnp.int32)
    near_mask, far_masks = dp_masks(dp, False)[0][-1], dp_masks(dp, False)[0][:-1]

    def over(value, mask, *events):
        return swap(after(value, *events), "dp", dp, mask)

    def other_core(value, *events):
        return swap(after(value, *events), "seq", seq, 1)

    def line(piece, begin=(), later=()):
        held, arrived = piece, []
        for mask in far_masks:
            arrived.append(over(held, mask, *(later if arrived else begin)))
            held = jnp.concatenate([held, arrived[-1]])
        return held, arrived

    def spread(value, *events):
        held = {0: after(value, *events)}
        for mask in halvings(seq)[:-1]:
            for g in list(held):
                held[g ^ mask // 2] = swap(held[g], "seq", seq, mask)
        return [held[g] for g in range(groups)]

    token_far = spread(token_rows)
    token_pair = (token_rows, other_core(token_rows))
    cot_pair = (cot_rows, other_core(cot_rows))
    attend_lines = [
        line(w[None], later=(token_pair[1], cot_pair[1]))
        for w in cut_attend(seq, pairs, place, attend_weight)
    ]
    first, second, down = cut_rest(seq, place, output_weight, expand_weight, shrink_weight)
    quarter = down.shape[0] // 4
    few = over(down[None, :quarter], near_mask, attend_lines[0][1][0])
    few = jnp.concatenate([down[None, :quarter], few])
    attend_pairs = [(w, over(w, near_mask)) for w, _ in attend_lines]
    normed_rows = [norm(w) for w in token_pair]
    line_a, steps_a = line(
        first[None],
        (few, *[steps[-1] for _, steps in attend_lines]),
        (attend_pairs[0][1],),
    )
    for w in token_far[1:]:
        normed_rows += [norm(w), norm(other_core(w))]
    line_b, steps_b = line(second[None], (steps_a[0], attend_pairs[0][1]), (attend_pairs[-1][1],))

    embed = after(prefix_embed, attend_lines[-1][1][-1])
    embed = jnp.pad(embed, ((0, PREFIX_ROWS - PREFIX), (0, 0)))
    prefix_kv, prefix_hidden, *prefix_parts = reparam(
        seq, pairs, place, embed, inner_weight, inner_bias, outer_weight, outer_bias
    )
    prefix_pairs = [(prefix_parts[p], prefix_parts[pairs + p]) for p in range(pairs)]
    mask_q, mask_k, mask_p = masks(lengths[0], s_len)
    saved, heads = [], []

    def attend(p, *events):
        qkv, stat, weight, *outs = attend_forward(
            after(place, *events), normed_rows, *attend_pairs[p], *prefix_pairs[p],
            mask_q, mask_k, mask_p,
        )
        saved.append((qkv, stat, weight, outs))
        for g in range(groups):
            got = outs[0] if g == 0 else swap(outs[g], "seq", seq, 2 * g)
            heads.extend((got, other_core(got)))

    attend(0, attend_pairs[-1][1], steps_a[-1], steps_b[0])
    other_a = over(line_a, near_mask, attend_pairs[-1][1])
    near_a = spread(line_a, normed_rows[-1])
    many = over(down[None, quarter:], far_masks[0], steps_b[0])
    many = jnp.concatenate([down[None, quarter:], many])
    begun = saved[0][1]
    other_b = over(line_b, near_mask, begun, other_a)
    far_a = spread(other_a, begun, *near_a)
    for mask in far_masks[1:]:
        many = jnp.concatenate([many, over(many, mask, begun, steps_b[-1])])
    for p in range(1, pairs):
        attend(p, other_a, *near_a, steps_b[-1])
    ended = saved[-1][1]
    many = (many, over(many, near_mask, ended, other_b, *far_a, *heads[: 2 * groups]))
    near_b = spread(line_b, ended, *far_a)
    far_b = spread(other_b, ended, *far_a)
    for mask in far_masks[:-1]:
        few = jnp.concatenate([few, over(few, mask, ended)])
    few = (few, over(few, far_masks[-1], *heads, *near_b))
    ups = [
        [w for g in range(groups) for w in (a[g], b[g])]
        for a, b in ((near_a, far_a), (near_b, far_b))
    ]
    wide = width // seq
    across = other_core(jnp.stack([w[..., :wide] for w in ups[0]]))
    unit, scale, out_own, out_give, back_own, back_give, wo = middle(
        seq, dp, pairs, place, token_pair, cot_pair, heads, *ups, across, few, many
    )
    mid_grad, *out_grads = turn(
        seq, pairs, place, unit, scale, cot_rows, back_own, other_core(back_give), wo
    )
    outputs = (out_own + other_core(out_give).astype(f32)).astype(bf16)
    grads, prefix_terms = [], []
    for p in range(pairs):
        qkv, stat, weight, outs = saved[p]
        got = exchange_seq(out_grads[p * seq : (p + 1) * seq], seq)
        *parts, prefix_part = attend_backward(
            place, qkv, *prefix_pairs[p], stat, mask_k, mask_p, outs, got
        )
        grads.append(parts)
        prefix_terms.append(prefix_part)

    prefix_sum = jnp.stack(spread(jnp.stack(prefix_terms)))

    weights = [entry[2] for entry in saved]
    block = lambda r: [grads[p][r] for p in range(pairs)]
    sent = product(weights, [block(r) for r in range(1, seq, 2)], [], bf16)
    got = [other_core(v) for v in sent]
    late = [after(weights[0], prefix_sum), *weights[1:]]
    evens = product(late, [block(r) for r in range(2, seq, 2)], got[1:], bf16)
    (own,) = product(weights, [block(0)], got[:1], f32)
    left = dict(zip(range(2, seq, 2), evens))
    for mask in reversed(halvings(seq)[:-1]):
        keep = {}
        for r in [0, *left]:
            if r & mask:
                continue
            arrived = swap(left[r ^ mask], "seq", seq, mask)
            if r:
                keep[r] = left[r] + arrived
            elif len(left) > 1:
                own = own + arrived.astype(f32)
        left = keep
    input_grad = finish(token_rows, mid_grad, own, arrived)

    prefix_sum = after(prefix_sum, *evens)
    reach = [0]
    for mask in far_masks:
        reach += [mask ^ other for other in reach]
    terms = [prefix_sum] + [swap(prefix_sum, "dp", dp, mask) for mask in reach[1:]]
    while len(terms) > 1:
        half = len(terms) // 2
        terms = [terms[i] + terms[i + half] for i in range(half)]
    prefix_sum = terms[0] + swap(terms[0], "dp", dp, near_mask)
    prefix_all = (prefix_sum, other_core(prefix_sum))
    back = reparam_back(
        pairs, place, embed, inner_weight, outer_weight, prefix_hidden, prefix_all
    )
    return (outputs[None], input_grad[None], *back, prefix_kv)


def solution(mesh):
    placed = (
        P("dp", "seq", None),
        P("dp", None),
        P("dp", None),
        P("dp", None),
        P("dp", None),
        P("dp", None),
        P(),
        P(),
        P(),
        P(),
        P(),
        P("dp", "seq", None),
    )
    return jax.shard_map(
        functools.partial(shards, mesh.shape["seq"], mesh.shape["dp"]),
        mesh=mesh,
        in_specs=placed,
        out_specs=(P("dp", "seq", None), P("dp", "seq", None), P(), P(), P(), P(), P(), P()),
        check_vma=False,
    )
```

```python
import functools

import jax
import jax.numpy as jnp
from jax import lax
from jax.experimental import pallas as pl
from jax.experimental.pallas import tpu as pltpu
from jax.sharding import PartitionSpec as P

PREFIX = 10
HEAD = 64
PAIR = 128
PREFIX_ROWS = 16
VT_ROWS = 80
blocked = -1e30
norm_epsilon = 1e-05
f32, bf16 = jnp.float32, jnp.bfloat16
in_vmem = pl.BlockSpec(memory_space=pltpu.VMEM)
in_smem = pl.BlockSpec(memory_space=pltpu.SMEM)
in_place = pl.BlockSpec(memory_space=pl.ANY)


def params(mib):
    return pltpu.CompilerParams(vmem_limit_bytes=mib << 20)


def cost(flops, moved, special=0):
    return pl.CostEstimate(flops=int(flops), bytes_accessed=int(moved), transcendentals=int(special))


def like(shape, dtype=bf16):
    return jax.ShapeDtypeStruct(shape, dtype)


def dot(a, b, ca, cb):
    return lax.dot_general(a, b, (((ca,), (cb,)), ((), ())), preferred_element_type=f32)


def lane(shape):
    return lax.broadcasted_iota(jnp.int32, shape, len(shape) - 1)


def head_half(h, shape):
    l = lane(shape)
    return (l < HEAD) if h == 0 else (l >= HEAD)


def keep_past(x, fill):
    size = x.shape[0]
    square = x[:, :size]
    ok = lax.broadcasted_iota(jnp.int32, square.shape, 0) <= lane(square.shape)
    square = jnp.where(ok, square, fill)
    return square if x.shape[1] == size else jnp.concatenate([square, x[:, size:]], axis=1)


def split3(v):
    hi = v.astype(bf16)
    r = v - hi.astype(f32)
    mid = r.astype(bf16)
    lo = (r - mid.astype(f32)).astype(bf16)
    return hi.astype(f32), mid.astype(f32), lo.astype(f32)


def at(index, size):
    return pl.ds(pl.multiple_of(index * size, size), size)


def normalize(hidden):
    centered = hidden - jnp.mean(hidden, axis=-1, keepdims=True)
    scale = lax.rsqrt(jnp.mean(centered * centered, axis=-1, keepdims=True) + norm_epsilon)
    return centered * scale, scale


def normalize_back(normed, scale, grad):
    return scale * (
        grad
        - jnp.mean(grad, axis=-1, keepdims=True)
        - normed * jnp.mean(grad * normed, axis=-1, keepdims=True)
    )


def cut_attend_body(seq, pairs, place, attend_ref, *outs):
    width = attend_ref.shape[1] // 3
    for p in range(pairs):
        for t in range(3):
            column = t * width + (place[0] * pairs + p) * PAIR
            outs[p][:, t * PAIR : (t + 1) * PAIR] = attend_ref[
                :, pl.ds(pl.multiple_of(column, PAIR), PAIR)
            ]


def cut_attend(seq, pairs, place, attend_weight):
    rows = attend_weight.shape[0]
    return pl.pallas_call(
        functools.partial(cut_attend_body, seq, pairs),
        in_specs=[in_smem, in_vmem],
        out_specs=[in_vmem] * pairs,
        out_shape=[like((rows, 3 * PAIR))] * pairs,
        cost_estimate=cost(0, attend_weight.size * 3),
        compiler_params=params(4),
        name="cut_attend",
    )(place, attend_weight)


def cut_rest_body(seq, place, output_ref, expand_ref, shrink_ref, first_ref, second_ref, down_ref):
    s = place[0]
    wide = output_ref.shape[1] // seq
    part = shrink_ref.shape[0] // seq
    half = second_ref.shape[1] // part
    first_ref[:, :wide] = output_ref[:, at(s, wide)]
    for d in range(2 * half):
        piece = expand_ref[:, at(d * seq + s, part)]
        if d < half:
            first_ref[:, wide + d * part : wide + (d + 1) * part] = piece
        else:
            second_ref[:, (d - half) * part : (d - half + 1) * part] = piece
    for x in range(seq // 2):
        down_ref[x * part : (x + 1) * part, :] = shrink_ref[at(2 * x + lax.rem(s, 2), part), :]


def cut_rest(seq, place, output_weight, expand_weight, shrink_weight):
    rows, width = output_weight.shape
    hidden = expand_weight.shape[1]
    part = shrink_weight.shape[0] // seq
    wide, half = width // seq, hidden // seq // 2
    if part % PAIR:
        s = lax.axis_index("seq")
        up = lax.dynamic_index_in_dim(
            expand_weight.reshape(rows, -1, seq, part), s, 2, keepdims=False
        ).reshape(rows, 2 * half)
        out = lax.dynamic_slice_in_dim(output_weight, s * wide, wide, 1)
        down = lax.dynamic_index_in_dim(
            shrink_weight.reshape(seq // 2, 2, part, width), lax.rem(s, 2), 1, keepdims=False
        ).reshape(seq // 2 * part, width)
        return jnp.concatenate([out, up[:, :half]], axis=1), up[:, half:], down
    return pl.pallas_call(
        functools.partial(cut_rest_body, seq),
        in_specs=[in_smem, in_vmem, in_vmem, in_vmem],
        out_specs=[in_vmem] * 3,
        out_shape=[
            like((rows, wide + half)),
            like((rows, half)),
            like((shrink_weight.shape[0] // 2, width)),
        ],
        cost_estimate=cost(0, expand_weight.size * 6),
        compiler_params=params(8),
        name="cut_rest",
    )(place, output_weight, expand_weight, shrink_weight)


def forward_body(seq, dp, bq, bk, place, *refs):
    normed, (line, other, pk_ref, pv_ref, mq_ref, mk_ref, pm_ref) = refs[:seq], refs[seq : seq + 7]
    qkv_ref, stat_ref, weight_ref = refs[seq + 7 : seq + 10]
    groups = seq // 2
    outs, refs = refs[seq + 10 : seq + 10 + groups], refs[seq + 10 + groups :]
    ka, vt, pka, pvt, qh, o_all = refs
    s = place[0]
    s_len = qkv_ref.shape[0]
    rows = s_len // seq
    count = line.shape[0]
    shard = line.shape[1]
    order = dp_masks(dp, False)[1]
    for j in range(count):
        weight_ref[at(lax.bitwise_xor(place[1], order[j]), shard), :] = line[j]
        weight_ref[at(lax.bitwise_xor(place[1], order[count + j]), shard), :] = other[j]
    for r in range(seq):
        got = jnp.dot(normed[r][...], weight_ref[...], preferred_element_type=f32)
        qkv_ref[at(lax.bitwise_xor(s, r), rows), :] = got.astype(bf16)
    ka[:, :PAIR] = qkv_ref[:, PAIR : 2 * PAIR]
    ka[:, PAIR:] = mk_ref[...]
    pka[:, :PAIR] = pk_ref[...]
    pka[:, PAIR:] = pm_ref[...]
    first_row = lax.broadcasted_iota(jnp.int32, (VT_ROWS - HEAD, s_len), 0) == 0
    ones = jnp.where(first_row, 1.0, 0.0).astype(bf16)
    vtr = qkv_ref[:, 2 * PAIR :].T
    pvr = pv_ref[...].T
    for h in (0, 1):
        vt[h, :HEAD, :] = vtr[h * HEAD : (h + 1) * HEAD, :]
        vt[h, HEAD:, :] = ones
        pvt[h, :HEAD, :] = pvr[h * HEAD : (h + 1) * HEAD, :]
        pvt[h, HEAD:, :] = ones[:, :PREFIX_ROWS]

    def block(start, state, first, causal):
        out = []
        start = pl.multiple_of(start, bk)
        scores = [dot(ka[pl.ds(start, bk), :], qh[h, first:, :], 1, 1) for h in (0, 1)]
        for h in (0, 1):
            m, acc = state[2 * h], state[2 * h + 1]
            x = scores[h]
            if causal:
                x = keep_past(x, blocked)
            if first:
                keep_m, keep_acc = m[:, :first], acc[:, :first]
                m, acc = m[:, first:], acc[:, first:]
            new = jnp.maximum(m, jnp.max(x, axis=0, keepdims=True))
            p = jnp.exp(x - new)
            acc = acc * jnp.exp(m - new) + dot(vt[h, :, pl.ds(start, bk)], p.astype(bf16), 1, 0)
            if first:
                new = jnp.concatenate([keep_m, new], axis=1)
                acc = jnp.concatenate([keep_acc, acc], axis=1)
            out += [new, acc]
        return tuple(out)

    for i in range(s_len // bq):
        span = slice(i * bq, (i + 1) * bq)
        q = qkv_ref[span, :PAIR] * bf16(0.125)
        for h in (0, 1):
            qh[h, :, :PAIR] = jnp.where(head_half(h, q.shape), q, bf16(0))
            qh[h, :, PAIR:] = mq_ref[span, :]
        state = []
        for h in (0, 1):
            x = dot(pka[...], qh[h], 1, 1)
            m = jnp.max(x, axis=0, keepdims=True)
            state += [m, dot(pvt[h], jnp.exp(x - m).astype(bf16), 1, 0)]
        state = tuple(state)
        if i:
            state = lax.fori_loop(
                0, i * (bq // bk), lambda j, st: block(j * bk, st, 0, False), state
            )
        for j in range(bq // bk):
            state = block(i * bq + j * bk, state, j * bk, True)
        tops, parts = [], []
        for h in (0, 1):
            m, acc = state[2 * h], state[2 * h + 1]
            total = acc[HEAD : HEAD + 1]
            tops.append(acc[:HEAD] / total)
            parts += split3(-(m + jnp.log(total)))
        o_all[span, :] = jnp.concatenate(tops, axis=0).T.astype(bf16)
        pad = jnp.zeros((PAIR - 4 - len(parts), bq), f32)
        logs = jnp.concatenate([jnp.zeros((4, bq), f32)] + parts + [pad], axis=0).T
        stat_ref[span, :] = (logs + mq_ref[span, :].astype(f32)).astype(bf16)
    for r in range(seq):
        outs[r // 2][r % 2 * rows : (r % 2 + 1) * rows, :] = o_all[at(lax.bitwise_xor(s, r), rows), :]


def attend_forward(place, normed, line, other, pk, pv, mq, mk, pm):
    seq = len(normed)
    rows, width = normed[0].shape
    s_len = rows * seq
    bq, bk = min(2048, s_len), min(512, s_len)
    return pl.pallas_call(
        functools.partial(forward_body, seq, 2 * line.shape[0], bq, bk),
        in_specs=[in_smem] + [in_vmem] * (seq + 7),
        out_specs=[in_vmem] * (3 + seq // 2),
        out_shape=[like((s_len, 3 * PAIR)), like((s_len, PAIR)), like((width, 3 * PAIR))]
        + [like((2 * rows, PAIR))] * (seq // 2),
        scratch_shapes=[
            pltpu.VMEM((s_len, 2 * PAIR), bf16),
            pltpu.VMEM((2, VT_ROWS, s_len), bf16),
            pltpu.VMEM((PREFIX_ROWS, 2 * PAIR), bf16),
            pltpu.VMEM((2, VT_ROWS, PREFIX_ROWS), bf16),
            pltpu.VMEM((2, bq, 2 * PAIR), bf16),
            pltpu.VMEM((s_len, PAIR), bf16),
        ],
        compiler_params=params(40),
        cost_estimate=cost(
            2 * s_len * s_len * 512 + 2 * s_len * width * 3 * PAIR, s_len * width * 3, s_len * s_len
        ),
        name="attend_forward",
    )(place, *normed, line, other, pk, pv, mq, mk, pm)


def backward_body(seq, bq, bk, place, *refs):
    (qkv_ref, pk_ref, pv_ref, stat_ref, mk_ref, pm_ref), refs = refs[:6], refs[6:]
    groups = seq // 2
    o_parts, do_parts, refs = refs[:groups], refs[groups : groups + seq], refs[groups + seq :]
    grad_refs, (dp_ref,), refs = refs[:seq], refs[seq : seq + 1], refs[seq + 1 :]
    ka, va, kt, pka, pva, pkt, qh, dh, dk_acc, dv_acc, o_all, do_all, dq_all = refs
    s = place[0]
    s_len = qkv_ref.shape[0]
    rows = s_len // seq
    for r in range(seq):
        o_all[at(lax.bitwise_xor(s, r), rows), :] = o_parts[r // 2][
            r % 2 * rows : (r % 2 + 1) * rows, :
        ]
        do_all[at(lax.bitwise_xor(s, r), rows), :] = do_parts[r][...]
    ones = jnp.where(lane((s_len, PAIR)) < 3, 1.0, 0.0).astype(bf16)
    l = lane((s_len, PAIR))
    k = qkv_ref[:, PAIR : 2 * PAIR]
    for h in (0, 1):
        mine = (l >= 4 + 3 * h) & (l < 7 + 3 * h)
        ka[h, :, :PAIR] = k
        ka[h, :, PAIR:] = jnp.where(mine, bf16(1), mk_ref[...])
        pka[h, :, :PAIR] = pk_ref[...]
        pka[h, :, PAIR:] = jnp.where(mine[:PREFIX_ROWS], bf16(1), pm_ref[...])
    va[:, :PAIR] = qkv_ref[:, 2 * PAIR :]
    va[:, PAIR:] = ones
    pva[:, :PAIR] = pv_ref[...]
    pva[:, PAIR:] = ones[:PREFIX_ROWS]
    kt[...] = k.T
    pkt[...] = pk_ref[...].T
    dk_acc[...] = jnp.zeros_like(dk_acc)
    dv_acc[...] = jnp.zeros_like(dv_acc)

    def block(start, state, first, causal):
        start = pl.multiple_of(start, bk)
        here = pl.ds(start, bk)
        out = []
        dv = dk = None
        scores = [dot(ka[h, here, :], qh[h, first:, :], 1, 1) for h in (0, 1)]
        dps = [dot(va[here, :], dh[h, first:, :], 1, 1) for h in (0, 1)]
        for h in (0, 1):
            p = jnp.exp(scores[h])
            if causal:
                p = keep_past(p, 0.0)
            ds = (p * dps[h]).astype(bf16)
            a = dot(p.astype(bf16), dh[h, first:, :PAIR], 1, 0)
            b = dot(ds, qh[h, first:, :PAIR], 1, 0)
            dv = a if dv is None else dv + a
            dk = b if dk is None else dk + b
            c = dot(kt[h * HEAD : (h + 1) * HEAD, here], ds, 1, 0)
            if first:
                out.append(jnp.concatenate([state[h][:, :first], state[h][:, first:] + c], axis=1))
            else:
                out.append(state[h] + c)
        dv_acc[here, :] += dv
        dk_acc[here, :] += dk
        return tuple(out)

    for i in range(s_len // bq):
        span = slice(i * bq, (i + 1) * bq)
        q = qkv_ref[span, :PAIR] * bf16(0.125)
        do = do_all[span, :]
        prod = do.astype(f32) * o_all[span, :].astype(f32)
        for h in (0, 1):
            half = head_half(h, q.shape)
            qh[h, :, :PAIR] = jnp.where(half, q, bf16(0))
            qh[h, :, PAIR:] = stat_ref[span, :]
            dh[h, :, :PAIR] = jnp.where(half, do, bf16(0))
            delta = -jnp.sum(jnp.where(half, prod, 0.0), axis=1, keepdims=True)
            hi, mid, lo = split3(delta)
            n = lane((bq, PAIR))
            dh[h, :, PAIR:] = jnp.where(
                n == 0, hi, jnp.where(n == 1, mid, jnp.where(n == 2, lo, 0.0))
            ).astype(bf16)
        state = []
        dpk = dpv = jnp.zeros((PREFIX_ROWS, PAIR), f32)
        for h in (0, 1):
            p = jnp.exp(dot(pka[h], qh[h], 1, 1))
            ds = (p * dot(pva[...], dh[h], 1, 1)).astype(bf16)
            dpv = dpv + dot(p.astype(bf16), dh[h, :, :PAIR], 1, 0)
            dpk = dpk + dot(ds, qh[h, :, :PAIR], 1, 0)
            state.append(dot(pkt[h * HEAD : (h + 1) * HEAD, :], ds, 1, 0))
        dp_ref[0] = dpk if i == 0 else dp_ref[0] + dpk
        dp_ref[1] = dpv if i == 0 else dp_ref[1] + dpv
        state = tuple(state)
        if i:
            state = lax.fori_loop(
                0, i * (bq // bk), lambda j, st: block(j * bk, st, 0, False), state
            )
        for j in range(bq // bk):
            state = block(i * bq + j * bk, state, j * bk, True)
        dq_all[span, :] = (jnp.concatenate(state, axis=0) * 0.125).T.astype(bf16)
    for r in range(seq):
        here = at(lax.bitwise_xor(s, r), rows)
        grad_refs[r][:, :PAIR] = dq_all[here, :]
        grad_refs[r][:, PAIR : 2 * PAIR] = dk_acc[here, :].astype(bf16)
        grad_refs[r][:, 2 * PAIR :] = dv_acc[here, :].astype(bf16)


def attend_backward(place, qkv, pk, pv, stat, mk, pm, o_parts, do_parts):
    seq = len(do_parts)
    s_len = qkv.shape[0]
    rows = s_len // seq
    bq, bk = min(2048, s_len), min(256, s_len)
    return pl.pallas_call(
        functools.partial(backward_body, seq, bq, bk),
        in_specs=[in_smem] + [in_vmem] * (6 + seq // 2 + seq),
        out_specs=[in_vmem] * (seq + 1),
        out_shape=[like((rows, 3 * PAIR))] * seq + [like((2, PREFIX_ROWS, PAIR), f32)],
        scratch_shapes=[
            pltpu.VMEM((2, s_len, 2 * PAIR), bf16),
            pltpu.VMEM((s_len, 2 * PAIR), bf16),
            pltpu.VMEM((PAIR, s_len), bf16),
            pltpu.VMEM((2, PREFIX_ROWS, 2 * PAIR), bf16),
            pltpu.VMEM((PREFIX_ROWS, 2 * PAIR), bf16),
            pltpu.VMEM((PAIR, PREFIX_ROWS), bf16),
            pltpu.VMEM((2, bq, 2 * PAIR), bf16),
            pltpu.VMEM((2, bq, 2 * PAIR), bf16),
            pltpu.VMEM((s_len, PAIR), f32),
            pltpu.VMEM((s_len, PAIR), f32),
            pltpu.VMEM((s_len, PAIR), bf16),
            pltpu.VMEM((s_len, PAIR), bf16),
            pltpu.VMEM((s_len, PAIR), bf16),
        ],
        compiler_params=params(44),
        cost_estimate=cost(5 * s_len * s_len * 512, s_len * PAIR * 24, s_len * s_len),
        name="attend_backward",
    )(place, qkv, pk, pv, stat, mk, pm, *o_parts, *do_parts)


def dp_masks(dp, near_first):
    masks = [1] + halvings(dp)[:-1] if near_first else halvings(dp)
    order = [0]
    for mask in masks:
        order += [i ^ mask for i in order]
    return masks, order


def middle_body(seq, pairs, dp, rows, place, *refs):
    groups = seq // 2
    tokens, cots, refs = refs[:2], refs[2:4], refs[4:]
    heads, refs = refs[: 2 * groups * pairs], refs[2 * groups * pairs :]
    firsts, seconds, refs = refs[: 2 * groups], refs[2 * groups : 4 * groups], refs[4 * groups :]
    across, (few, many), refs = refs[0], (refs[1:3], refs[3:5]), refs[5:]
    normed_ref, scale_ref, out_ref, out_give_ref, back_ref, back_give_ref, wo = refs[:7]
    up, down, normed, active, grads, cot = refs[7:]
    s, me = place[0], place[1]
    width = tokens[0].shape[1]
    shard = width // dp
    wide = width // seq
    half = seconds[0].shape[2]
    part = down.shape[1] // dp
    far_order = dp_masks(dp, False)[1]
    near_order = dp_masks(dp, True)[1]
    per_array = dp // 2

    for g in range(groups):
        owner = lax.bitwise_xor(s, 2 * g)
        for t in (0, 1):
            for j in range(per_array):
                here = at(lax.bitwise_xor(me, far_order[t * per_array + j]), shard)
                wo[owner, here, :] = firsts[2 * g + t][j, :, :wide]
                wo[lax.bitwise_xor(owner, 1), here, :] = across[2 * g + t, j]
                up[owner // 2, here, :half] = firsts[2 * g + t][j, :, wide:]
                up[owner // 2, here, half:] = seconds[2 * g + t][j]
    start = 0
    for arrays, order in ((few, near_order), (many, far_order)):
        size = arrays[0].shape[1]
        for t in (0, 1):
            for j in range(per_array):
                d = lax.bitwise_xor(me, order[t * per_array + j])
                done = 0
                while done < size:
                    x, row = (start + done) // part, (start + done) % part
                    take = min(part - row, size - done)
                    to = pl.multiple_of(d * part + row, min(take, part))
                    down[x, pl.ds(to, take), :] = arrays[t][j, done : done + take, :]
                    done += take
        start += size
    for p in range(pairs):
        for g in range(groups):
            for flip in (0, 1):
                source = heads[(p * groups + g) * 2 + flip]
                owner = lax.bitwise_xor(s, 2 * g + flip)
                column = pl.ds(pl.multiple_of(owner * (pairs * PAIR) + p * PAIR, PAIR), PAIR)
                for k in (0, 1):
                    here = k ^ flip
                    normed[k * rows : (k + 1) * rows, column] = source[
                        here * rows : (here + 1) * rows, :
                    ]
    for k in (0, 1):
        cot[k * rows : (k + 1) * rows, :] = cots[k][...]
    for k in (0, 1):
        merged = normed[k * rows : (k + 1) * rows, :]
        acc = tokens[k][...].astype(f32) + jnp.concatenate(
            [dot(merged, wo[o], 1, 0) for o in range(seq)], axis=1
        )
        unit, scale = normalize(acc)
        normed[k * rows : (k + 1) * rows, :] = unit.astype(bf16)
        if k == 0:
            out_ref[...] = acc
            normed_ref[...] = unit.astype(bf16)
            scale_ref[...] = jnp.broadcast_to(scale, scale_ref.shape)
    chunk = min(512, 2 * half)
    inner = 2 * half // chunk

    def step(h, carry):
        block, piece = h // inner, lax.rem(h, inner)
        w_up = up[block, :, at(piece, chunk)]
        w_down = down[block, at(piece, chunk), :]
        u = jnp.dot(normed[...], w_up, preferred_element_type=f32)
        gelu_grad = dot(cot[...], w_down, 1, 1)
        square = u * u
        side = 0.5 + 0.5 * jnp.tanh(u * (0.7978845608028654 + 0.7978845608028654 * 0.044715 * square))
        rise = 2 * 0.7978845608028654 + 6 * 0.7978845608028654 * 0.044715 * square
        slope = side + side * (1.0 - side) * (u * rise)
        active[block, :, at(piece, chunk)] = (u * side).astype(bf16)
        grads[block, :, at(piece, chunk)] = (gelu_grad * slope).astype(bf16)
        return carry

    lax.fori_loop(0, groups * inner, step, 0)
    for n in (0, 1):
        side = slice(n * width // 2, (n + 1) * width // 2)
        total = sum(dot(grads[g], up[g, side, :], 1, 1) for g in range(groups)).astype(bf16)
        back_ref[:, side] = total[:rows]
        back_give_ref[:, side] = total[rows:]
    for n in (0, 1):
        side = slice(n * width // 2, (n + 1) * width // 2)
        total = sum(dot(active[g], down[g, :, side], 1, 0) for g in range(groups))
        out_give_ref[:, side] = total[rows:].astype(bf16)
        out_ref[:, side] += total[:rows]


def middle(seq, dp, pairs, place, tokens, cots, heads, firsts, seconds, across, few, many):
    rows, width = tokens[0].shape
    groups = seq // 2
    half = seconds[0].shape[2]
    part = (few[0].shape[1] + many[0].shape[1]) // groups
    hidden = groups * 2 * half
    return pl.pallas_call(
        functools.partial(middle_body, seq, pairs, dp, rows),
        in_specs=[in_smem]
        + [in_vmem] * (9 + len(heads) + len(firsts) + len(seconds)),
        out_specs=[in_vmem] * 7,
        out_shape=[
            like((rows, width)),
            like((rows, PAIR), f32),
            like((rows, width), f32),
            like((rows, width)),
            like((rows, width)),
            like((rows, width)),
            like((seq, width, width // seq)),
        ],
        scratch_shapes=[
            pltpu.VMEM((groups, width, 2 * half), bf16),
            pltpu.VMEM((groups, dp * part, width), bf16),
            pltpu.VMEM((2 * rows, width), bf16),
            pltpu.VMEM((groups, 2 * rows, 2 * half), bf16),
            pltpu.VMEM((groups, 2 * rows, 2 * half), bf16),
            pltpu.VMEM((2 * rows, width), bf16),
        ],
        compiler_params=params(42),
        cost_estimate=cost(
            16 * rows * width * hidden + 4 * rows * width * width,
            4 * width * hidden + 20 * rows * width,
            2 * rows * hidden,
        ),
        name="middle",
    )(place, *tokens, *cots, *heads, *firsts, *seconds, across, *few, *many)


def turn_body(seq, pairs, place, unit_ref, scale_ref, cot_ref, own_ref, got_ref, wo, *refs):
    mid_grad_ref, grads, (merged,) = refs[0], refs[1:-1], refs[-1:]
    s = place[0]
    wide = wo.shape[2]
    grad = own_ref[...].astype(f32) + got_ref[...].astype(f32)
    mid_grad = cot_ref[...].astype(f32) + normalize_back(
        unit_ref[...].astype(f32), scale_ref[:, :1], grad
    )
    mid_grad_ref[...] = mid_grad
    rounded = mid_grad.astype(bf16)
    grad = sum(dot(rounded[:, o * wide : (o + 1) * wide], wo[o], 1, 1) for o in range(seq))
    merged[...] = grad.astype(bf16)
    for r in range(seq):
        for p in range(pairs):
            column = lax.bitwise_xor(s, r) * (pairs * PAIR) + p * PAIR
            grads[p * seq + r][...] = merged[:, pl.ds(pl.multiple_of(column, PAIR), PAIR)]


def turn(seq, pairs, place, unit, scale, cot, own, got, wo):
    rows, width = unit.shape
    return pl.pallas_call(
        functools.partial(turn_body, seq, pairs),
        in_specs=[in_smem] + [in_vmem] * 6,
        out_specs=[in_vmem] * (1 + seq * pairs),
        out_shape=[like((rows, width), f32)] + [like((rows, PAIR))] * (seq * pairs),
        scratch_shapes=[pltpu.VMEM((rows, width), bf16)],
        compiler_params=params(24),
        cost_estimate=cost(2 * rows * width * width, 16 * rows * width),
        name="turn",
    )(place, unit, scale, cot, own, got, wo)


def finish_body(tokens_ref, mid_grad_ref, own_ref, got_ref, out_ref):
    normed, scale = normalize(tokens_ref[...].astype(f32))
    grad = own_ref[...] + got_ref[...].astype(f32)
    out_ref[...] = (mid_grad_ref[...] + normalize_back(normed, scale, grad)).astype(bf16)


def finish(tokens, mid_grad, own, got):
    return pl.pallas_call(
        finish_body,
        in_specs=[in_vmem] * 4,
        out_specs=in_vmem,
        out_shape=like(tokens.shape),
        compiler_params=params(24),
        cost_estimate=cost(tokens.size * 20, tokens.size * 14),
        name="finish",
    )(tokens, mid_grad, own, got)


def masks(lengths, s_len):
    e0 = lengths[0]
    e1 = e0 + lengths[1]
    e2 = e1 + lengths[2]
    pos = jnp.arange(s_len, dtype=jnp.int32)
    doc = sum((pos >= e).astype(jnp.int32) for e in (e0, e1, e2))
    l = lax.broadcasted_iota(jnp.int32, (s_len, PAIR), 1)
    same = l == doc[:, None]
    mq = jnp.where((l < 4) & ~same, blocked, 0.0).astype(bf16)
    mk = jnp.where((l < 4) & same, 1.0, 0.0).astype(bf16)
    r = lax.broadcasted_iota(jnp.int32, (PREFIX_ROWS, PAIR), 0)
    lp = lax.broadcasted_iota(jnp.int32, (PREFIX_ROWS, PAIR), 1)
    pm = jnp.where((r >= PREFIX) & (lp == 3), 1.0, 0.0).astype(bf16)
    return mq, mk, pm


def parts_of(v):
    return [p.astype(bf16) for p in split3(v)]


def precise(a, b, side):
    high, mid, low = parts_of(a)
    few = a.shape[0]
    total = None
    for stack, part in zip(([high, mid, low], [high, mid], [high]), parts_of(b)):
        got = dot(jnp.concatenate(stack, axis=0), part, 1, side)
        for k in reversed(range(len(stack))):
            piece = got[k * few : (k + 1) * few]
            total = piece if total is None else total + piece
    return total


def full(a, b):
    return jnp.dot(a, b, precision=lax.Precision.HIGHEST, preferred_element_type=f32)


def precise_outer(a, b):
    high, mid, low = parts_of(a)
    high_b, mid_b, low_b = parts_of(b)
    left = jnp.concatenate([low, mid, high, mid, high, high], axis=0)
    right = jnp.concatenate([high_b, mid_b, low_b, high_b, mid_b, high_b], axis=0)
    return dot(left.astype(f32).T.astype(bf16), right, 1, 0)


def norm_body(rows_ref, out_ref):
    out_ref[...] = normalize(rows_ref[...].astype(f32))[0].astype(bf16)


def norm(rows):
    return pl.pallas_call(
        norm_body,
        in_specs=[in_vmem],
        out_specs=in_vmem,
        out_shape=like(rows.shape),
        compiler_params=params(8),
        cost_estimate=cost(rows.size * 8, rows.size * 4),
        name="norm",
    )(rows)


def reparam_body(seq, pairs, place, embed, inner, inner_bias, outer, outer_bias, kv, hidden, *parts):
    s = place[0]
    half = outer.shape[1] // 2
    hidden[...] = jnp.tanh(full(embed[...], inner[...]) + inner_bias[...])
    both = full(hidden[...], outer[...]) + outer_bias[...]
    kv[...] = both[:PREFIX]
    *parts, held = parts
    row = lax.broadcasted_iota(jnp.int32, both.shape, 0)
    held[...] = jnp.where(row < PREFIX, both, 0.0)
    for t in (0, 1):
        for p in range(pairs):
            column = pl.multiple_of(t * half + (s * pairs + p) * PAIR, PAIR)
            parts[t * pairs + p][...] = held[:, pl.ds(column, PAIR)].astype(bf16)


def reparam(seq, pairs, place, embed, inner, inner_bias, outer, outer_bias):
    width = outer.shape[1]
    return pl.pallas_call(
        functools.partial(reparam_body, seq, pairs),
        in_specs=[in_smem] + [in_vmem] * 5,
        out_specs=[in_vmem] * (2 + 2 * pairs),
        out_shape=[like((PREFIX, width), f32), like((PREFIX_ROWS, inner.shape[1]), f32)]
        + [like((PREFIX_ROWS, PAIR))] * (2 * pairs),
        scratch_shapes=[pltpu.VMEM((PREFIX_ROWS, width), f32)],
        compiler_params=params(20),
        cost_estimate=cost(12 * PREFIX_ROWS * (inner.size + outer.size), 4 * (inner.size + outer.size)),
        name="reparam",
    )(place, embed, inner, inner_bias[None], outer, outer_bias[None])


def reparam_back_body(seq, pairs, place, embed, inner, outer, hidden, *refs):
    got, (d_embed, d_inner, d_inner_bias, d_outer, d_outer_bias, grad) = refs[:2], refs[2:]
    s = place[0]
    half = outer.shape[1] // 2
    for r in range(seq):
        for t in (0, 1):
            for p in range(pairs):
                column = t * half + (lax.bitwise_xor(s, r) * pairs + p) * PAIR
                grad[:, pl.ds(pl.multiple_of(column, PAIR), PAIR)] = got[r % 2][r // 2, p, t]
    d_outer_bias[...] = jnp.sum(grad[...], axis=0, keepdims=True)
    d_outer[...] = precise_outer(hidden[...], grad[...])
    back = precise(grad[...], outer[...], 1) * (1.0 - hidden[...] * hidden[...])
    d_inner_bias[...] = jnp.sum(back, axis=0, keepdims=True)
    d_inner[...] = precise_outer(embed[...], back)
    d_embed[...] = precise(back, inner[...], 1)[:PREFIX]


def reparam_back(pairs, place, embed, inner, outer, hidden, got):
    seq = 2 * got[0].shape[0]
    wide, (deep, width) = inner.shape[0], outer.shape
    outs = pl.pallas_call(
        functools.partial(reparam_back_body, seq, pairs),
        in_specs=[in_smem] + [in_vmem] * 6,
        out_specs=[in_vmem] * 5,
        out_shape=[
            like((PREFIX, wide), f32),
            like((wide, deep), f32),
            like((1, deep), f32),
            like((deep, width), f32),
            like((1, width), f32),
        ],
        scratch_shapes=[pltpu.VMEM((PREFIX_ROWS, width), f32)],
        compiler_params=params(28),
        cost_estimate=cost(24 * PREFIX_ROWS * (inner.size + outer.size), 8 * (inner.size + outer.size)),
        name="reparam_back",
    )(place, embed, inner, outer, hidden, *got)
    return outs[0], outs[1], outs[2][0], outs[3], outs[4][0]


def product_body(pairs, adds, out_dtype, *refs):
    weights, refs = refs[:pairs], refs[pairs:]
    count = len(refs) // (pairs + adds + 1)
    rows, refs = refs[: count * pairs], refs[count * pairs :]
    extra, outs = refs[: count * adds], refs[count * adds :]
    for i in range(count):
        total = sum(dot(rows[i * pairs + p][...], weights[p][...], 1, 1) for p in range(pairs))
        if adds:
            total = total + extra[i][...].astype(f32)
        outs[i][...] = total.astype(out_dtype)


def product(weights, rows, extra, out_dtype):
    pairs = len(weights)
    height, width = rows[0][0].shape[0], weights[0].shape[0]
    flat = [w for entry in rows for w in entry]
    return pl.pallas_call(
        functools.partial(product_body, pairs, int(bool(extra)), out_dtype),
        in_specs=[in_vmem] * (pairs + len(flat) + len(extra)),
        out_specs=[in_vmem] * len(rows),
        out_shape=[like((height, width), out_dtype)] * len(rows),
        compiler_params=params(24),
        cost_estimate=cost(
            2 * len(flat) * height * width * flat[0].shape[1], 4 * len(rows) * height * width
        ),
        name="product",
    )(*weights, *flat, *extra)


def halvings(count):
    steps = []
    while count > 1:
        count //= 2
        steps.append(count)
    return steps


def swap(value, axis, size, mask):
    return lax.ppermute(value, axis, [(i, i ^ mask) for i in range(size)])


def after(value, *events):
    return lax.optimization_barrier((value, *events))[0] if events else value


def spread_seq(value, seq):
    held = {0: value}
    for mask in halvings(seq):
        for r in list(held):
            held[r ^ mask] = swap(held[r], "seq", seq, mask)
    return [held[r] for r in range(seq)]


def exchange_seq(pieces, seq):
    return [pieces[0]] + [swap(pieces[r], "seq", seq, r) for r in range(1, seq)]


def shards(seq, dp, tokens, lengths, attend_weight, output_weight, expand_weight, shrink_weight,
           prefix_embed, inner_weight, inner_bias, outer_weight, outer_bias, cotangent):
    s = lax.axis_index("seq")
    rows, width = tokens.shape[1:]
    s_len = rows * seq
    pairs = width // seq // PAIR
    groups = seq // 2
    token_rows, cot_rows = tokens[0], cotangent[0]
    place = jnp.stack([s, lax.axis_index("dp")]).astype(jnp.int32)
    near_mask, far_masks = dp_masks(dp, False)[0][-1], dp_masks(dp, False)[0][:-1]

    def over(value, mask, *events):
        return swap(after(value, *events), "dp", dp, mask)

    def other_core(value, *events):
        return swap(after(value, *events), "seq", seq, 1)

    def line(piece, begin=(), later=()):
        held, arrived = piece, []
        for mask in far_masks:
            arrived.append(over(held, mask, *(later if arrived else begin)))
            held = jnp.concatenate([held, arrived[-1]])
        return held, arrived

    def spread(value, *events):
        held = {0: after(value, *events)}
        for mask in halvings(seq)[:-1]:
            for g in list(held):
                held[g ^ mask // 2] = swap(held[g], "seq", seq, mask)
        return [held[g] for g in range(groups)]

    token_far = spread(token_rows)
    token_pair = (token_rows, other_core(token_rows))
    cot_pair = (cot_rows, other_core(cot_rows))
    attend_lines = [
        line(w[None], later=(token_pair[1], cot_pair[1]))
        for w in cut_attend(seq, pairs, place, attend_weight)
    ]
    first, second, down = cut_rest(seq, place, output_weight, expand_weight, shrink_weight)
    quarter = down.shape[0] // 4
    few = over(down[None, :quarter], near_mask, attend_lines[0][1][0])
    few = jnp.concatenate([down[None, :quarter], few])
    attend_pairs = [(w, over(w, near_mask)) for w, _ in attend_lines]
    normed_rows = [norm(w) for w in token_pair]
    line_a, steps_a = line(
        first[None],
        (few, *[steps[-1] for _, steps in attend_lines]),
        (attend_pairs[0][1],),
    )
    for w in token_far[1:]:
        normed_rows += [norm(w), norm(other_core(w))]
    line_b, steps_b = line(second[None], (steps_a[0], attend_pairs[0][1]), (attend_pairs[-1][1],))

    embed = after(prefix_embed, attend_lines[-1][1][-1])
    embed = jnp.pad(embed, ((0, PREFIX_ROWS - PREFIX), (0, 0)))
    prefix_kv, prefix_hidden, *prefix_parts = reparam(
        seq, pairs, place, embed, inner_weight, inner_bias, outer_weight, outer_bias
    )
    prefix_pairs = [(prefix_parts[p], prefix_parts[pairs + p]) for p in range(pairs)]
    mask_q, mask_k, mask_p = masks(lengths[0], s_len)
    saved, heads = [], []

    def attend(p, *events):
        qkv, stat, weight, *outs = attend_forward(
            after(place, *events), normed_rows, *attend_pairs[p], *prefix_pairs[p],
            mask_q, mask_k, mask_p,
        )
        saved.append((qkv, stat, weight, outs))
        for g in range(groups):
            got = outs[0] if g == 0 else swap(outs[g], "seq", seq, 2 * g)
            heads.extend((got, other_core(got)))

    attend(0, attend_pairs[-1][1], steps_a[-1], steps_b[0])
    other_a = over(line_a, near_mask, attend_pairs[-1][1])
    near_a = spread(line_a, normed_rows[-1])
    many = over(down[None, quarter:], far_masks[0], steps_b[0])
    many = jnp.concatenate([down[None, quarter:], many])
    begun = saved[0][1]
    other_b = over(line_b, near_mask, begun, other_a)
    far_a = spread(other_a, begun, *near_a)
    for mask in far_masks[1:]:
        many = jnp.concatenate([many, over(many, mask, begun, steps_b[-1])])
    for p in range(1, pairs):
        attend(p, other_a, *near_a, steps_b[-1])
    ended = saved[-1][1]
    many = (many, over(many, near_mask, ended, other_b, *far_a, *heads[: 2 * groups]))
    near_b = spread(line_b, ended, *far_a)
    far_b = spread(other_b, ended, *far_a)
    for mask in far_masks[:-1]:
        few = jnp.concatenate([few, over(few, mask, ended)])
    few = (few, over(few, far_masks[-1], *heads, *near_b))
    ups = [
        [w for g in range(groups) for w in (a[g], b[g])]
        for a, b in ((near_a, far_a), (near_b, far_b))
    ]
    wide = width // seq
    across = other_core(jnp.stack([w[..., :wide] for w in ups[0]]))
    unit, scale, out_own, out_give, back_own, back_give, wo = middle(
        seq, dp, pairs, place, token_pair, cot_pair, heads, *ups, across, few, many
    )
    mid_grad, *out_grads = turn(
        seq, pairs, place, unit, scale, cot_rows, back_own, other_core(back_give), wo
    )
    outputs = (out_own + other_core(out_give).astype(f32)).astype(bf16)
    grads, prefix_terms = [], []
    for p in range(pairs):
        qkv, stat, weight, outs = saved[p]
        got = exchange_seq(out_grads[p * seq : (p + 1) * seq], seq)
        *parts, prefix_part = attend_backward(
            place, qkv, *prefix_pairs[p], stat, mask_k, mask_p, outs, got
        )
        grads.append(parts)
        prefix_terms.append(prefix_part)

    prefix_sum = jnp.stack(spread(jnp.stack(prefix_terms)))

    weights = [entry[2] for entry in saved]
    block = lambda r: [grads[p][r] for p in range(pairs)]
    sent = product(weights, [block(r) for r in range(1, seq, 2)], [], bf16)
    got = [other_core(v) for v in sent]
    late = [after(weights[0], prefix_sum), *weights[1:]]
    evens = product(late, [block(r) for r in range(2, seq, 2)], got[1:], bf16)
    (own,) = product(weights, [block(0)], got[:1], f32)
    left = dict(zip(range(2, seq, 2), evens))
    for mask in reversed(halvings(seq)[:-1]):
        keep = {}
        for r in [0, *left]:
            if r & mask:
                continue
            arrived = swap(left[r ^ mask], "seq", seq, mask)
            if r:
                keep[r] = left[r] + arrived
            elif len(left) > 1:
                own = own + arrived.astype(f32)
        left = keep
    input_grad = finish(token_rows, mid_grad, own, arrived)

    prefix_sum = after(prefix_sum, *evens)
    reach = [0]
    for mask in far_masks:
        reach += [mask ^ other for other in reach]
    terms = [prefix_sum] + [swap(prefix_sum, "dp", dp, mask) for mask in reach[1:]]
    while len(terms) > 1:
        half = len(terms) // 2
        terms = [terms[i] + terms[i + half] for i in range(half)]
    prefix_sum = terms[0] + swap(terms[0], "dp", dp, near_mask)
    prefix_all = (prefix_sum, other_core(prefix_sum))
    back = reparam_back(
        pairs, place, embed, inner_weight, outer_weight, prefix_hidden, prefix_all
    )
    return (outputs[None], input_grad[None], *back, prefix_kv)


def solution(mesh):
    placed = (
        P("dp", "seq", None),
        P("dp", None),
        P("dp", None),
        P("dp", None),
        P("dp", None),
        P("dp", None),
        P(),
        P(),
        P(),
        P(),
        P(),
        P("dp", "seq", None),
    )
    return jax.shard_map(
        functools.partial(shards, mesh.shape["seq"], mesh.shape["dp"]),
        mesh=mesh,
        in_specs=placed,
        out_specs=(P("dp", "seq", None), P("dp", "seq", None), P(), P(), P(), P(), P(), P()),
        check_vma=False,
    )
```
